128 devices in a mesh: row: 8 (over z, y_hi), col: 16 (over y_lo, x, core).
Axes of the slice: x: 4, y: 4 (y_hi: 2, y_lo: 2; y = y_hi * 2 + y_lo), z: 4, core: 2. Of those that a mesh axis runs over, the one named last changes fastest.
Arguments:
- object_field: float32 [2, 2, 2048, 4096], P(None, None, 'row', 'col'), may hold values from -0.6 to 1
- probe_modes: float32 [2, 2, 256, 256], replicated, may hold values from -5 to 5
- amplitudes: float32 [2, 24, 16, 256, 256], P(None, 'row', 'col'), may hold values from 0 to 2
- offsets: int32 [2, 2, 24, 16], P(None, None, 'row', 'col'), may hold values from 0 to 255
- counts: int32 [2, 8, 16], P(None, 'row', 'col'), may hold values from 1 to 3, as said below
Outputs:
- new_object: float32 [2, 2, 2048, 4096], P(None, None, 'row', 'col')
- new_probe: float32 [2, 2, 256, 256], replicated
The draws below stay inside these ranges and needn't reach their ends.
Inputs may be any that keep to these rules, and one draw needn't show every extreme that they name: offsets[b, 0, r * 3 + s, c] and offsets[b, 1, r * 3 + s, c] are the row and column, counted from tile (r, c)'s first cell, of the centre of slot s's 256 x 256 patch in batch b. Tile (r, c) has counts[b, r, c] scan positions in batch b, in its first slots; the other slots are unused; in each batch some tile has 3.
All inputs are finite; a program needn't handle non-finite values.
Results may differ from the reference program's by a relative error of at most 0.02.
Values sent between devices are 32-bit elements; how exact they have to be, the bound alone decides.
A program may use at most 128 MiB of HBM per device.

```python
import math
import jax
import jax.numpy as jnp
from jax import lax

P_SIZE = 256
MODES = 2
SLICES = 2
BATCHES = 2
TILE = 256
MAXP = 3
NY = 2048
NX = 4096
SLOTR = 24
N_ROW = 8
N_COL = 16


def draw_counts(key, part):
    own_key = jax.random.fold_in(key, 11)
    level_key, pick_key = jax.random.split(own_key, 2)
    levels = jax.random.randint(level_key, (BATCHES, N_ROW * N_COL), 0, 8)
    base = jnp.where(levels < 5, 1, jnp.where(levels < 7, 2, MAXP))
    base = jnp.minimum(base, MAXP)
    picked = jax.random.randint(pick_key, (BATCHES,), 0, N_ROW * N_COL)
    cells = jnp.arange(N_ROW * N_COL, dtype=jnp.int32)
    filled = jnp.where(cells[None, :] == picked[:, None], MAXP, base)
    return filled.reshape(BATCHES, N_ROW, N_COL).astype(jnp.int32)


def place_ends(values, stream_key, least, high):
    longest = values.shape.index(max(values.shape))
    spots = []
    for shift in (0, 1):
        where = [jax.random.randint(jax.random.fold_in(stream_key, axis), (), 0, length) for axis, length in enumerate(values.shape)]
        where[longest] = (where[longest] + shift) % values.shape[longest]
        spots.append(tuple(where))
    return values.at[spots[0]].set(least).at[spots[1]].set(high)


def shard_levels(stream_key, shape, shards, least, high):
    def one(axis_at, blocks):
        draws = jax.random.uniform(jax.random.fold_in(jax.random.fold_in(stream_key, 6), axis_at), (blocks,), jnp.float32, least / len(shards), high / len(shards))
        return jnp.repeat(jnp.exp(draws), shape[axis_at] // blocks).reshape((-1,) + (1,) * (len(shape) - axis_at - 1))

    loudness = one(*shards[0])
    for cut in shards[1:]:
        loudness = loudness * one(*cut)
    return loudness


def gaussian(rng, shape, spread, most, kind=jnp.bfloat16):
    array = jax.random.normal(rng, shape, jnp.float32) * spread
    return jnp.minimum(jnp.maximum(array, -most), most).astype(kind)


def setup_inputs(seed: int = 0) -> dict:
    key_of = jax.random.split(jax.random.key(seed), 6)
    object_field = jnp.clip(-0.6 + 1.6 * jax.random.uniform(key_of[0], (2, SLICES, NY, NX), jnp.float32) ** shard_levels(key_of[0], (2, SLICES, NY, NX), ((2, 8), (3, 16)), -0.2, 0.2), -0.6, 1.0)
    probe_modes = gaussian(key_of[1], (2, MODES, P_SIZE, P_SIZE), 1.0, 5.0, jnp.float32)
    amplitudes = jnp.clip(2.0 * jax.random.uniform(key_of[2], (BATCHES, SLOTR, N_COL, P_SIZE, P_SIZE), jnp.float32) ** shard_levels(key_of[2], (BATCHES, SLOTR, N_COL, P_SIZE, P_SIZE), ((1, 8), (2, 16)), -0.2, 0.2), 0.0, 2.0)
    offsets = place_ends(jax.random.randint(key_of[3], (BATCHES, 2, SLOTR, N_COL), 0, TILE), jax.random.fold_in(key_of[3], 1), 0, TILE - 1).astype(jnp.int32)
    counts = draw_counts(jax.random.fold_in(key_of[5], 71), 0)
    return dict(object_field=object_field, probe_modes=probe_modes, amplitudes=amplitudes, offsets=offsets, counts=counts)


AMPLITUDE_FLOOR = 0.5
OBJECT_STEP = 0.25
PROBE_STEP = 0.125

def tables(pattern_side):
    indices = jnp.arange(pattern_side, dtype=jnp.int32)
    products = indices[:, None] * indices[None, :] % pattern_side
    angles = products.astype(jnp.float32) * (2.0 * math.pi / pattern_side)
    norm_scale = 1.0 / math.sqrt(pattern_side)
    forward_re = (jnp.cos(angles) * norm_scale).astype(jnp.bfloat16)
    forward_im = (-jnp.sin(angles) * norm_scale).astype(jnp.bfloat16)
    frequency = jnp.where(indices < pattern_side // 2, indices, indices - pattern_side)
    phases = (frequency[:, None] * frequency[:, None] + frequency[None, :] * frequency[None, :]) % (16 * pattern_side)
    chirp_angles = phases.astype(jnp.float32) * (2.0 * math.pi / (16 * pattern_side))
    return (forward_re, forward_im, jnp.cos(chirp_angles), -jnp.sin(chirp_angles))

def contract(form, left, right):
    return jnp.einsum(form, left.astype(jnp.float32), right.astype(jnp.float32), precision=lax.Precision.HIGHEST)

def rounded(values):
    return lax.optimization_barrier(values.astype(jnp.bfloat16))

def transform(field_re, field_im, table_re, table_im, inverse):
    sign_value = -1.0 if inverse else 1.0
    left_re = rounded(field_re)
    left_im = rounded(field_im)
    first_rr = contract('mjk,kl->mjl', left_re, table_re)
    first_ri = contract('mjk,kl->mjl', left_re, table_im)
    first_ir = contract('mjk,kl->mjl', left_im, table_re)
    first_ii = contract('mjk,kl->mjl', left_im, table_im)
    middle_re = rounded(first_rr - sign_value * first_ii)
    middle_im = rounded(first_ir + sign_value * first_ri)
    out_re = contract('jk,mkl->mjl', table_re, middle_re) - sign_value * contract('jk,mkl->mjl', table_im, middle_im)
    out_im = contract('jk,mkl->mjl', table_re, middle_im) + sign_value * contract('jk,mkl->mjl', table_im, middle_re)
    return (out_re, out_im)

def position_terms(patch_cells, probe_modes, amplitude, dft_table):
    forward_re, forward_im, chirp_re, chirp_im = dft_table
    slice_count = patch_cells.shape[1]
    wave_re = probe_modes[0]
    wave_im = probe_modes[1]
    incoming = []
    for slice_index in range(slice_count):
        incoming.append((wave_re, wave_im))
        object_re = patch_cells[0, slice_index]
        object_im = patch_cells[1, slice_index]
        exit_re = wave_re * object_re - wave_im * object_im
        exit_im = wave_re * object_im + wave_im * object_re
        if slice_index + 1 < slice_count:
            spread_re, spread_im = transform(exit_re, exit_im, forward_re, forward_im, False)
            turned_re = spread_re * chirp_re - spread_im * chirp_im
            turned_im = spread_re * chirp_im + spread_im * chirp_re
            wave_re, wave_im = transform(turned_re, turned_im, forward_re, forward_im, True)
    far_re, far_im = transform(exit_re, exit_im, forward_re, forward_im, False)
    intensity = lax.optimization_barrier(jnp.sum(far_re * far_re + far_im * far_im, axis=0))
    modulus_ratio = 1.0 - amplitude / jnp.maximum(jnp.sqrt(intensity), AMPLITUDE_FLOOR)
    back_re, back_im = transform(far_re * modulus_ratio, far_im * modulus_ratio, forward_re, forward_im, True)
    object_terms = [None] * slice_count
    for slice_index in reversed(range(slice_count)):
        wave_re, wave_im = incoming[slice_index]
        object_re = patch_cells[0, slice_index]
        object_im = patch_cells[1, slice_index]
        term_re = lax.optimization_barrier(jnp.sum(wave_re * back_re + wave_im * back_im, axis=0))
        term_im = lax.optimization_barrier(jnp.sum(wave_re * back_im - wave_im * back_re, axis=0))
        object_terms[slice_index] = (term_re, term_im)
        inner_re = object_re * back_re + object_im * back_im
        inner_im = object_re * back_im - object_im * back_re
        if slice_index > 0:
            spread_re, spread_im = transform(inner_re, inner_im, forward_re, forward_im, False)
            turned_re = spread_re * chirp_re + spread_im * chirp_im
            turned_im = spread_im * chirp_re - spread_re * chirp_im
            back_re, back_im = transform(turned_re, turned_im, forward_re, forward_im, True)
    object_stack = jnp.stack([jnp.stack([pair_terms[0] for pair_terms in object_terms]), jnp.stack([pair_terms[1] for pair_terms in object_terms])])
    probe_stack = jnp.stack([inner_re, inner_im])
    return (object_stack, probe_stack)

def reference(object_field, probe_modes, amplitudes, offsets, counts):
    rim_width = P_SIZE // 2
    dft_table = tables(P_SIZE)
    current = object_field
    probe_total = jnp.zeros(probe_modes.shape, jnp.float32)
    item_count = N_ROW * N_COL * MAXP
    for batch_index in range(BATCHES):
        padded = jnp.pad(current, ((0, 0), (0, 0), (rim_width, rim_width), (rim_width, rim_width)))

        def visit_item(running, item_index):
            gradient, probe_part = running
            row_index = item_index // (N_COL * MAXP)
            col_index = item_index // MAXP % N_COL
            slot_index = item_index % MAXP
            slot_row = row_index * MAXP + slot_index
            start_row = (row_index * TILE + offsets[batch_index, 0, slot_row, col_index]).astype(jnp.int32)
            start_col = (col_index * TILE + offsets[batch_index, 1, slot_row, col_index]).astype(jnp.int32)
            zero_index = jnp.zeros((), jnp.int32)
            anchor = (zero_index, zero_index, start_row, start_col)

            def compute_terms(unused):
                patch_cells = lax.dynamic_slice(padded, anchor, (2, SLICES, P_SIZE, P_SIZE))
                return position_terms(patch_cells, probe_modes, amplitudes[batch_index, slot_row, col_index], dft_table)

            def zero_terms(unused):
                return (jnp.zeros((2, SLICES, P_SIZE, P_SIZE), jnp.float32), jnp.zeros(probe_modes.shape, jnp.float32))
            is_live = slot_index < counts[batch_index, row_index, col_index]
            object_stack, probe_stack = lax.cond(is_live, compute_terms, zero_terms, 0)
            window = lax.dynamic_slice(gradient, anchor, (2, SLICES, P_SIZE, P_SIZE))
            gradient = lax.dynamic_update_slice(gradient, window + object_stack, anchor)
            return ((gradient, probe_part + probe_stack), None)
        start_state = (jnp.zeros(padded.shape, jnp.float32), jnp.zeros(probe_modes.shape, jnp.float32))
        final_state, unused = lax.scan(visit_item, start_state, jnp.arange(item_count, dtype=jnp.int32))
        gradient, probe_part = final_state
        current = current - OBJECT_STEP * gradient[:, :, rim_width:rim_width + NY, rim_width:rim_width + NX]
        probe_total = probe_total + probe_part
    return (current, probe_modes - PROBE_STEP * probe_total)
```

```python
import math

import jax
import jax.numpy as jnp
import numpy as np
from jax import lax
from jax.experimental import pallas as pl
from jax.experimental.pallas import tpu as pltpu
from jax.sharding import PartitionSpec as P

AMPLITUDE_FLOOR = 0.5
OBJECT_STEP = 0.25
PROBE_STEP = 0.125
SIDE = 256
HALF = SIDE // 2
MODES = 2
CHUNK = 16


def real_form(table):
    re, im = table.real, table.imag
    return np.block([[re, im], [-im, re]]).astype(jnp.bfloat16)


def make_tables():
    index = np.arange(SIDE)
    angles = (index[:, None] * index[None, :] % SIDE).astype(np.float32) * np.float32(2.0 * math.pi / SIDE)
    scale = np.float32(1.0 / math.sqrt(SIDE))
    rounded = lambda v: (v * scale).astype(jnp.bfloat16).astype(np.float64)
    forward = rounded(np.cos(angles)) - 1j * rounded(np.sin(angles))
    frequency = np.where(index < HALF, index, index - SIDE).astype(np.float64)
    chirp = np.exp(-2j * math.pi * (frequency * frequency % (16 * SIDE)) / (16 * SIDE))
    spread = (forward.conj() * chirp[None, :]) @ forward
    same = 0.25 * (spread[:HALF, :HALF] + spread[HALF:, HALF:] + spread[:HALF, HALF:] + spread[HALF:, :HALF])
    other = 0.25 * (spread[:HALF, :HALF] + spread[HALF:, HALF:] - spread[:HALF, HALF:] - spread[HALF:, :HALF])
    same = 0.5 * (same + same.T)
    other = 0.5 * (other + other.T)
    even = forward[:HALF, 0::2]
    odd = forward[:HALF, 1::2]
    rows = []
    for table in (same, other, even, odd):
        matrix = real_form(table)
        rows += [matrix, np.ascontiguousarray(matrix.T)]
    order = np.zeros((SIDE, SIDE), np.float32)
    order[0::2, :HALF] = np.eye(HALF)
    order[1::2, HALF:] = np.eye(HALF)
    return np.stack(rows), order.astype(jnp.bfloat16)


TABLES, ORDER = make_tables()
(SUM_R, SUM_L, DIF_R, DIF_L, EVEN_R, EVEN_L, ODD_R, ODD_L) = range(8)


def dot(left, right):
    return jnp.dot(left, right, preferred_element_type=jnp.float32)


def three_parts(value):
    high = value.astype(jnp.bfloat16)
    rest = value - high.astype(jnp.float32)
    middle = rest.astype(jnp.bfloat16)
    return high, middle, (rest - middle.astype(jnp.float32)).astype(jnp.bfloat16)


def reorder_kernel(amp_ref, order_ref, turn_ref, out_ref):
    def one(slot, carry):
        high, middle, low = [dot(part, order_ref[...]) for part in three_parts(amp_ref[slot])]
        high, middle, low = [dot(turn_ref[...], part) for part in three_parts(high + (middle + low))]
        out_ref[slot] = high + (middle + low)
        return carry

    lax.fori_loop(0, amp_ref.shape[0], one, 0)


def reorder(amplitudes):
    slots = amplitudes.shape[0]
    spec = pl.BlockSpec(memory_space=pltpu.VMEM)
    return pl.pallas_call(
        reorder_kernel,
        out_shape=jax.ShapeDtypeStruct((slots, SIDE, SIDE), jnp.float32),
        in_specs=[spec, spec, spec],
        out_specs=spec,
        compiler_params=pltpu.CompilerParams(vmem_limit_bytes=16 << 20),
        cost_estimate=pl.CostEstimate(flops=slots * 12 * SIDE**3, bytes_accessed=slots * 8 * SIDE * SIDE, transcendentals=0),
    )(amplitudes, jnp.asarray(ORDER), jnp.asarray(ORDER.T))


def batch_kernel(
    offset_ref, count_ref, ext_ref, probe_ref, amp_ref, table_ref, grad_ref, probe_grad_ref,
    obj, psi, right_a, right_b, yield_a, yield_b, left_a, left_b, out_a, out_b,
):
    lanes = lax.broadcasted_iota(jnp.int32, (CHUNK, HALF), 1)
    lo, hi = pl.ds(0, HALF), pl.ds(HALF, HALF)

    def chunks(total, body):
        def step(index, carry):
            body(pl.multiple_of(index * CHUNK, CHUNK))
            return carry

        lax.fori_loop(0, total // CHUNK, step, 0)

    def bf(value):
        return value.astype(jnp.bfloat16)

    def zero_grad(row):
        for part in range(2):
            for layer in range(2):
                for block in range(4):
                    grad_ref[part, layer, block, pl.ds(row, CHUNK), :] = jnp.zeros((CHUNK, HALF), jnp.float32)

    chunks(2 * SIDE, zero_grad)

    def zero_probe(row):
        for part in range(2):
            for mode in range(MODES):
                probe_grad_ref[part, mode, pl.ds(row, CHUNK), :] = jnp.zeros((CHUNK, SIDE), jnp.float32)

    chunks(SIDE, zero_probe)

    def right(table_a, table_b):
        yield_a[...] = dot(right_a[...], table_ref[table_a])
        yield_b[...] = dot(right_b[...], table_ref[table_b])

    def left(table_a, table_b):
        out_a[...] = dot(table_ref[table_a], left_a[...])
        out_b[...] = dot(table_ref[table_b], left_b[...])

    def put_split(mode, row, re, im):
        at = pl.ds(mode * SIDE + row, CHUNK)
        right_a[at, lo] = bf(re[0] + re[1])
        right_a[at, hi] = bf(im[0] + im[1])
        right_b[at, lo] = bf(re[0] - re[1])
        right_b[at, hi] = bf(im[0] - im[1])

    def columns(ref, mode):
        return pl.ds(mode * SIDE, HALF), pl.ds(mode * SIDE + HALF, HALF)

    def middle_spread(row):
        for mode in range(MODES):
            here = columns(left_a, mode)
            for part, lane in ((0, lo), (1, hi)):
                top = pl.ds(mode * SIDE + row, CHUNK)
                low = pl.ds(mode * SIDE + HALF + row, CHUNK)
                at, ab = yield_a[top, lane], yield_a[low, lane]
                bt, bb = yield_b[top, lane], yield_b[low, lane]
                to = pl.ds(part * HALF + row, CHUNK)
                a_sum, a_dif = at + ab, at - ab
                b_sum, b_dif = bt + bb, bt - bb
                left_a[to, here[0]] = bf(a_sum + b_sum)
                left_a[to, here[1]] = bf(a_sum - b_sum)
                left_b[to, here[0]] = bf(a_dif + b_dif)
                left_b[to, here[1]] = bf(a_dif - b_dif)

    def middle_forward(row):
        for mode in range(MODES):
            here = columns(left_a, mode)
            for part, lane in ((0, lo), (1, hi)):
                top = pl.ds(mode * SIDE + row, CHUNK)
                low = pl.ds(mode * SIDE + HALF + row, CHUNK)
                to = pl.ds(part * HALF + row, CHUNK)
                for source, at in ((yield_a, here[0]), (yield_b, here[1])):
                    upper, lower = source[top, lane], source[low, lane]
                    left_a[to, at] = bf(upper + lower)
                    left_b[to, at] = bf(upper - lower)

    def middle_backward(row):
        for mode in range(MODES):
            here = columns(left_a, mode)
            for part, lane in ((0, lo), (1, hi)):
                to = pl.ds(part * HALF + row, CHUNK)
                for base, target in ((0, left_a), (HALF, left_b)):
                    at = pl.ds(mode * SIDE + base + row, CHUNK)
                    even, odd = yield_a[at, lane], yield_b[at, lane]
                    target[to, here[0]] = bf(even + odd)
                    target[to, here[1]] = bf(even - odd)

    def joined(mode, row):
        result = []
        for sign in (1, -1):
            pair = []
            for part in range(2):
                at = pl.ds(part * HALF + row, CHUNK)
                halves = []
                for lane in columns(out_a, mode):
                    a, b = out_a[at, lane], out_b[at, lane]
                    halves.append(a + b if sign > 0 else a - b)
                pair.append(halves)
            result.append(pair)
        return result

    def pair_of(ref, first, second, row):
        return [ref[first, second, pl.ds(row, CHUNK), lane] for lane in (lo, hi)]

    def one_slot(slot, carry):
        start_row = offset_ref[0, slot]
        start_col = offset_ref[1, slot]
        base = start_col // HALF
        shift = start_col % HALF
        take_left = lanes < HALF - shift
        put_right = lanes >= shift
        back = lax.rem(HALF - shift, HALF)

        def fetch(row):
            for part in range(2):
                for layer in range(2):
                    at = pl.ds(start_row + row, CHUNK)
                    turned = [pltpu.roll(ext_ref[part, layer, base + k, at, :], back, 1) for k in range(3)]
                    obj[part, layer, pl.ds(row, CHUNK), lo] = jnp.where(take_left, turned[0], turned[1])
                    obj[part, layer, pl.ds(row, CHUNK), hi] = jnp.where(take_left, turned[1], turned[2])

        chunks(SIDE, fetch)

        def enter(row):
            o_re, o_im = pair_of(obj, 0, 0, row), pair_of(obj, 1, 0, row)
            for mode in range(MODES):
                p_re, p_im = pair_of(probe_ref, 0, mode, row), pair_of(probe_ref, 1, mode, row)
                re = [p_re[k] * o_re[k] - p_im[k] * o_im[k] for k in range(2)]
                im = [p_re[k] * o_im[k] + p_im[k] * o_re[k] for k in range(2)]
                put_split(mode, row, re, im)

        chunks(SIDE, enter)
        right(SUM_R, DIF_R)
        chunks(HALF, middle_spread)
        left(SUM_L, DIF_L)

        def second_slice(row):
            for side in range(2):
                at = row + side * HALF
                o_re, o_im = pair_of(obj, 0, 1, at), pair_of(obj, 1, 1, at)
                for mode in range(MODES):
                    w_re, w_im = joined(mode, row)[side]
                    for k, lane in ((0, lo), (1, hi)):
                        psi[0, mode, pl.ds(at, CHUNK), lane] = w_re[k]
                        psi[1, mode, pl.ds(at, CHUNK), lane] = w_im[k]
                    re = [w_re[k] * o_re[k] - w_im[k] * o_im[k] for k in range(2)]
                    im = [w_re[k] * o_im[k] + w_im[k] * o_re[k] for k in range(2)]
                    put_split(mode, at, re, im)

        chunks(HALF, second_slice)
        right(EVEN_R, ODD_R)
        chunks(HALF, middle_forward)
        left(EVEN_L, ODD_L)

        def compare(row):
            for base_row, source in ((0, out_a), (HALF, out_b)):
                waves = []
                for mode in range(MODES):
                    here = columns(source, mode)
                    re = [source[pl.ds(row, CHUNK), lane] for lane in here]
                    im = [source[pl.ds(HALF + row, CHUNK), lane] for lane in here]
                    waves.append((re, im))
                for k, lane in ((0, lo), (1, hi)):
                    intensity = waves[0][0][k] * waves[0][0][k] + waves[0][1][k] * waves[0][1][k]
                    for re, im in waves[1:]:
                        intensity = intensity + (re[k] * re[k] + im[k] * im[k])
                    amplitude = amp_ref[slot, pl.ds(base_row + row, CHUNK), lane]
                    ratio = 1.0 - amplitude * lax.rsqrt(jnp.maximum(intensity, AMPLITUDE_FLOOR**2))
                    target = right_a if k == 0 else right_b
                    for mode, (re, im) in enumerate(waves):
                        at = pl.ds(mode * SIDE + base_row + row, CHUNK)
                        target[at, lo] = bf(re[k] * ratio)
                        target[at, hi] = bf(im[k] * ratio)

        chunks(HALF, compare)
        right(EVEN_L, ODD_L)
        chunks(HALF, middle_backward)
        left(EVEN_R, ODD_R)

        def add_term(part, layer, row, term):
            turned = [pltpu.roll(value, shift, 1) for value in term]
            zero = jnp.zeros_like(turned[0])
            spread = [
                jnp.where(put_right, turned[0], zero),
                jnp.where(put_right, turned[1], turned[0]),
                jnp.where(put_right, zero, turned[1]),
            ]
            at = pl.ds(start_row + row, CHUNK)
            for k in range(3):
                grad_ref[part, layer, base + k, at, :] = grad_ref[part, layer, base + k, at, :] + spread[k]

        def object_term(layer, row, waves, backs):
            re, im = [], []
            for k in range(2):
                re.append(sum(w[0][k] * b[0][k] + w[1][k] * b[1][k] for w, b in zip(waves, backs)))
                im.append(sum(w[0][k] * b[1][k] - w[1][k] * b[0][k] for w, b in zip(waves, backs)))
            add_term(0, layer, row, re)
            add_term(1, layer, row, im)

        def last_back(row):
            for side in range(2):
                at = row + side * HALF
                backs = [joined(mode, row)[side] for mode in range(MODES)]
                waves = [(pair_of(psi, 0, mode, at), pair_of(psi, 1, mode, at)) for mode in range(MODES)]
                o_re, o_im = pair_of(obj, 0, 1, at), pair_of(obj, 1, 1, at)
                for mode, (b_re, b_im) in enumerate(backs):
                    re = [o_re[k] * b_re[k] + o_im[k] * b_im[k] for k in range(2)]
                    im = [o_re[k] * b_im[k] - o_im[k] * b_re[k] for k in range(2)]
                    put_split(mode, at, re, im)
                object_term(1, at, waves, backs)

        chunks(HALF, last_back)
        right(SUM_L, DIF_L)
        chunks(HALF, middle_spread)
        left(SUM_R, DIF_R)

        def first_back(row):
            for side in range(2):
                at = row + side * HALF
                backs = [joined(mode, row)[side] for mode in range(MODES)]
                waves = [(pair_of(probe_ref, 0, mode, at), pair_of(probe_ref, 1, mode, at)) for mode in range(MODES)]
                o_re, o_im = pair_of(obj, 0, 0, at), pair_of(obj, 1, 0, at)
                for mode, (b_re, b_im) in enumerate(backs):
                    for k, lane in ((0, lo), (1, hi)):
                        spot = (mode, pl.ds(at, CHUNK), lane)
                        probe_grad_ref[(0, *spot)] = probe_grad_ref[(0, *spot)] + (o_re[k] * b_re[k] + o_im[k] * b_im[k])
                        probe_grad_ref[(1, *spot)] = probe_grad_ref[(1, *spot)] + (o_re[k] * b_im[k] - o_im[k] * b_re[k])
                object_term(0, at, waves, backs)

        chunks(HALF, first_back)
        return carry

    lax.fori_loop(0, count_ref[0], one_slot, 0)


def batch_terms(extended, probe_modes, amplitudes, offsets, counts, table):
    vmem = pl.BlockSpec(memory_space=pltpu.VMEM)
    smem = pl.BlockSpec(memory_space=pltpu.SMEM)
    field = pltpu.VMEM((2, 2, SIDE, SIDE), jnp.float32)
    return pl.pallas_call(
        batch_kernel,
        out_shape=(
            jax.ShapeDtypeStruct((2, 2, 4, 2 * SIDE, HALF), jnp.float32),
            jax.ShapeDtypeStruct((2, MODES, SIDE, SIDE), jnp.float32),
        ),
        in_specs=[smem, smem, vmem, vmem, vmem, vmem],
        out_specs=(vmem, vmem),
        scratch_shapes=[
            field,
            field,
            pltpu.VMEM((MODES * SIDE, SIDE), jnp.bfloat16),
            pltpu.VMEM((MODES * SIDE, SIDE), jnp.bfloat16),
            pltpu.VMEM((MODES * SIDE, SIDE), jnp.float32),
            pltpu.VMEM((MODES * SIDE, SIDE), jnp.float32),
            pltpu.VMEM((SIDE, MODES * SIDE), jnp.bfloat16),
            pltpu.VMEM((SIDE, MODES * SIDE), jnp.bfloat16),
            pltpu.VMEM((SIDE, MODES * SIDE), jnp.float32),
            pltpu.VMEM((SIDE, MODES * SIDE), jnp.float32),
        ],
        compiler_params=pltpu.CompilerParams(vmem_limit_bytes=40 << 20),
        cost_estimate=pl.CostEstimate(flops=3 * 64 * SIDE**3, bytes_accessed=12 << 20, transcendentals=0),
    )(offsets, counts, extended, probe_modes, amplitudes, table)


def from_behind(value, axis, steps):
    count = lax.axis_size(axis)
    leading, last = (max(0, -steps), min(count, count - steps))
    return lax.ppermute(value, axis, [(source, source + steps) for source in range(leading, last)])


def with_halo(array, sides, width):
    for axis, dim in sides:
        length = array.shape[dim]
        last = lax.slice_in_dim(array, length - width, length, axis=dim)
        leading = lax.slice_in_dim(array, 0, width, axis=dim)
        before = from_behind(last, axis, 1)
        after = from_behind(leading, axis, -1)
        array = jnp.concatenate([before, array, after], axis=dim)
    return array


def return_sectioned(gradient, rim_width, tile_cells):
    rim_start = rim_width + tile_cells
    rim_end = tile_cells - rim_width
    from_left = from_behind(gradient[:, :, :, rim_start:], "col", 1)
    from_right = from_behind(gradient[:, :, :, :rim_width], "col", -1)
    middle = gradient[:, :, :, rim_width:rim_start]
    middle = middle.at[:, :, :, :rim_width].add(from_left)
    middle = middle.at[:, :, :, rim_end:].add(from_right)
    from_above = from_behind(middle[:, :, rim_start:, :], "row", 1)
    from_below = from_behind(middle[:, :, :rim_width, :], "row", -1)
    tile_grad = middle[:, :, rim_width:rim_start, :]
    tile_grad = tile_grad.at[:, :, :rim_width, :].add(from_above)
    tile_grad = tile_grad.at[:, :, rim_end:, :].add(from_below)
    return tile_grad


def body(object_field, probe_modes, amplitudes, offsets, counts):
    batches, slots = amplitudes.shape[:2]
    table = jnp.asarray(TABLES)
    ordered = reorder(amplitudes.reshape(batches * slots, SIDE, SIDE)).reshape(batches, slots, SIDE, SIDE)
    current = object_field
    probe_total = None
    for batch in range(batches):
        extended = with_halo(current, (("row", 2), ("col", 3)), HALF)
        extended = extended.reshape(2, 2, 2 * SIDE, 4, HALF).transpose(0, 1, 3, 2, 4)
        gradient, probe_part = batch_terms(
            extended, probe_modes, ordered[batch], offsets[batch, :, :, 0], counts[batch, 0], table
        )
        gradient = gradient.transpose(0, 1, 3, 2, 4).reshape(2, 2, 2 * SIDE, 2 * SIDE)
        current = current - OBJECT_STEP * return_sectioned(gradient, HALF, SIDE)
        probe_total = probe_part if probe_total is None else probe_total + probe_part
    return (current, probe_modes - PROBE_STEP * lax.psum(probe_total, ("row", "col")))


def solution(mesh):
    return jax.shard_map(
        body,
        mesh=mesh,
        in_specs=(
            P(None, None, "row", "col"),
            P(),
            P(None, "row", "col", None, None),
            P(None, None, "row", "col"),
            P(None, "row", "col"),
        ),
        out_specs=(P(None, None, "row", "col"), P()),
        check_vma=False,
    )
```

```python
import math

import jax
import jax.numpy as jnp
import numpy as np
from jax import lax
from jax.experimental import pallas as pl
from jax.experimental.pallas import tpu as pltpu
from jax.sharding import PartitionSpec as P

AMPLITUDE_FLOOR = 0.5
OBJECT_STEP = 0.25
PROBE_STEP = 0.125
SIDE = 256
HALF = SIDE // 2
MODES = 2
CHUNK = 16
MESH = pl.DeviceIdType.MESH
SIDES = ("up", "down", "left", "right")
OPPOSITE = {"up": "down", "down": "up", "left": "right", "right": "left"}


def real_form(table):
    re, im = table.real, table.imag
    return np.block([[re, im], [-im, re]]).astype(jnp.bfloat16)


def make_tables():
    index = np.arange(SIDE)
    angles = (index[:, None] * index[None, :] % SIDE).astype(np.float32) * np.float32(2.0 * math.pi / SIDE)
    scale = np.float32(1.0 / math.sqrt(SIDE))
    rounded = lambda v: (v * scale).astype(jnp.bfloat16).astype(np.float64)
    forward = rounded(np.cos(angles)) - 1j * rounded(np.sin(angles))
    frequency = np.where(index < HALF, index, index - SIDE).astype(np.float64)
    chirp = np.exp(-2j * math.pi * (frequency * frequency % (16 * SIDE)) / (16 * SIDE))
    spread = (forward.conj() * chirp[None, :]) @ forward
    same = 0.25 * (spread[:HALF, :HALF] + spread[HALF:, HALF:] + spread[:HALF, HALF:] + spread[HALF:, :HALF])
    other = 0.25 * (spread[:HALF, :HALF] + spread[HALF:, HALF:] - spread[:HALF, HALF:] - spread[HALF:, :HALF])
    same = 0.5 * (same + same.T)
    other = 0.5 * (other + other.T)
    even = forward[:HALF, 0::2]
    odd = forward[:HALF, 1::2]
    rows = []
    for table in (same, other, even, odd):
        matrix = real_form(table)
        rows += [matrix, np.ascontiguousarray(matrix.T)]
    order = np.zeros((SIDE, SIDE), np.float32)
    order[0::2, :HALF] = np.eye(HALF)
    order[1::2, HALF:] = np.eye(HALF)
    return np.stack(rows), order.astype(jnp.bfloat16)


TABLES, ORDER = make_tables()
(SUM_R, SUM_L, DIF_R, DIF_L, EVEN_R, EVEN_L, ODD_R, ODD_L) = range(8)


def dot(left, right):
    return jnp.dot(left, right, preferred_element_type=jnp.float32)


def three_parts(value):
    high = value.astype(jnp.bfloat16)
    rest = value - high.astype(jnp.float32)
    middle = rest.astype(jnp.bfloat16)
    return high, middle, (rest - middle.astype(jnp.float32)).astype(jnp.bfloat16)


def reorder_plane(plane, order, turn):
    high, middle, low = [dot(part, order) for part in three_parts(plane)]
    high, middle, low = [dot(turn, part) for part in three_parts(high + (middle + low))]
    return high + (middle + low)


class Links:
    def __init__(self, send_sems, recv_sems):
        self.row, self.col = lax.axis_index("row"), lax.axis_index("col")
        rows, cols = lax.axis_size("row"), lax.axis_size("col")
        self.has = {
            "up": self.row > 0,
            "down": self.row < rows - 1,
            "left": self.col > 0,
            "right": self.col < cols - 1,
        }
        self.at = {
            "up": (self.row - 1, self.col),
            "down": (self.row + 1, self.col),
            "left": (self.row, self.col - 1),
            "right": (self.row, self.col + 1),
        }
        self.send_sems, self.recv_sems = send_sems, recv_sems
        self.used = 0
        self.sent = []

    def greet(self, peers=()):
        barrier = pltpu.get_barrier_semaphore()
        for side in SIDES:

            @pl.when(self.has[side])
            def _():
                pl.semaphore_signal(barrier, inc=1, device_id=self.at[side], device_id_type=MESH)

        for peer in peers:
            pl.semaphore_signal(barrier, inc=1, device_id=peer, device_id_type=MESH)
        pl.semaphore_wait(barrier, len(peers) + sum(self.has[side].astype(jnp.int32) for side in SIDES))

    def copy(self, source, target, device):
        index = self.used
        self.used += 1
        return pltpu.make_async_remote_copy(
            src_ref=source,
            dst_ref=target,
            send_sem=self.send_sems.at[index],
            recv_sem=self.recv_sems.at[index],
            device_id=device,
            device_id_type=MESH,
        )

    def send(self, source, target, side, also=None):
        item = self.copy(source, target, self.at[side])
        condition = self.has[side] if also is None else jnp.logical_and(self.has[side], also)

        @pl.when(condition)
        def _():
            item.start()

        self.sent.append((item, condition))
        source_side = self.has[OPPOSITE[side]]
        arrives = source_side if also is None else jnp.logical_and(source_side, also)

        def arrived():
            @pl.when(arrives)
            def _():
                item.wait_recv()

        return arrived

    def finish(self):
        for item, condition in self.sent:

            @pl.when(condition)
            def _():
                item.wait_send()


def by_rows(start, stop, step, body):
    def one(index, carry):
        body(pl.ds(pl.multiple_of(start + index * step, 8), step))
        return carry

    lax.fori_loop(0, (stop - start) // step, one, 0)


def first_kernel(tile_ref, amp_ref, order_ref, turn_ref, ext_ref, ordered_ref, send_sems, recv_sems):
    links = Links(send_sems, recv_sems)
    links.greet()
    upper, lower, own = pl.ds(0, HALF), pl.ds(3 * HALF, HALF), pl.ds(HALF, SIDE)
    waits, col_waits, corner_waits = [], [], []
    for layer in range(2):
        arrivals = []
        for block in range(2):
            lane = pl.ds(block * HALF, HALF)
            arrivals.append(
                links.send(tile_ref.at[:, layer, pl.ds(0, HALF), lane], ext_ref.at[:, layer, 1 + block, lower], "up")
            )
            arrivals.append(
                links.send(tile_ref.at[:, layer, pl.ds(HALF, HALF), lane], ext_ref.at[:, layer, 1 + block, upper], "down")
            )
        waits.append(arrivals)
    for layer in range(2):
        col_waits.append(links.send(tile_ref.at[:, layer, :, pl.ds(0, HALF)], ext_ref.at[:, layer, 3, own], "left"))
        col_waits.append(links.send(tile_ref.at[:, layer, :, pl.ds(HALF, HALF)], ext_ref.at[:, layer, 0, own], "right"))

    def clear(side, blocks, rows):
        @pl.when(jnp.logical_not(links.has[side]))
        def _():
            for part in range(2):
                for layer in range(2):
                    for block in blocks:
                        ext_ref[part, layer, block, rows, :] = jnp.zeros((rows.size, HALF), jnp.float32)

    clear("up", (1, 2), upper)
    clear("down", (1, 2), lower)
    clear("left", (0,), own)
    clear("right", (3,), own)
    for rows, side in ((upper, "up"), (lower, "down")):
        for block, other in ((0, "left"), (3, "right")):

            @pl.when(jnp.logical_not(jnp.logical_and(links.has[side], links.has[other])))
            def _():
                for part in range(2):
                    for layer in range(2):
                        ext_ref[part, layer, block, rows, :] = jnp.zeros((HALF, HALF), jnp.float32)

    for part in range(2):
        for layer in range(2):
            for block in range(2):
                ext_ref[part, layer, 1 + block, own, :] = tile_ref[part, layer, :, block * HALF : (block + 1) * HALF]

    def one_plane(index, carry):
        ordered_ref[index] = reorder_plane(amp_ref[index], order_ref[...], turn_ref[...])
        return carry

    lax.fori_loop(0, amp_ref.shape[0], one_plane, 0)
    for layer in range(2):
        for arrived in waits[layer]:
            arrived()
        for rows, side in ((upper, "up"), (lower, "down")):
            for block, to, target in ((1, "left", 3), (2, "right", 0)):
                corner_waits.append(
                    links.send(
                        ext_ref.at[:, layer, block, rows], ext_ref.at[:, layer, target, rows], to, also=links.has[side]
                    )
                )
    for arrived in col_waits + corner_waits:
        arrived()
    links.finish()


def collect_columns(links, grad_ref, from_left, from_right, total, order):
    for side, buffer in (("left", from_left), ("right", from_right)):

        @pl.when(jnp.logical_not(links.has[side]))
        def _():
            for part, layer in order:
                buffer[part, layer] = jnp.zeros((2 * SIDE, HALF), jnp.float32)

    arrivals = []
    for part, layer in order:
        arrivals.append(
            (
                links.send(grad_ref.at[part, layer, 0], from_right.at[part, layer], "left"),
                links.send(grad_ref.at[part, layer, 3], from_left.at[part, layer], "right"),
            )
        )

    def finish(index):
        part, layer = order[index]
        for arrived in arrivals[index]:
            arrived()

        def add(rows):
            total[part, layer, 0, rows, :] = grad_ref[part, layer, 1, rows, :] + from_left[part, layer, rows, :]
            total[part, layer, 1, rows, :] = grad_ref[part, layer, 2, rows, :] + from_right[part, layer, rows, :]

        by_rows(0, 2 * SIDE, 64, add)

    return finish


PLANES = [(part, layer) for layer in range(2) for part in range(2)]


def middle_kernel(ext_ref, grad_ref, out_ref, from_left, from_right, from_up, from_down, total, send_sems, recv_sems):
    links = Links(send_sems, recv_sems)
    links.greet()
    finish_columns = collect_columns(links, grad_ref, from_left, from_right, total, PLANES)
    for side, buffer in (("up", from_up), ("down", from_down)):

        @pl.when(jnp.logical_not(links.has[side]))
        def _():
            for part, layer in PLANES:
                buffer[part, layer] = jnp.zeros((2, SIDE, HALF), jnp.float32)

    for side, block in (("left", 0), ("right", 3)):

        @pl.when(jnp.logical_not(links.has[side]))
        def _():
            for part, layer in PLANES:
                out_ref[part, layer, block] = jnp.zeros((2 * SIDE, HALF), jnp.float32)

    arrivals = []
    for index, (part, layer) in enumerate(PLANES):
        finish_columns(index)
        arrivals.append(
            (
                links.send(total.at[part, layer, :, pl.ds(0, SIDE)], from_down.at[part, layer], "up"),
                links.send(total.at[part, layer, :, pl.ds(SIDE, SIDE)], from_up.at[part, layer], "down"),
            )
        )
    step_up = jnp.where(links.has["up"], OBJECT_STEP, 0.0).astype(jnp.float32)
    step_down = jnp.where(links.has["down"], OBJECT_STEP, 0.0).astype(jnp.float32)
    halos = []
    for index, (part, layer) in enumerate(PLANES):
        for arrived in arrivals[index]:
            arrived()
        for block in range(2):
            for start, buffer, offset, step in (
                (0, from_up, 0, step_up),
                (HALF, from_up, 0, OBJECT_STEP),
                (SIDE, from_down, SIDE, OBJECT_STEP),
                (3 * HALF, from_down, SIDE, step_down),
            ):
                for row in range(start, start + HALF, 64):
                    rows, near = pl.ds(row, 64), pl.ds(row - offset, 64)
                    gradient = total[part, layer, block, rows, :] + buffer[part, layer, block, near, :]
                    out_ref[part, layer, 1 + block, rows, :] = ext_ref[part, layer, 1 + block, rows, :] - step * gradient
        halos.append(links.send(out_ref.at[part, layer, 1], out_ref.at[part, layer, 3], "left"))
        halos.append(links.send(out_ref.at[part, layer, 2], out_ref.at[part, layer, 0], "right"))
    for arrived in halos:
        arrived()
    links.finish()


def last_kernel(
    ext_ref, grad_ref, first_probe_ref, second_probe_ref, probe_ref, object_ref, new_probe_ref,
    from_left, from_right, from_up, from_down, total, partial, pair, quarters, sums, gathered, send_sems, recv_sems,
):
    links = Links(send_sems, recv_sems)
    row, col = links.row, links.col
    core, x, y_low = lax.rem(col, 2), lax.rem(col // 2, 4), col // 8
    y_high, z = lax.rem(row, 2), row // 2
    y = y_high * 2 + y_low
    partner = (row, col + 1 - 2 * core)
    groups = [
        (z, lambda k: (k * 2 + y_high, col)),
        (x, lambda k: (row, y_low * 8 + k * 2 + core)),
        (y, lambda k: (z * 2 + k // 2, lax.rem(k, 2) * 8 + x * 2 + core)),
    ]
    peers = [partner]
    for place, device in groups:
        peers += [device(lax.rem(place + k, 4)) for k in range(1, 4)]
    links.greet(peers)
    finish_columns = collect_columns(links, grad_ref, from_left, from_right, total, PLANES)
    count = 4 * SIDE
    half = count // 2

    def rows_at(start, size):
        return pl.ds(pl.multiple_of(start, 8), size)

    def start(source, target, device):
        item = links.copy(source, target, device)
        item.start()
        return item

    def add_probe(rows):
        partial[rows, :] = first_probe_ref[rows, :] + second_probe_ref[rows, :]

    by_rows(0, count, 64, add_probe)
    swap = start(partial.at[rows_at((1 - core) * half, half)], pair, partner)
    for side, buffer in (("up", from_up), ("down", from_down)):

        @pl.when(jnp.logical_not(links.has[side]))
        def _():
            for part, layer in PLANES:
                buffer[part, layer] = jnp.zeros((2, HALF, HALF), jnp.float32)

    arrivals = []
    for index, (part, layer) in enumerate(PLANES):
        finish_columns(index)
        arrivals.append(
            (
                links.send(total.at[part, layer, :, pl.ds(0, HALF)], from_down.at[part, layer], "up"),
                links.send(total.at[part, layer, :, pl.ds(3 * HALF, HALF)], from_up.at[part, layer], "down"),
            )
        )
    swap.wait_recv()
    base = core * half

    def add_pair(index, carry):
        near = pl.ds(pl.multiple_of(index * 64, 64), 64)
        mine = rows_at(base + index * 64, 64)
        sums[mine, :] = partial[mine, :] + pair[near, :]
        return carry

    lax.fori_loop(0, half // 64, add_pair, 0)
    size = half
    places = []
    for number, (place, device) in enumerate(groups):
        size = size // 4
        landing = quarters[number]
        items = []
        for k in range(1, 4):
            other = lax.rem(place + k, 4)
            items.append(start(sums.at[rows_at(base + other * size, size)], landing.at[k - 1], device(other)))
        places.append((place, device, base, size))
        base = base + place * size
        for item in items:
            item.wait_recv()
        for item in items:
            item.wait_send()
        for begin in range(0, size, 32):
            step = min(32, size)
            mine = rows_at(base + begin, step)
            value = sums[mine, :]
            for k in range(3):
                value = value + landing[k, pl.ds(begin, step), :]
            (gathered if number == 2 else sums)[mine, :] = value
    gathers = [swap]
    for place, device, group_base, size in reversed(places):
        mine = rows_at(group_base + place * size, size)
        items = [start(gathered.at[mine], gathered.at[mine], device(lax.rem(place + k, 4))) for k in range(1, 4)]
        gathers += items
        for item in items:
            item.wait_recv()
    mine = rows_at(core * half, half)
    swap_back = start(gathered.at[mine], gathered.at[mine], partner)
    for index, (part, layer) in enumerate(PLANES):
        for arrived in arrivals[index]:
            arrived()
        for block in range(2):
            lane = pl.ds(block * HALF, HALF)
            for begin, buffer in ((HALF, from_up), (SIDE, from_down)):
                for offset in range(0, HALF, 64):
                    rows, near = pl.ds(begin + offset, 64), pl.ds(offset, 64)
                    gradient = total[part, layer, block, rows, :] + buffer[part, layer, block, near, :]
                    target = pl.ds(begin - HALF + offset, 64)
                    object_ref[part, layer, target, lane] = (
                        ext_ref[part, layer, 1 + block, rows, :] - OBJECT_STEP * gradient
                    )
    swap_back.wait_recv()

    def finish_probe(rows):
        new_probe_ref[rows, :] = probe_ref[rows, :] - PROBE_STEP * gathered[rows, :]

    by_rows(0, count, 64, finish_probe)
    for item in gathers + [swap_back]:
        item.wait_send()
    links.finish()


def vmem_specs(count):
    return [pl.BlockSpec(memory_space=pltpu.VMEM)] * count


def comm_params(identity):
    return pltpu.CompilerParams(collective_id=identity, has_side_effects=True, vmem_limit_bytes=48 << 20)


def semaphores(count):
    return [pltpu.SemaphoreType.DMA((count,)), pltpu.SemaphoreType.DMA((count,))]


EXTENDED = jax.ShapeDtypeStruct((2, 2, 4, 2 * SIDE, HALF), jnp.float32)


def first_exchange(tile, amplitudes):
    slots = amplitudes.shape[0]
    return pl.pallas_call(
        first_kernel,
        out_shape=(EXTENDED, jax.ShapeDtypeStruct((slots, SIDE, SIDE), jnp.float32)),
        in_specs=vmem_specs(4),
        out_specs=tuple(vmem_specs(2)),
        scratch_shapes=semaphores(20),
        compiler_params=comm_params(0),
    )(tile, amplitudes, jnp.asarray(ORDER), jnp.asarray(ORDER.T))


def columns_buffers():
    return [pltpu.VMEM((2, 2, 2 * SIDE, HALF), jnp.float32)] * 2


def middle_exchange(extended, gradient):
    return pl.pallas_call(
        middle_kernel,
        out_shape=EXTENDED,
        in_specs=vmem_specs(2),
        out_specs=vmem_specs(1)[0],
        scratch_shapes=[
            *columns_buffers(),
            *[pltpu.VMEM((2, 2, 2, SIDE, HALF), jnp.float32)] * 2,
            pltpu.VMEM((2, 2, 2, 2 * SIDE, HALF), jnp.float32),
            *semaphores(24),
        ],
        compiler_params=comm_params(1),
    )(extended, gradient)


def last_exchange(extended, gradient, first_probe, second_probe, probe_modes):
    flat = (4 * SIDE, SIDE)
    new_object, new_probe = pl.pallas_call(
        last_kernel,
        out_shape=(
            jax.ShapeDtypeStruct((2, 2, SIDE, SIDE), jnp.float32),
            jax.ShapeDtypeStruct(flat, jnp.float32),
        ),
        in_specs=vmem_specs(5),
        out_specs=tuple(vmem_specs(2)),
        scratch_shapes=[
            *columns_buffers(),
            *[pltpu.VMEM((2, 2, 2, HALF, HALF), jnp.float32)] * 2,
            pltpu.VMEM((2, 2, 2, 2 * SIDE, HALF), jnp.float32),
            pltpu.VMEM(flat, jnp.float32),
            pltpu.VMEM((2 * SIDE, SIDE), jnp.float32),
            [pltpu.VMEM((3, 2 * SIDE // 4**k, SIDE), jnp.float32) for k in (1, 2, 3)],
            pltpu.VMEM(flat, jnp.float32),
            pltpu.VMEM(flat, jnp.float32),
            *semaphores(36),
        ],
        compiler_params=comm_params(2),
    )(extended, gradient, first_probe.reshape(flat), second_probe.reshape(flat), probe_modes.reshape(flat))
    return new_object, new_probe.reshape(probe_modes.shape)


def batch_kernel(
    offset_ref, count_ref, ext_ref, probe_ref, amp_ref, table_ref, grad_ref, probe_grad_ref,
    obj, psi, right_a, right_b, yield_a, yield_b, left_a, left_b, out_a, out_b,
):
    lanes = lax.broadcasted_iota(jnp.int32, (CHUNK, HALF), 1)
    lo, hi = pl.ds(0, HALF), pl.ds(HALF, HALF)

    def chunks(total, body):
        def step(index, carry):
            body(pl.multiple_of(index * CHUNK, CHUNK))
            return carry

        lax.fori_loop(0, total // CHUNK, step, 0)

    def bf(value):
        return value.astype(jnp.bfloat16)

    def zero_grad(row):
        for part in range(2):
            for layer in range(2):
                for block in range(4):
                    grad_ref[part, layer, block, pl.ds(row, CHUNK), :] = jnp.zeros((CHUNK, HALF), jnp.float32)

    chunks(2 * SIDE, zero_grad)

    def zero_probe(row):
        for part in range(2):
            for mode in range(MODES):
                probe_grad_ref[part, mode, pl.ds(row, CHUNK), :] = jnp.zeros((CHUNK, SIDE), jnp.float32)

    chunks(SIDE, zero_probe)

    def right(table_a, table_b):
        yield_a[...] = dot(right_a[...], table_ref[table_a])
        yield_b[...] = dot(right_b[...], table_ref[table_b])

    def left(table_a, table_b):
        out_a[...] = dot(table_ref[table_a], left_a[...])
        out_b[...] = dot(table_ref[table_b], left_b[...])

    def put_split(mode, row, re, im):
        at = pl.ds(mode * SIDE + row, CHUNK)
        right_a[at, lo] = bf(re[0] + re[1])
        right_a[at, hi] = bf(im[0] + im[1])
        right_b[at, lo] = bf(re[0] - re[1])
        right_b[at, hi] = bf(im[0] - im[1])

    def columns(ref, mode):
        return pl.ds(mode * SIDE, HALF), pl.ds(mode * SIDE + HALF, HALF)

    def middle_spread(row):
        for mode in range(MODES):
            here = columns(left_a, mode)
            for part, lane in ((0, lo), (1, hi)):
                top = pl.ds(mode * SIDE + row, CHUNK)
                low = pl.ds(mode * SIDE + HALF + row, CHUNK)
                at, ab = yield_a[top, lane], yield_a[low, lane]
                bt, bb = yield_b[top, lane], yield_b[low, lane]
                to = pl.ds(part * HALF + row, CHUNK)
                a_sum, a_dif = at + ab, at - ab
                b_sum, b_dif = bt + bb, bt - bb
                left_a[to, here[0]] = bf(a_sum + b_sum)
                left_a[to, here[1]] = bf(a_sum - b_sum)
                left_b[to, here[0]] = bf(a_dif + b_dif)
                left_b[to, here[1]] = bf(a_dif - b_dif)

    def middle_forward(row):
        for mode in range(MODES):
            here = columns(left_a, mode)
            for part, lane in ((0, lo), (1, hi)):
                top = pl.ds(mode * SIDE + row, CHUNK)
                low = pl.ds(mode * SIDE + HALF + row, CHUNK)
                to = pl.ds(part * HALF + row, CHUNK)
                for source, at in ((yield_a, here[0]), (yield_b, here[1])):
                    upper, lower = source[top, lane], source[low, lane]
                    left_a[to, at] = bf(upper + lower)
                    left_b[to, at] = bf(upper - lower)

    def middle_backward(row):
        for mode in range(MODES):
            here = columns(left_a, mode)
            for part, lane in ((0, lo), (1, hi)):
                to = pl.ds(part * HALF + row, CHUNK)
                for base, target in ((0, left_a), (HALF, left_b)):
                    at = pl.ds(mode * SIDE + base + row, CHUNK)
                    even, odd = yield_a[at, lane], yield_b[at, lane]
                    target[to, here[0]] = bf(even + odd)
                    target[to, here[1]] = bf(even - odd)

    def joined(mode, row):
        result = []
        for sign in (1, -1):
            pair = []
            for part in range(2):
                at = pl.ds(part * HALF + row, CHUNK)
                halves = []
                for lane in columns(out_a, mode):
                    a, b = out_a[at, lane], out_b[at, lane]
                    halves.append(a + b if sign > 0 else a - b)
                pair.append(halves)
            result.append(pair)
        return result

    def pair_of(ref, first, second, row):
        return [ref[first, second, pl.ds(row, CHUNK), lane] for lane in (lo, hi)]

    def one_slot(slot, carry):
        start_row = offset_ref[0, slot]
        start_col = offset_ref[1, slot]
        base = start_col // HALF
        shift = start_col % HALF
        take_left = lanes < HALF - shift
        put_right = lanes >= shift
        back = lax.rem(HALF - shift, HALF)

        def fetch(row):
            for part in range(2):
                for layer in range(2):
                    at = pl.ds(start_row + row, CHUNK)
                    turned = [pltpu.roll(ext_ref[part, layer, base + k, at, :], back, 1) for k in range(3)]
                    obj[part, layer, pl.ds(row, CHUNK), lo] = jnp.where(take_left, turned[0], turned[1])
                    obj[part, layer, pl.ds(row, CHUNK), hi] = jnp.where(take_left, turned[1], turned[2])

        chunks(SIDE, fetch)

        def enter(row):
            o_re, o_im = pair_of(obj, 0, 0, row), pair_of(obj, 1, 0, row)
            for mode in range(MODES):
                p_re, p_im = pair_of(probe_ref, 0, mode, row), pair_of(probe_ref, 1, mode, row)
                re = [p_re[k] * o_re[k] - p_im[k] * o_im[k] for k in range(2)]
                im = [p_re[k] * o_im[k] + p_im[k] * o_re[k] for k in range(2)]
                put_split(mode, row, re, im)

        chunks(SIDE, enter)
        right(SUM_R, DIF_R)
        chunks(HALF, middle_spread)
        left(SUM_L, DIF_L)

        def second_slice(row):
            for side in range(2):
                at = row + side * HALF
                o_re, o_im = pair_of(obj, 0, 1, at), pair_of(obj, 1, 1, at)
                for mode in range(MODES):
                    w_re, w_im = joined(mode, row)[side]
                    for k, lane in ((0, lo), (1, hi)):
                        psi[0, mode, pl.ds(at, CHUNK), lane] = w_re[k]
                        psi[1, mode, pl.ds(at, CHUNK), lane] = w_im[k]
                    re = [w_re[k] * o_re[k] - w_im[k] * o_im[k] for k in range(2)]
                    im = [w_re[k] * o_im[k] + w_im[k] * o_re[k] for k in range(2)]
                    put_split(mode, at, re, im)

        chunks(HALF, second_slice)
        right(EVEN_R, ODD_R)
        chunks(HALF, middle_forward)
        left(EVEN_L, ODD_L)

        def compare(row):
            for base_row, source in ((0, out_a), (HALF, out_b)):
                waves = []
                for mode in range(MODES):
                    here = columns(source, mode)
                    re = [source[pl.ds(row, CHUNK), lane] for lane in here]
                    im = [source[pl.ds(HALF + row, CHUNK), lane] for lane in here]
                    waves.append((re, im))
                for k, lane in ((0, lo), (1, hi)):
                    intensity = waves[0][0][k] * waves[0][0][k] + waves[0][1][k] * waves[0][1][k]
                    for re, im in waves[1:]:
                        intensity = intensity + (re[k] * re[k] + im[k] * im[k])
                    amplitude = amp_ref[slot, pl.ds(base_row + row, CHUNK), lane]
                    ratio = 1.0 - amplitude * lax.rsqrt(jnp.maximum(intensity, AMPLITUDE_FLOOR**2))
                    target = right_a if k == 0 else right_b
                    for mode, (re, im) in enumerate(waves):
                        at = pl.ds(mode * SIDE + base_row + row, CHUNK)
                        target[at, lo] = bf(re[k] * ratio)
                        target[at, hi] = bf(im[k] * ratio)

        chunks(HALF, compare)
        right(EVEN_L, ODD_L)
        chunks(HALF, middle_backward)
        left(EVEN_R, ODD_R)

        def add_term(part, layer, row, term):
            turned = [pltpu.roll(value, shift, 1) for value in term]
            zero = jnp.zeros_like(turned[0])
            spread = [
                jnp.where(put_right, turned[0], zero),
                jnp.where(put_right, turned[1], turned[0]),
                jnp.where(put_right, zero, turned[1]),
            ]
            at = pl.ds(start_row + row, CHUNK)
            for k in range(3):
                grad_ref[part, layer, base + k, at, :] = grad_ref[part, layer, base + k, at, :] + spread[k]

        def object_term(layer, row, waves, backs):
            re, im = [], []
            for k in range(2):
                re.append(sum(w[0][k] * b[0][k] + w[1][k] * b[1][k] for w, b in zip(waves, backs)))
                im.append(sum(w[0][k] * b[1][k] - w[1][k] * b[0][k] for w, b in zip(waves, backs)))
            add_term(0, layer, row, re)
            add_term(1, layer, row, im)

        def last_back(row):
            for side in range(2):
                at = row + side * HALF
                backs = [joined(mode, row)[side] for mode in range(MODES)]
                waves = [(pair_of(psi, 0, mode, at), pair_of(psi, 1, mode, at)) for mode in range(MODES)]
                o_re, o_im = pair_of(obj, 0, 1, at), pair_of(obj, 1, 1, at)
                for mode, (b_re, b_im) in enumerate(backs):
                    re = [o_re[k] * b_re[k] + o_im[k] * b_im[k] for k in range(2)]
                    im = [o_re[k] * b_im[k] - o_im[k] * b_re[k] for k in range(2)]
                    put_split(mode, at, re, im)
                object_term(1, at, waves, backs)

        chunks(HALF, last_back)
        right(SUM_L, DIF_L)
        chunks(HALF, middle_spread)
        left(SUM_R, DIF_R)

        def first_back(row):
            for side in range(2):
                at = row + side * HALF
                backs = [joined(mode, row)[side] for mode in range(MODES)]
                waves = [(pair_of(probe_ref, 0, mode, at), pair_of(probe_ref, 1, mode, at)) for mode in range(MODES)]
                o_re, o_im = pair_of(obj, 0, 0, at), pair_of(obj, 1, 0, at)
                for mode, (b_re, b_im) in enumerate(backs):
                    for k, lane in ((0, lo), (1, hi)):
                        spot = (mode, pl.ds(at, CHUNK), lane)
                        probe_grad_ref[(0, *spot)] = probe_grad_ref[(0, *spot)] + (o_re[k] * b_re[k] + o_im[k] * b_im[k])
                        probe_grad_ref[(1, *spot)] = probe_grad_ref[(1, *spot)] + (o_re[k] * b_im[k] - o_im[k] * b_re[k])
                object_term(0, at, waves, backs)

        chunks(HALF, first_back)
        return carry

    lax.fori_loop(0, count_ref[0], one_slot, 0)


def batch_terms(extended, probe_modes, amplitudes, offsets, counts, table):
    vmem = pl.BlockSpec(memory_space=pltpu.VMEM)
    smem = pl.BlockSpec(memory_space=pltpu.SMEM)
    field = pltpu.VMEM((2, 2, SIDE, SIDE), jnp.float32)
    return pl.pallas_call(
        batch_kernel,
        out_shape=(
            jax.ShapeDtypeStruct((2, 2, 4, 2 * SIDE, HALF), jnp.float32),
            jax.ShapeDtypeStruct((2, MODES, SIDE, SIDE), jnp.float32),
        ),
        in_specs=[smem, smem, vmem, vmem, vmem, vmem],
        out_specs=(vmem, vmem),
        scratch_shapes=[
            field,
            field,
            pltpu.VMEM((MODES * SIDE, SIDE), jnp.bfloat16),
            pltpu.VMEM((MODES * SIDE, SIDE), jnp.bfloat16),
            pltpu.VMEM((MODES * SIDE, SIDE), jnp.float32),
            pltpu.VMEM((MODES * SIDE, SIDE), jnp.float32),
            pltpu.VMEM((SIDE, MODES * SIDE), jnp.bfloat16),
            pltpu.VMEM((SIDE, MODES * SIDE), jnp.bfloat16),
            pltpu.VMEM((SIDE, MODES * SIDE), jnp.float32),
            pltpu.VMEM((SIDE, MODES * SIDE), jnp.float32),
        ],
        compiler_params=pltpu.CompilerParams(vmem_limit_bytes=40 << 20),
        cost_estimate=pl.CostEstimate(flops=3 * 64 * SIDE**3, bytes_accessed=12 << 20, transcendentals=0),
    )(offsets, counts, extended, probe_modes, amplitudes, table)


def body(object_field, probe_modes, amplitudes, offsets, counts):
    batches, slots = amplitudes.shape[:2]
    table = jnp.asarray(TABLES)
    extended, ordered = first_exchange(object_field, amplitudes.reshape(batches * slots, SIDE, SIDE))
    ordered = ordered.reshape(batches, slots, SIDE, SIDE)
    terms = lambda cells, batch: batch_terms(
        cells, probe_modes, ordered[batch], offsets[batch, :, :, 0], counts[batch, 0], table
    )
    gradient, first_probe = terms(extended, 0)
    extended = middle_exchange(extended, gradient)
    gradient, second_probe = terms(extended, 1)
    return last_exchange(extended, gradient, first_probe, second_probe, probe_modes)


def solution(mesh):
    return jax.shard_map(
        body,
        mesh=mesh,
        in_specs=(
            P(None, None, "row", "col"),
            P(),
            P(None, "row", "col", None, None),
            P(None, None, "row", "col"),
            P(None, "row", "col"),
        ),
        out_specs=(P(None, None, "row", "col"), P()),
        check_vma=False,
    )
```

```python
import functools
import math

import jax
import jax.numpy as jnp
import numpy as np
from jax import lax
from jax.experimental import pallas as pl
from jax.experimental.pallas import tpu as pltpu
from jax.sharding import PartitionSpec as P

AMPLITUDE_FLOOR = 0.5
OBJECT_STEP = 0.25
PROBE_STEP = 0.125
SIDE = 256
HALF = SIDE // 2
MODES = 2
CHUNK = 16
MESH = pl.DeviceIdType.MESH
SIDES = ("up", "down", "left", "right")
OPPOSITE = {"up": "down", "down": "up", "left": "right", "right": "left"}


def real_form(table):
    re, im = table.real, table.imag
    return np.block([[re, im], [-im, re]]).astype(jnp.bfloat16)


def make_tables():
    index = np.arange(SIDE)
    angles = (index[:, None] * index[None, :] % SIDE).astype(np.float32) * np.float32(2.0 * math.pi / SIDE)
    scale = np.float32(1.0 / math.sqrt(SIDE))
    rounded = lambda v: (v * scale).astype(jnp.bfloat16).astype(np.float64)
    forward = rounded(np.cos(angles)) - 1j * rounded(np.sin(angles))
    frequency = np.where(index < HALF, index, index - SIDE).astype(np.float64)
    chirp = np.exp(-2j * math.pi * (frequency * frequency % (16 * SIDE)) / (16 * SIDE))
    spread = (forward.conj() * chirp[None, :]) @ forward
    same = 0.25 * (spread[:HALF, :HALF] + spread[HALF:, HALF:] + spread[:HALF, HALF:] + spread[HALF:, :HALF])
    other = 0.25 * (spread[:HALF, :HALF] + spread[HALF:, HALF:] - spread[:HALF, HALF:] - spread[HALF:, :HALF])
    same = 0.5 * (same + same.T)
    other = 0.5 * (other + other.T)
    even = forward[:HALF, 0::2]
    odd = forward[:HALF, 1::2]
    rows = []
    for table in (same, other, even, odd):
        matrix = real_form(table)
        rows += [matrix, np.ascontiguousarray(matrix.T)]
    order = np.zeros((SIDE, SIDE), np.float32)
    order[0::2, :HALF] = np.eye(HALF)
    order[1::2, HALF:] = np.eye(HALF)
    return np.stack(rows), order.astype(jnp.bfloat16)


TABLES, ORDER = make_tables()
(SUM_R, SUM_L, DIF_R, DIF_L, EVEN_R, EVEN_L, ODD_R, ODD_L) = range(8)


def dot(left, right):
    return jnp.dot(left, right, preferred_element_type=jnp.float32)


def three_parts(value):
    high = value.astype(jnp.bfloat16)
    rest = value - high.astype(jnp.float32)
    middle = rest.astype(jnp.bfloat16)
    return high, middle, (rest - middle.astype(jnp.float32)).astype(jnp.bfloat16)


def reorder_plane(plane, order, turn):
    high, middle, low = [dot(part, order) for part in three_parts(plane)]
    high, middle, low = [dot(turn, part) for part in three_parts(high + (middle + low))]
    return high + (middle + low)


class Links:
    def __init__(self, send_sems, recv_sems):
        self.row, self.col = lax.axis_index("row"), lax.axis_index("col")
        rows, cols = lax.axis_size("row"), lax.axis_size("col")
        self.has = {
            "up": self.row > 0,
            "down": self.row < rows - 1,
            "left": self.col > 0,
            "right": self.col < cols - 1,
        }
        self.at = {
            "up": (self.row - 1, self.col),
            "down": (self.row + 1, self.col),
            "left": (self.row, self.col - 1),
            "right": (self.row, self.col + 1),
        }
        middle, last = cols // 2, cols - 1
        self.crosses = {"right": self.col == middle - 1, "left": self.col == middle}
        self.relays = {"right": self.col == last, "left": self.col == 0}
        self.relay = {"right": (self.row, last), "left": (self.row, 0)}
        self.beyond = {"right": (self.row, middle), "left": (self.row, middle - 1)}
        self.send_sems, self.recv_sems = send_sems, recv_sems
        self.used = 0
        self.sent = []

    def greet(self, peers=()):
        barrier = pltpu.get_barrier_semaphore()
        for side in SIDES:

            @pl.when(self.has[side])
            def _():
                pl.semaphore_signal(barrier, inc=1, device_id=self.at[side], device_id_type=MESH)

        inner = jnp.logical_or(self.crosses["left"], self.crosses["right"])
        outer = jnp.logical_or(self.relays["left"], self.relays["right"])
        for condition, devices in ((inner, self.relay), (outer, self.beyond)):

            @pl.when(condition)
            def _():
                for side in ("left", "right"):
                    pl.semaphore_signal(barrier, inc=1, device_id=devices[side], device_id_type=MESH)

        for peer in peers:
            pl.semaphore_signal(barrier, inc=1, device_id=peer, device_id_type=MESH)
        extra = 2 * jnp.logical_or(inner, outer).astype(jnp.int32)
        pl.semaphore_wait(barrier, len(peers) + extra + sum(self.has[side].astype(jnp.int32) for side in SIDES))

    def copy(self, source, target, device, landing=None):
        index = self.used
        self.used += 1
        return pltpu.make_async_remote_copy(
            src_ref=source,
            dst_ref=target,
            send_sem=self.send_sems.at[index],
            recv_sem=self.recv_sems.at[index if landing is None else landing],
            device_id=device,
            device_id_type=MESH,
        )

    def send(self, source, target, side, also=None):
        item = self.copy(source, target, self.at[side])
        condition = self.has[side] if also is None else jnp.logical_and(self.has[side], also)

        @pl.when(condition)
        def _():
            item.start()

        self.sent.append((item, condition))
        source_side = self.has[OPPOSITE[side]]
        arrives = source_side if also is None else jnp.logical_and(source_side, also)

        def arrived():
            @pl.when(arrives)
            def _():
                item.wait_recv()

        return arrived

    def send_columns(self, source, target, side, slot, also=None):
        rows = source.shape[-2]
        lead = (slice(None),) * (len(source.shape) - 2)
        first, second = (*lead, pl.ds(0, rows // 2)), (*lead, pl.ds(rows // 2, rows // 2))
        item_index = self.used
        head = self.copy(source.at[first], target.at[first], self.at[side])
        tail = self.copy(source.at[second], target.at[second], self.at[side])
        detour = self.copy(source.at[second], slot, self.relay[side])
        onward = self.copy(slot, target.at[second], self.beyond[side], landing=item_index + 1)
        both = lambda a: a if also is None else jnp.logical_and(a, also)
        crosses = self.crosses[side]
        going = [
            (detour, both(crosses)),
            (head, both(self.has[side])),
            (tail, both(jnp.logical_and(self.has[side], jnp.logical_not(crosses)))),
        ]
        for item, condition in going:

            @pl.when(condition)
            def _():
                item.start()

        relays = both(self.relays[side])
        self.sent += going + [(onward, relays)]
        arrives = both(self.has[OPPOSITE[side]])

        def arrived():
            @pl.when(relays)
            def _():
                detour.wait_recv()
                onward.start()

            @pl.when(arrives)
            def _():
                head.wait_recv()
                tail.wait_recv()

        return arrived

    def finish(self):
        for item, condition in self.sent:

            @pl.when(condition)
            def _():
                item.wait_send()


def by_rows(start, stop, step, body):
    def one(index, carry):
        body(pl.ds(pl.multiple_of(start + index * step, 8), step))
        return carry

    lax.fori_loop(0, (stop - start) // step, one, 0)


def first_kernel(
    tile_ref, amp_ref, order_ref, turn_ref, ext_ref, ordered_ref,
    planes, order, turn, tile_slots, corner_slots, local_sems, send_sems, recv_sems,
):
    links = Links(send_sems, recv_sems)
    upper, lower, own = pl.ds(0, HALF), pl.ds(3 * HALF, HALF), pl.ds(HALF, SIDE)
    local = [
        pltpu.make_async_copy(amp_ref, planes, local_sems.at[0]),
        pltpu.make_async_copy(order_ref, order, local_sems.at[1]),
        pltpu.make_async_copy(turn_ref, turn, local_sems.at[2]),
    ]
    inner = [
        pltpu.make_async_copy(
            tile_ref.at[:, :, :, pl.ds(block * HALF, HALF)], ext_ref.at[:, :, 1 + block, own], local_sems.at[3 + block]
        )
        for block in range(2)
    ]
    for item in local + inner:
        item.start()
    links.greet()
    waits, col_waits, corner_waits = [], [], []
    for layer in range(2):
        arrivals = []
        for block in range(2):
            lane = pl.ds(block * HALF, HALF)
            arrivals.append(
                links.send(tile_ref.at[:, layer, pl.ds(0, HALF), lane], ext_ref.at[:, layer, 1 + block, lower], "up")
            )
            arrivals.append(
                links.send(tile_ref.at[:, layer, pl.ds(HALF, HALF), lane], ext_ref.at[:, layer, 1 + block, upper], "down")
            )
        waits.append(arrivals)
        for side, start, block in (("left", 0, 3), ("right", HALF, 0)):
            col_waits.append(
                links.send_columns(
                    tile_ref.at[:, layer, :, pl.ds(start, HALF)],
                    ext_ref.at[:, layer, block, own],
                    side,
                    tile_slots.at[layer],
                )
            )

    def clear(side, blocks, rows):
        @pl.when(jnp.logical_not(links.has[side]))
        def _():
            for part, layer in PLANES:
                for block in blocks:
                    ext_ref[part, layer, block, rows, :] = jnp.zeros((rows.size, HALF), jnp.float32)

    clear("up", (1, 2), upper)
    clear("down", (1, 2), lower)
    clear("left", (0,), own)
    clear("right", (3,), own)
    for rows, side in ((upper, "up"), (lower, "down")):
        for block, other in ((0, "left"), (3, "right")):

            @pl.when(jnp.logical_not(jnp.logical_and(links.has[side], links.has[other])))
            def _():
                for part, layer in PLANES:
                    ext_ref[part, layer, block, rows, :] = jnp.zeros((HALF, HALF), jnp.float32)

    for item in local:
        item.wait()

    def one_plane(index, carry):
        ordered_ref[index] = reorder_plane(planes[index], order[...], turn[...])
        return carry

    lax.fori_loop(0, planes.shape[0], one_plane, 0)
    for arrived in col_waits:
        arrived()
    for layer in range(2):
        for arrived in waits[layer]:
            arrived()
        for number, (rows, side) in enumerate(((upper, "up"), (lower, "down"))):
            for block, to, target in ((1, "left", 3), (2, "right", 0)):
                corner_waits.append(
                    links.send_columns(
                        ext_ref.at[:, layer, block, rows],
                        ext_ref.at[:, layer, target, rows],
                        to,
                        corner_slots.at[layer, number],
                        also=links.has[side],
                    )
                )
    for arrived in corner_waits:
        arrived()
    for item in inner:
        item.wait()
    links.finish()


PLANES = [(part, layer) for layer in range(2) for part in range(2)]


def collect_columns(links, grad_ref, from_left, from_right, total, slots, order):
    for side, buffer in (("left", from_left), ("right", from_right)):

        @pl.when(jnp.logical_not(links.has[side]))
        def _():
            for part, layer in order:
                buffer[part, layer] = jnp.zeros((2 * SIDE, HALF), jnp.float32)

    arrivals = []
    for part, layer in order:
        arrivals.append(
            (
                links.send_columns(grad_ref.at[part, layer, 0], from_right.at[part, layer], "left", slots.at[part, layer]),
                links.send_columns(grad_ref.at[part, layer, 3], from_left.at[part, layer], "right", slots.at[part, layer]),
            )
        )

    def finish(index):
        part, layer = order[index]
        for arrived in arrivals[index]:
            arrived()

        def add(rows):
            total[part, layer, 0, rows, :] = grad_ref[part, layer, 1, rows, :] + from_left[part, layer, rows, :]
            total[part, layer, 1, rows, :] = grad_ref[part, layer, 2, rows, :] + from_right[part, layer, rows, :]

        by_rows(0, 2 * SIDE, 64, add)

    return finish


def middle_kernel(
    ext_ref, grad_ref, out_ref, from_left, from_right, slots, from_up, from_down, total, halo_slots, send_sems, recv_sems
):
    links = Links(send_sems, recv_sems)
    links.greet()
    finish_columns = collect_columns(links, grad_ref, from_left, from_right, total, slots, PLANES)
    for side, buffer in (("up", from_up), ("down", from_down)):

        @pl.when(jnp.logical_not(links.has[side]))
        def _():
            for part, layer in PLANES:
                buffer[part, layer] = jnp.zeros((2, SIDE, HALF), jnp.float32)

    for side, block in (("left", 0), ("right", 3)):

        @pl.when(jnp.logical_not(links.has[side]))
        def _():
            for part, layer in PLANES:
                out_ref[part, layer, block] = jnp.zeros((2 * SIDE, HALF), jnp.float32)

    arrivals = []
    for index, (part, layer) in enumerate(PLANES):
        finish_columns(index)
        arrivals.append(
            (
                links.send(total.at[part, layer, :, pl.ds(0, SIDE)], from_down.at[part, layer], "up"),
                links.send(total.at[part, layer, :, pl.ds(SIDE, SIDE)], from_up.at[part, layer], "down"),
            )
        )
    step_up = jnp.where(links.has["up"], OBJECT_STEP, 0.0).astype(jnp.float32)
    step_down = jnp.where(links.has["down"], OBJECT_STEP, 0.0).astype(jnp.float32)
    halos = []
    for index, (part, layer) in enumerate(PLANES):
        for arrived in arrivals[index]:
            arrived()
        for block in range(2):
            for start, buffer, offset, step in (
                (0, from_up, 0, step_up),
                (HALF, from_up, 0, OBJECT_STEP),
                (SIDE, from_down, SIDE, OBJECT_STEP),
                (3 * HALF, from_down, SIDE, step_down),
            ):
                for row in range(start, start + HALF, 64):
                    rows, near = pl.ds(row, 64), pl.ds(row - offset, 64)
                    gradient = total[part, layer, block, rows, :] + buffer[part, layer, block, near, :]
                    out_ref[part, layer, 1 + block, rows, :] = ext_ref[part, layer, 1 + block, rows, :] - step * gradient
        slot = halo_slots.at[part, layer]
        halos.append(links.send_columns(out_ref.at[part, layer, 1], out_ref.at[part, layer, 3], "left", slot))
        halos.append(links.send_columns(out_ref.at[part, layer, 2], out_ref.at[part, layer, 0], "right", slot))
    for arrived in halos:
        arrived()
    links.finish()


def last_kernel(
    ext_ref, grad_ref, first_probe_ref, second_probe_ref, probe_ref, object_ref, new_probe_ref,
    from_left, from_right, slots, from_up, from_down, total, partial, pair, landings, sums, gathered, send_sems, recv_sems,
):
    links = Links(send_sems, recv_sems)
    row, col = links.row, links.col
    core, x, y_low = lax.rem(col, 2), lax.rem(col // 2, 4), col // 8
    y_high, z = lax.rem(row, 2), row // 2
    y = y_high * 2 + y_low
    partner = (row, col + 1 - 2 * core)
    plane = lambda k: ((k // 4) * 2 + y_high, y_low * 8 + lax.rem(k, 4) * 2 + core)
    line = lambda k: (z * 2 + k // 2, lax.rem(k, 2) * 8 + x * 2 + core)
    groups = [(z * 4 + x, plane, 16), (y, line, 4)]
    peers = [partner]
    for place, device, members in groups:
        peers += [device(lax.rem(place + k, members)) for k in range(1, members)]
    links.greet(peers)
    count = 4 * SIDE
    half = count // 2

    def rows_at(start, size):
        return pl.ds(pl.multiple_of(start, 8), size)

    def start(source, target, device):
        item = links.copy(source, target, device)
        item.start()
        return item

    def add_probe(rows):
        partial[rows, :] = first_probe_ref[rows, :] + second_probe_ref[rows, :]

    by_rows(0, count, 64, add_probe)
    swap = start(partial.at[rows_at((1 - core) * half, half)], pair, partner)
    finish_columns = collect_columns(links, grad_ref, from_left, from_right, total, slots, PLANES)
    for side, buffer in (("up", from_up), ("down", from_down)):

        @pl.when(jnp.logical_not(links.has[side]))
        def _():
            for part, layer in PLANES:
                buffer[part, layer] = jnp.zeros((2, HALF, HALF), jnp.float32)

    swap.wait_recv()
    base = core * half

    def add_pair(index, carry):
        near = pl.ds(pl.multiple_of(index * 64, 64), 64)
        mine = rows_at(base + index * 64, 64)
        sums[mine, :] = partial[mine, :] + pair[near, :]
        return carry

    lax.fori_loop(0, half // 64, add_pair, 0)
    gathers = [swap]
    places = []
    arrivals = []

    def scatter(number, base, size):
        place, device, members = groups[number]
        items = []
        for k in range(1, members):
            other = lax.rem(place + k, members)
            source = sums.at[rows_at(base + other * size, size)]
            items.append(start(source, landings[number].at[k - 1], device(other)))
        gathers.extend(items)
        places.append((place, device, members, base, size))
        return items

    def reduce(number, items, base, size):
        for item in items:
            item.wait_recv()
        mine = rows_at(base, size)
        value = sums[mine, :]
        for k in range(len(items)):
            value = value + landings[number][k]
        (gathered if number == len(groups) - 1 else sums)[mine, :] = value

    def rows_out(index):
        part, layer = PLANES[index]
        finish_columns(index)
        arrivals.append(
            (
                links.send(total.at[part, layer, :, pl.ds(0, HALF)], from_down.at[part, layer], "up"),
                links.send(total.at[part, layer, :, pl.ds(3 * HALF, HALF)], from_up.at[part, layer], "down"),
            )
        )

    size = half // 16
    items = scatter(0, base, size)
    rows_out(0)
    rows_out(1)
    base = base + groups[0][0] * size
    reduce(0, items, base, size)
    size = size // 4
    items = scatter(1, base, size)
    rows_out(2)
    rows_out(3)
    base = base + groups[1][0] * size
    reduce(1, items, base, size)
    for place, device, members, group_base, size in reversed(places):
        mine = rows_at(group_base + place * size, size)
        items = [
            start(gathered.at[mine], gathered.at[mine], device(lax.rem(place + k, members))) for k in range(1, members)
        ]
        gathers += items
        for item in items:
            item.wait_recv()
    mine = rows_at(core * half, half)
    swap_back = start(gathered.at[mine], gathered.at[mine], partner)
    for index, (part, layer) in enumerate(PLANES):
        for arrived in arrivals[index]:
            arrived()
        for block in range(2):
            lane = pl.ds(block * HALF, HALF)
            for begin, buffer in ((HALF, from_up), (SIDE, from_down)):
                for offset in range(0, HALF, 64):
                    rows, near = pl.ds(begin + offset, 64), pl.ds(offset, 64)
                    gradient = total[part, layer, block, rows, :] + buffer[part, layer, block, near, :]
                    target = pl.ds(begin - HALF + offset, 64)
                    object_ref[part, layer, target, lane] = (
                        ext_ref[part, layer, 1 + block, rows, :] - OBJECT_STEP * gradient
                    )
    swap_back.wait_recv()

    def finish_probe(rows):
        new_probe_ref[rows, :] = probe_ref[rows, :] - PROBE_STEP * gathered[rows, :]

    by_rows(0, count, 64, finish_probe)
    for item in gathers + [swap_back]:
        item.wait_send()
    links.finish()


def vmem_specs(count):
    return [pl.BlockSpec(memory_space=pltpu.VMEM)] * count


def comm_params(identity, limit):
    return pltpu.CompilerParams(collective_id=identity, has_side_effects=True, vmem_limit_bytes=limit << 20)


def semaphores(count):
    return [pltpu.SemaphoreType.DMA((count,)), pltpu.SemaphoreType.DMA((count,))]


def f32(*shape):
    return pltpu.VMEM(shape, jnp.float32)


EXTENDED = jax.ShapeDtypeStruct((2, 2, 4, 2 * SIDE, HALF), jnp.float32)


def first_exchange(tile, amplitudes):
    planes = amplitudes.shape[0]
    return pl.pallas_call(
        first_kernel,
        out_shape=(EXTENDED, jax.ShapeDtypeStruct((planes, SIDE, SIDE), jnp.float32)),
        in_specs=[pl.BlockSpec(memory_space=pltpu.HBM)] * 4,
        out_specs=tuple(vmem_specs(2)),
        scratch_shapes=[
            f32(planes, SIDE, SIDE),
            pltpu.VMEM((SIDE, SIDE), jnp.bfloat16),
            pltpu.VMEM((SIDE, SIDE), jnp.bfloat16),
            f32(2, 2, HALF, HALF),
            f32(2, 2, 2, HALF // 2, HALF),
            pltpu.SemaphoreType.DMA((5,)),
            *semaphores(8 + 16 + 32),
        ],
        compiler_params=comm_params(0, 14),
    )(tile, amplitudes, jnp.asarray(ORDER), jnp.asarray(ORDER.T))


def columns_buffers():
    return [f32(2, 2, 2 * SIDE, HALF), f32(2, 2, 2 * SIDE, HALF), f32(2, 2, SIDE, HALF)]


def middle_exchange(extended, gradient):
    return pl.pallas_call(
        middle_kernel,
        out_shape=EXTENDED,
        in_specs=vmem_specs(2),
        out_specs=vmem_specs(1)[0],
        scratch_shapes=[
            *columns_buffers(),
            f32(2, 2, 2, SIDE, HALF),
            f32(2, 2, 2, SIDE, HALF),
            f32(2, 2, 2, 2 * SIDE, HALF),
            f32(2, 2, SIDE, HALF),
            *semaphores(32 + 8 + 32),
        ],
        compiler_params=comm_params(1, 24),
    )(extended, gradient)


def last_exchange(extended, gradient, first_probe, second_probe, probe_modes):
    flat = (4 * SIDE, SIDE)
    new_object, new_probe = pl.pallas_call(
        last_kernel,
        out_shape=(
            jax.ShapeDtypeStruct((2, 2, SIDE, SIDE), jnp.float32),
            jax.ShapeDtypeStruct(flat, jnp.float32),
        ),
        in_specs=vmem_specs(5),
        out_specs=tuple(vmem_specs(2)),
        scratch_shapes=[
            *columns_buffers(),
            f32(2, 2, 2, HALF, HALF),
            f32(2, 2, 2, HALF, HALF),
            f32(2, 2, 2, 2 * SIDE, HALF),
            f32(*flat),
            f32(2 * SIDE, SIDE),
            [f32(15, 2 * SIDE // 16, SIDE), f32(3, 2 * SIDE // 64, SIDE)],
            f32(*flat),
            f32(*flat),
            *semaphores(32 + 8 + 2 + 2 * 18),
        ],
        compiler_params=comm_params(2, 26),
    )(extended, gradient, first_probe.reshape(flat), second_probe.reshape(flat), probe_modes.reshape(flat))
    return new_object, new_probe.reshape(probe_modes.shape)


def batch_kernel(
    batch, offset_ref, count_ref, ext_ref, probe_ref, amp_ref, table_ref, grad_ref, probe_grad_ref,
    obj, psi, right_a, right_b, yield_a, yield_b, left_a, left_b, out_a, out_b,
):
    lanes = lax.broadcasted_iota(jnp.int32, (CHUNK, HALF), 1)
    lo, hi = pl.ds(0, HALF), pl.ds(HALF, HALF)

    def chunks(total, body):
        def step(index, carry):
            body(pl.multiple_of(index * CHUNK, CHUNK))
            return carry

        lax.fori_loop(0, total // CHUNK, step, 0, unroll=True)

    def bf(value):
        return value.astype(jnp.bfloat16)

    def zero_grad(row):
        for part in range(2):
            for layer in range(2):
                for block in range(4):
                    grad_ref[part, layer, block, pl.ds(row, CHUNK), :] = jnp.zeros((CHUNK, HALF), jnp.float32)

    chunks(2 * SIDE, zero_grad)

    def zero_probe(row):
        for part in range(2):
            for mode in range(MODES):
                probe_grad_ref[part, mode, pl.ds(row, CHUNK), :] = jnp.zeros((CHUNK, SIDE), jnp.float32)

    chunks(SIDE, zero_probe)

    def right(table_a, table_b):
        yield_a[...] = dot(right_a[...], table_ref[table_a])
        yield_b[...] = dot(right_b[...], table_ref[table_b])

    def left(table_a, table_b):
        out_a[...] = dot(table_ref[table_a], left_a[...])
        out_b[...] = dot(table_ref[table_b], left_b[...])

    def put_split(mode, row, re, im):
        at = pl.ds(mode * SIDE + row, CHUNK)
        right_a[at, lo] = bf(re[0] + re[1])
        right_a[at, hi] = bf(im[0] + im[1])
        right_b[at, lo] = bf(re[0] - re[1])
        right_b[at, hi] = bf(im[0] - im[1])

    def columns(ref, mode):
        return pl.ds(mode * SIDE, HALF), pl.ds(mode * SIDE + HALF, HALF)

    def middle_spread(row):
        for mode in range(MODES):
            here = columns(left_a, mode)
            for part, lane in ((0, lo), (1, hi)):
                top = pl.ds(mode * SIDE + row, CHUNK)
                low = pl.ds(mode * SIDE + HALF + row, CHUNK)
                at, ab = yield_a[top, lane], yield_a[low, lane]
                bt, bb = yield_b[top, lane], yield_b[low, lane]
                to = pl.ds(part * HALF + row, CHUNK)
                a_sum, a_dif = at + ab, at - ab
                b_sum, b_dif = bt + bb, bt - bb
                left_a[to, here[0]] = bf(a_sum + b_sum)
                left_a[to, here[1]] = bf(a_sum - b_sum)
                left_b[to, here[0]] = bf(a_dif + b_dif)
                left_b[to, here[1]] = bf(a_dif - b_dif)

    def middle_forward(row):
        for mode in range(MODES):
            here = columns(left_a, mode)
            for part, lane in ((0, lo), (1, hi)):
                top = pl.ds(mode * SIDE + row, CHUNK)
                low = pl.ds(mode * SIDE + HALF + row, CHUNK)
                to = pl.ds(part * HALF + row, CHUNK)
                for source, at in ((yield_a, here[0]), (yield_b, here[1])):
                    upper, lower = source[top, lane], source[low, lane]
                    left_a[to, at] = bf(upper + lower)
                    left_b[to, at] = bf(upper - lower)

    def middle_backward(row):
        for mode in range(MODES):
            here = columns(left_a, mode)
            for part, lane in ((0, lo), (1, hi)):
                to = pl.ds(part * HALF + row, CHUNK)
                for base, target in ((0, left_a), (HALF, left_b)):
                    at = pl.ds(mode * SIDE + base + row, CHUNK)
                    even, odd = yield_a[at, lane], yield_b[at, lane]
                    target[to, here[0]] = bf(even + odd)
                    target[to, here[1]] = bf(even - odd)

    def joined(mode, row):
        result = []
        for sign in (1, -1):
            pair = []
            for part in range(2):
                at = pl.ds(part * HALF + row, CHUNK)
                halves = []
                for lane in columns(out_a, mode):
                    a, b = out_a[at, lane], out_b[at, lane]
                    halves.append(a + b if sign > 0 else a - b)
                pair.append(halves)
            result.append(pair)
        return result

    def pair_of(ref, first, second, row):
        return [ref[first, second, pl.ds(row, CHUNK), lane] for lane in (lo, hi)]

    def one_slot(slot, carry):
        start_row = offset_ref[batch, 0, slot, 0]
        start_col = offset_ref[batch, 1, slot, 0]
        base = start_col // HALF
        shift = start_col % HALF
        take_left = lanes < HALF - shift
        put_right = lanes >= shift
        back = lax.rem(HALF - shift, HALF)

        def fetch(row):
            for part in range(2):
                for layer in range(2):
                    at = pl.ds(start_row + row, CHUNK)
                    turned = [pltpu.roll(ext_ref[part, layer, base + k, at, :], back, 1) for k in range(3)]
                    obj[part, layer, pl.ds(row, CHUNK), lo] = jnp.where(take_left, turned[0], turned[1])
                    obj[part, layer, pl.ds(row, CHUNK), hi] = jnp.where(take_left, turned[1], turned[2])

        chunks(SIDE, fetch)

        def enter(row):
            o_re, o_im = pair_of(obj, 0, 0, row), pair_of(obj, 1, 0, row)
            for mode in range(MODES):
                p_re, p_im = pair_of(probe_ref, 0, mode, row), pair_of(probe_ref, 1, mode, row)
                re = [p_re[k] * o_re[k] - p_im[k] * o_im[k] for k in range(2)]
                im = [p_re[k] * o_im[k] + p_im[k] * o_re[k] for k in range(2)]
                put_split(mode, row, re, im)

        chunks(SIDE, enter)
        right(SUM_R, DIF_R)
        chunks(HALF, middle_spread)
        left(SUM_L, DIF_L)

        def second_slice(row):
            for side in range(2):
                at = row + side * HALF
                o_re, o_im = pair_of(obj, 0, 1, at), pair_of(obj, 1, 1, at)
                for mode in range(MODES):
                    w_re, w_im = joined(mode, row)[side]
                    for k, lane in ((0, lo), (1, hi)):
                        psi[0, mode, pl.ds(at, CHUNK), lane] = w_re[k]
                        psi[1, mode, pl.ds(at, CHUNK), lane] = w_im[k]
                    re = [w_re[k] * o_re[k] - w_im[k] * o_im[k] for k in range(2)]
                    im = [w_re[k] * o_im[k] + w_im[k] * o_re[k] for k in range(2)]
                    put_split(mode, at, re, im)

        chunks(HALF, second_slice)
        right(EVEN_R, ODD_R)
        chunks(HALF, middle_forward)
        left(EVEN_L, ODD_L)

        def compare(row):
            for base_row, source in ((0, out_a), (HALF, out_b)):
                waves = []
                for mode in range(MODES):
                    here = columns(source, mode)
                    re = [source[pl.ds(row, CHUNK), lane] for lane in here]
                    im = [source[pl.ds(HALF + row, CHUNK), lane] for lane in here]
                    waves.append((re, im))
                for k, lane in ((0, lo), (1, hi)):
                    intensity = waves[0][0][k] * waves[0][0][k] + waves[0][1][k] * waves[0][1][k]
                    for re, im in waves[1:]:
                        intensity = intensity + (re[k] * re[k] + im[k] * im[k])
                    amplitude = amp_ref[batch * (amp_ref.shape[0] // 2) + slot, pl.ds(base_row + row, CHUNK), lane]
                    ratio = 1.0 - amplitude * lax.rsqrt(jnp.maximum(intensity, AMPLITUDE_FLOOR**2))
                    target = right_a if k == 0 else right_b
                    for mode, (re, im) in enumerate(waves):
                        at = pl.ds(mode * SIDE + base_row + row, CHUNK)
                        target[at, lo] = bf(re[k] * ratio)
                        target[at, hi] = bf(im[k] * ratio)

        chunks(HALF, compare)
        right(EVEN_L, ODD_L)
        chunks(HALF, middle_backward)
        left(EVEN_R, ODD_R)

        def add_term(part, layer, row, term):
            turned = [pltpu.roll(value, shift, 1) for value in term]
            zero = jnp.zeros_like(turned[0])
            spread = [
                jnp.where(put_right, turned[0], zero),
                jnp.where(put_right, turned[1], turned[0]),
                jnp.where(put_right, zero, turned[1]),
            ]
            at = pl.ds(start_row + row, CHUNK)
            for k in range(3):
                grad_ref[part, layer, base + k, at, :] = grad_ref[part, layer, base + k, at, :] + spread[k]

        def object_term(layer, row, waves, backs):
            re, im = [], []
            for k in range(2):
                re.append(sum(w[0][k] * b[0][k] + w[1][k] * b[1][k] for w, b in zip(waves, backs)))
                im.append(sum(w[0][k] * b[1][k] - w[1][k] * b[0][k] for w, b in zip(waves, backs)))
            add_term(0, layer, row, re)
            add_term(1, layer, row, im)

        def last_back(row):
            for side in range(2):
                at = row + side * HALF
                backs = [joined(mode, row)[side] for mode in range(MODES)]
                waves = [(pair_of(psi, 0, mode, at), pair_of(psi, 1, mode, at)) for mode in range(MODES)]
                o_re, o_im = pair_of(obj, 0, 1, at), pair_of(obj, 1, 1, at)
                for mode, (b_re, b_im) in enumerate(backs):
                    re = [o_re[k] * b_re[k] + o_im[k] * b_im[k] for k in range(2)]
                    im = [o_re[k] * b_im[k] - o_im[k] * b_re[k] for k in range(2)]
                    put_split(mode, at, re, im)
                object_term(1, at, waves, backs)

        chunks(HALF, last_back)
        right(SUM_L, DIF_L)
        chunks(HALF, middle_spread)
        left(SUM_R, DIF_R)

        def first_back(row):
            for side in range(2):
                at = row + side * HALF
                backs = [joined(mode, row)[side] for mode in range(MODES)]
                waves = [(pair_of(probe_ref, 0, mode, at), pair_of(probe_ref, 1, mode, at)) for mode in range(MODES)]
                o_re, o_im = pair_of(obj, 0, 0, at), pair_of(obj, 1, 0, at)
                for mode, (b_re, b_im) in enumerate(backs):
                    for k, lane in ((0, lo), (1, hi)):
                        spot = (mode, pl.ds(at, CHUNK), lane)
                        probe_grad_ref[(0, *spot)] = probe_grad_ref[(0, *spot)] + (o_re[k] * b_re[k] + o_im[k] * b_im[k])
                        probe_grad_ref[(1, *spot)] = probe_grad_ref[(1, *spot)] + (o_re[k] * b_im[k] - o_im[k] * b_re[k])
                object_term(0, at, waves, backs)

        chunks(HALF, first_back)
        return carry

    lax.fori_loop(0, count_ref[batch, 0, 0], one_slot, 0)


def batch_terms(batch, extended, probe_modes, amplitudes, offsets, counts, table):
    vmem = pl.BlockSpec(memory_space=pltpu.VMEM)
    smem = pl.BlockSpec(memory_space=pltpu.SMEM)
    field = pltpu.VMEM((2, 2, SIDE, SIDE), jnp.float32)
    return pl.pallas_call(
        functools.partial(batch_kernel, batch),
        out_shape=(
            jax.ShapeDtypeStruct((2, 2, 4, 2 * SIDE, HALF), jnp.float32),
            jax.ShapeDtypeStruct((2, MODES, SIDE, SIDE), jnp.float32),
        ),
        in_specs=[smem, smem, vmem, vmem, vmem, vmem],
        out_specs=(vmem, vmem),
        scratch_shapes=[
            field,
            field,
            pltpu.VMEM((MODES * SIDE, SIDE), jnp.bfloat16),
            pltpu.VMEM((MODES * SIDE, SIDE), jnp.bfloat16),
            pltpu.VMEM((MODES * SIDE, SIDE), jnp.float32),
            pltpu.VMEM((MODES * SIDE, SIDE), jnp.float32),
            pltpu.VMEM((SIDE, MODES * SIDE), jnp.bfloat16),
            pltpu.VMEM((SIDE, MODES * SIDE), jnp.bfloat16),
            pltpu.VMEM((SIDE, MODES * SIDE), jnp.float32),
            pltpu.VMEM((SIDE, MODES * SIDE), jnp.float32),
        ],
        compiler_params=pltpu.CompilerParams(vmem_limit_bytes=26 << 20),
        cost_estimate=pl.CostEstimate(flops=3 * 64 * SIDE**3, bytes_accessed=12 << 20, transcendentals=0),
    )(offsets, counts, extended, probe_modes, amplitudes, table)


def body(object_field, probe_modes, amplitudes, offsets, counts):
    batches, slots = amplitudes.shape[:2]
    table = jnp.asarray(TABLES)
    extended, ordered = first_exchange(object_field, amplitudes.reshape(batches * slots, SIDE, SIDE))
    terms = lambda cells, batch: batch_terms(batch, cells, probe_modes, ordered, offsets, counts, table)
    gradient, first_probe = terms(extended, 0)
    extended = middle_exchange(extended, gradient)
    gradient, second_probe = terms(extended, 1)
    return last_exchange(extended, gradient, first_probe, second_probe, probe_modes)


def solution(mesh):
    return jax.shard_map(
        body,
        mesh=mesh,
        in_specs=(
            P(None, None, "row", "col"),
            P(),
            P(None, "row", "col", None, None),
            P(None, None, "row", "col"),
            P(None, "row", "col"),
        ),
        out_specs=(P(None, None, "row", "col"), P()),
        check_vma=False,
    )
```

```python
import functools
import math

import jax
import jax.numpy as jnp
import numpy as np
from jax import lax
from jax.experimental import pallas as pl
from jax.experimental.pallas import tpu as pltpu
from jax.sharding import PartitionSpec as P

AMPLITUDE_FLOOR = 0.5
OBJECT_STEP = 0.25
PROBE_STEP = 0.125
SIDE = 256
HALF = SIDE // 2
MODES = 2
CHUNK = 16
MESH = pl.DeviceIdType.MESH
SIDES = ("up", "down", "left", "right")
OPPOSITE = {"up": "down", "down": "up", "left": "right", "right": "left"}


def real_form(table):
    re, im = table.real, table.imag
    return np.block([[re, im], [-im, re]]).astype(jnp.bfloat16)


def make_tables():
    index = np.arange(SIDE)
    angles = (index[:, None] * index[None, :] % SIDE).astype(np.float32) * np.float32(2.0 * math.pi / SIDE)
    scale = np.float32(1.0 / math.sqrt(SIDE))
    rounded = lambda v: (v * scale).astype(jnp.bfloat16).astype(np.float64)
    forward = rounded(np.cos(angles)) - 1j * rounded(np.sin(angles))
    frequency = np.where(index < HALF, index, index - SIDE).astype(np.float64)
    chirp = np.exp(-2j * math.pi * (frequency * frequency % (16 * SIDE)) / (16 * SIDE))
    spread = (forward.conj() * chirp[None, :]) @ forward
    same = 0.25 * (spread[:HALF, :HALF] + spread[HALF:, HALF:] + spread[:HALF, HALF:] + spread[HALF:, :HALF])
    other = 0.25 * (spread[:HALF, :HALF] + spread[HALF:, HALF:] - spread[:HALF, HALF:] - spread[HALF:, :HALF])
    same = 0.5 * (same + same.T)
    other = 0.5 * (other + other.T)
    even = forward[:HALF, 0::2]
    odd = forward[:HALF, 1::2]
    rows = []
    for table in (same, other, even, odd):
        matrix = real_form(table)
        rows += [matrix, np.ascontiguousarray(matrix.T)]
    order = np.zeros((SIDE, SIDE), np.float32)
    order[0::2, :HALF] = np.eye(HALF)
    order[1::2, HALF:] = np.eye(HALF)
    return np.stack(rows), order.astype(jnp.bfloat16)


TABLES, ORDER = make_tables()
(SUM_R, SUM_L, DIF_R, DIF_L, EVEN_R, EVEN_L, ODD_R, ODD_L) = range(8)


def dot(left, right):
    return jnp.dot(left, right, preferred_element_type=jnp.float32)


def three_parts(value):
    high = value.astype(jnp.bfloat16)
    rest = value - high.astype(jnp.float32)
    middle = rest.astype(jnp.bfloat16)
    return high, middle, (rest - middle.astype(jnp.float32)).astype(jnp.bfloat16)


def reorder_plane(plane, order, turn):
    high, middle, low = [dot(part, order) for part in three_parts(plane)]
    high, middle, low = [dot(turn, part) for part in three_parts(high + (middle + low))]
    return high + (middle + low)


class Links:
    def __init__(self, send_sems, recv_sems):
        self.row, self.col = lax.axis_index("row"), lax.axis_index("col")
        rows, cols = lax.axis_size("row"), lax.axis_size("col")
        self.has = {
            "up": self.row > 0,
            "down": self.row < rows - 1,
            "left": self.col > 0,
            "right": self.col < cols - 1,
        }
        self.at = {
            "up": (self.row - 1, self.col),
            "down": (self.row + 1, self.col),
            "left": (self.row, self.col - 1),
            "right": (self.row, self.col + 1),
        }
        middle, last = cols // 2, cols - 1
        relays = {"right": (last, last - 2, last - 4), "left": (0, 2, 4)}
        self.crosses = {"right": self.col == middle - 1, "left": self.col == middle}
        self.beyond = {"right": (self.row, middle), "left": (self.row, middle - 1)}
        self.relay = {side: [(self.row, col) for col in relays[side]] for side in relays}
        self.relays = {side: [self.col == col for col in relays[side]] for side in relays}
        self.send_sems, self.recv_sems = send_sems, recv_sems
        self.used = 0
        self.sent = []

    def greet(self, peers=()):
        barrier = pltpu.get_barrier_semaphore()
        for side in SIDES:

            @pl.when(self.has[side])
            def _():
                pl.semaphore_signal(barrier, inc=1, device_id=self.at[side], device_id_type=MESH)

        inner = jnp.logical_or(self.crosses["left"], self.crosses["right"])
        outer = functools.reduce(jnp.logical_or, self.relays["left"] + self.relays["right"])
        extra = 6 * inner.astype(jnp.int32) + 2 * outer.astype(jnp.int32)
        for condition, devices in (
            (inner, self.relay["left"] + self.relay["right"]),
            (outer, list(self.beyond.values())),
        ):

            @pl.when(condition)
            def _():
                for device in devices:
                    pl.semaphore_signal(barrier, inc=1, device_id=device, device_id_type=MESH)

        for peer in peers:
            pl.semaphore_signal(barrier, inc=1, device_id=peer, device_id_type=MESH)
        pl.semaphore_wait(barrier, len(peers) + extra + sum(self.has[side].astype(jnp.int32) for side in SIDES))

    def copy(self, source, target, device):
        index = self.used
        self.used += 1
        return pltpu.make_async_remote_copy(
            src_ref=source,
            dst_ref=target,
            send_sem=self.send_sems.at[index],
            recv_sem=self.recv_sems.at[index],
            device_id=device,
            device_id_type=MESH,
        )

    def send(self, source, target, side, also=None):
        item = self.copy(source, target, self.at[side])
        condition = self.has[side] if also is None else jnp.logical_and(self.has[side], also)

        @pl.when(condition)
        def _():
            item.start()

        self.sent.append((item, condition))
        source_side = self.has[OPPOSITE[side]]
        arrives = source_side if also is None else jnp.logical_and(source_side, also)

        def arrived():
            @pl.when(arrives)
            def _():
                item.wait_recv()

        return arrived

    def send_columns(self, source, target, side, slots, also=None):
        rows = source.shape[-2]
        lead = (slice(None),) * (len(source.shape) - 2)
        halves = [(*lead, pl.ds(k * rows // 2, rows // 2)) for k in range(2)]
        quarters = [(*lead, pl.ds(k * rows // 4, rows // 4)) for k in range(4)]
        both = lambda a: a if also is None else jnp.logical_and(a, also)
        crosses = self.crosses[side]
        direct = both(jnp.logical_and(self.has[side], jnp.logical_not(crosses)))
        whole = [(self.copy(source.at[at], target.at[at], self.at[side]), direct) for at in halves]
        first = self.copy(source.at[quarters[0]], target.at[quarters[0]], self.at[side])
        detours, onwards = [], []
        for k in range(3):
            at = quarters[k + 1]
            detours.append(self.copy(source.at[at], slots.at[k], self.relay[side][k]))
            onwards.append(self.copy(slots.at[k], target.at[at], self.beyond[side]))
        going = [(item, both(crosses)) for item in [*detours, first]] + whole
        for item, condition in going:

            @pl.when(condition)
            def _():
                item.start()

        relays = [both(here) for here in self.relays[side]]
        self.sent += going + list(zip(onwards, relays))
        receives_parts = self.crosses[OPPOSITE[side]]
        receives_whole = both(jnp.logical_and(self.has[OPPOSITE[side]], jnp.logical_not(receives_parts)))
        receives_parts = both(receives_parts)

        def forward():
            for detour, onward, here in zip(detours, onwards, relays):

                @pl.when(here)
                def _():
                    detour.wait_recv()
                    onward.start()

        def arrived(half):
            @pl.when(receives_whole)
            def _():
                whole[half][0].wait_recv()

            @pl.when(receives_parts)
            def _():
                for item in (first, onwards[0]) if half == 0 else onwards[1:]:
                    item.wait_recv()

        return forward, arrived

    def finish(self):
        for item, condition in self.sent:

            @pl.when(condition)
            def _():
                item.wait_send()


def by_rows(start, stop, step, body):
    def one(index, carry):
        body(pl.ds(pl.multiple_of(start + index * step, 8), step))
        return carry

    lax.fori_loop(0, (stop - start) // step, one, 0)


def first_kernel(
    tile_ref, amp_ref, order_ref, turn_ref, table_ref, probe_ref, ext_ref, ordered_ref, table_out, probe_out,
    planes, order, turn, tile_slots, corner_slots, local_sems, send_sems, recv_sems,
):
    links = Links(send_sems, recv_sems)
    upper, lower, own = pl.ds(0, HALF), pl.ds(3 * HALF, HALF), pl.ds(HALF, SIDE)
    local = [
        pltpu.make_async_copy(amp_ref, planes, local_sems.at[0]),
        pltpu.make_async_copy(order_ref, order, local_sems.at[1]),
        pltpu.make_async_copy(turn_ref, turn, local_sems.at[2]),
    ]
    inner = [
        pltpu.make_async_copy(
            tile_ref.at[:, :, :, pl.ds(block * HALF, HALF)], ext_ref.at[:, :, 1 + block, own], local_sems.at[3 + block]
        )
        for block in range(2)
    ]
    extra = [
        pltpu.make_async_copy(table_ref, table_out, local_sems.at[5]),
        pltpu.make_async_copy(probe_ref, probe_out, local_sems.at[6]),
    ]
    for item in local + inner + extra:
        item.start()
    links.greet()
    waits, col_waits, corner_waits = [], [], []
    for layer in range(2):
        arrivals = []
        for block in range(2):
            lane = pl.ds(block * HALF, HALF)
            arrivals.append(
                links.send(tile_ref.at[:, layer, pl.ds(0, HALF), lane], ext_ref.at[:, layer, 1 + block, lower], "up")
            )
            arrivals.append(
                links.send(tile_ref.at[:, layer, pl.ds(HALF, HALF), lane], ext_ref.at[:, layer, 1 + block, upper], "down")
            )
        waits.append(arrivals)
        for side, start, block in (("left", 0, 3), ("right", HALF, 0)):
            col_waits.append(
                links.send_columns(
                    tile_ref.at[:, layer, :, pl.ds(start, HALF)],
                    ext_ref.at[:, layer, block, own],
                    side,
                    tile_slots.at[layer],
                )
            )

    def clear(side, blocks, rows):
        @pl.when(jnp.logical_not(links.has[side]))
        def _():
            for part, layer in PLANES:
                for block in blocks:
                    ext_ref[part, layer, block, rows, :] = jnp.zeros((rows.size, HALF), jnp.float32)

    clear("up", (1, 2), upper)
    clear("down", (1, 2), lower)
    clear("left", (0,), own)
    clear("right", (3,), own)
    for rows, side in ((upper, "up"), (lower, "down")):
        for block, other in ((0, "left"), (3, "right")):

            @pl.when(jnp.logical_not(jnp.logical_and(links.has[side], links.has[other])))
            def _():
                for part, layer in PLANES:
                    ext_ref[part, layer, block, rows, :] = jnp.zeros((HALF, HALF), jnp.float32)

    for item in local:
        item.wait()

    def one_plane(index, carry):
        ordered_ref[index] = reorder_plane(planes[index], order[...], turn[...])
        return carry

    lax.fori_loop(0, planes.shape[0], one_plane, 0)
    for forward, _ in col_waits:
        forward()
    for layer in range(2):
        for arrived in waits[layer]:
            arrived()
        for number, (rows, side) in enumerate(((upper, "up"), (lower, "down"))):
            for block, to, target in ((1, "left", 3), (2, "right", 0)):
                corner_waits.append(
                    links.send_columns(
                        ext_ref.at[:, layer, block, rows],
                        ext_ref.at[:, layer, target, rows],
                        to,
                        corner_slots.at[layer, number],
                        also=links.has[side],
                    )
                )
    for forward, _ in corner_waits:
        forward()
    for item in inner + extra:
        item.wait()
    for _, arrived in col_waits + corner_waits:
        for half in range(2):
            arrived(half)
    links.finish()


PLANES = [(part, layer) for layer in range(2) for part in range(2)]


def collect_columns(links, grad_ref, from_left, from_right, total, slots, order):
    for side, buffer in (("left", from_left), ("right", from_right)):

        @pl.when(jnp.logical_not(links.has[side]))
        def _():
            for part, layer in order:
                buffer[part, layer] = jnp.zeros((2 * SIDE, HALF), jnp.float32)

    arrivals = []
    for part, layer in order:
        arrivals.append(
            (
                links.send_columns(grad_ref.at[part, layer, 0], from_right.at[part, layer], "left", slots.at[part, layer]),
                links.send_columns(grad_ref.at[part, layer, 3], from_left.at[part, layer], "right", slots.at[part, layer]),
            )
        )

    def finish(index, half):
        part, layer = order[index]
        for forward, arrived in arrivals[index]:
            if half == 0:
                forward()
            arrived(half)

        def add(rows):
            total[part, layer, 0, rows, :] = grad_ref[part, layer, 1, rows, :] + from_left[part, layer, rows, :]
            total[part, layer, 1, rows, :] = grad_ref[part, layer, 2, rows, :] + from_right[part, layer, rows, :]

        by_rows(half * SIDE, (half + 1) * SIDE, 64, add)

    return finish


def middle_kernel(
    ext_ref, grad_ref, out_ref, from_left, from_right, slots, from_up, from_down, total, halo_slots, send_sems, recv_sems
):
    links = Links(send_sems, recv_sems)
    links.greet()
    finish_columns = collect_columns(links, grad_ref, from_left, from_right, total, slots, PLANES)
    for side, buffer in (("up", from_up), ("down", from_down)):

        @pl.when(jnp.logical_not(links.has[side]))
        def _():
            for part, layer in PLANES:
                buffer[part, layer] = jnp.zeros((2, SIDE, HALF), jnp.float32)

    for side, block in (("left", 0), ("right", 3)):

        @pl.when(jnp.logical_not(links.has[side]))
        def _():
            for part, layer in PLANES:
                out_ref[part, layer, block] = jnp.zeros((2 * SIDE, HALF), jnp.float32)

    arrivals = []
    for index, (part, layer) in enumerate(PLANES):
        finish_columns(index, 0)
        up = links.send(total.at[part, layer, :, pl.ds(0, SIDE)], from_down.at[part, layer], "up")
        finish_columns(index, 1)
        down = links.send(total.at[part, layer, :, pl.ds(SIDE, SIDE)], from_up.at[part, layer], "down")
        arrivals.append((up, down))
    step_up = jnp.where(links.has["up"], OBJECT_STEP, 0.0).astype(jnp.float32)
    step_down = jnp.where(links.has["down"], OBJECT_STEP, 0.0).astype(jnp.float32)
    halos = []
    for index, (part, layer) in enumerate(PLANES):
        for arrived in arrivals[index]:
            arrived()
        for block in range(2):
            for start, buffer, offset, step in (
                (0, from_up, 0, step_up),
                (HALF, from_up, 0, OBJECT_STEP),
                (SIDE, from_down, SIDE, OBJECT_STEP),
                (3 * HALF, from_down, SIDE, step_down),
            ):
                for row in range(start, start + HALF, 64):
                    rows, near = pl.ds(row, 64), pl.ds(row - offset, 64)
                    gradient = total[part, layer, block, rows, :] + buffer[part, layer, block, near, :]
                    out_ref[part, layer, 1 + block, rows, :] = ext_ref[part, layer, 1 + block, rows, :] - step * gradient
        slot = halo_slots.at[part, layer]
        halos.append(links.send_columns(out_ref.at[part, layer, 1], out_ref.at[part, layer, 3], "left", slot))
        halos.append(links.send_columns(out_ref.at[part, layer, 2], out_ref.at[part, layer, 0], "right", slot))
        for forward, _ in halos[2 * index - 2 : 2 * index]:
            forward()
    for forward, _ in halos[-2:]:
        forward()
    for _, arrived in halos:
        for half in range(2):
            arrived(half)
    links.finish()


def last_kernel(
    ext_ref, grad_ref, first_probe_ref, second_probe_ref, probe_ref, object_ref, new_probe_ref,
    from_left, from_right, slots, from_up, from_down, total, partial, pair, landings, sums, gathered, send_sems, recv_sems,
):
    links = Links(send_sems, recv_sems)
    row, col = links.row, links.col
    core, x, y_low = lax.rem(col, 2), lax.rem(col // 2, 4), col // 8
    y_high, z = lax.rem(row, 2), row // 2
    y = y_high * 2 + y_low
    partner = (row, col + 1 - 2 * core)
    plane = lambda k: ((k // 4) * 2 + y_high, y_low * 8 + lax.rem(k, 4) * 2 + core)
    line = lambda k: (z * 2 + k // 2, lax.rem(k, 2) * 8 + x * 2 + core)
    groups = [(z * 4 + x, plane, 16), (y, line, 4)]
    peers = [partner]
    for place, device, members in groups:
        peers += [device(lax.rem(place + k, members)) for k in range(1, members)]
    links.greet(peers)
    count = 4 * SIDE
    half = count // 2

    def rows_at(start, size):
        return pl.ds(pl.multiple_of(start, 8), size)

    def start(source, target, device):
        item = links.copy(source, target, device)
        item.start()
        return item

    def add_probe(rows):
        partial[rows, :] = first_probe_ref[rows, :] + second_probe_ref[rows, :]

    by_rows(0, count, 64, add_probe)
    swap = start(partial.at[rows_at((1 - core) * half, half)], pair, partner)
    finish_columns = collect_columns(links, grad_ref, from_left, from_right, total, slots, PLANES)
    for side, buffer in (("up", from_up), ("down", from_down)):

        @pl.when(jnp.logical_not(links.has[side]))
        def _():
            for part, layer in PLANES:
                buffer[part, layer] = jnp.zeros((2, HALF, HALF), jnp.float32)

    swap.wait_recv()
    base = core * half

    def add_pair(index, carry):
        near = pl.ds(pl.multiple_of(index * 64, 64), 64)
        mine = rows_at(base + index * 64, 64)
        sums[mine, :] = partial[mine, :] + pair[near, :]
        return carry

    lax.fori_loop(0, half // 64, add_pair, 0)
    gathers = [swap]
    places = []
    arrivals = []

    def scatter(number, base, size):
        place, device, members = groups[number]
        items = []
        for k in range(1, members):
            other = lax.rem(place + k, members)
            source = sums.at[rows_at(base + other * size, size)]
            items.append(start(source, landings[number].at[k - 1], device(other)))
        gathers.extend(items)
        places.append((place, device, members, base, size))
        return items

    def reduce(number, items, base, size):
        for item in items:
            item.wait_recv()
        mine = rows_at(base, size)
        value = sums[mine, :]
        for k in range(len(items)):
            value = value + landings[number][k]
        (gathered if number == len(groups) - 1 else sums)[mine, :] = value

    def rows_out(index):
        part, layer = PLANES[index]
        finish_columns(index, 0)
        up = links.send(total.at[part, layer, :, pl.ds(0, HALF)], from_down.at[part, layer], "up")
        finish_columns(index, 1)
        down = links.send(total.at[part, layer, :, pl.ds(3 * HALF, HALF)], from_up.at[part, layer], "down")
        arrivals.append((up, down))

    size = half // 16
    items = scatter(0, base, size)
    rows_out(0)
    rows_out(1)
    base = base + groups[0][0] * size
    reduce(0, items, base, size)
    size = size // 4
    items = scatter(1, base, size)
    rows_out(2)
    rows_out(3)
    base = base + groups[1][0] * size
    reduce(1, items, base, size)
    for place, device, members, group_base, size in reversed(places):
        mine = rows_at(group_base + place * size, size)
        items = [
            start(gathered.at[mine], gathered.at[mine], device(lax.rem(place + k, members))) for k in range(1, members)
        ]
        gathers += items
        for item in items:
            item.wait_recv()
    mine = rows_at(core * half, half)
    swap_back = start(gathered.at[mine], gathered.at[mine], partner)
    for index, (part, layer) in enumerate(PLANES):
        for arrived in arrivals[index]:
            arrived()
        for block in range(2):
            lane = pl.ds(block * HALF, HALF)
            for begin, buffer in ((HALF, from_up), (SIDE, from_down)):
                for offset in range(0, HALF, 64):
                    rows, near = pl.ds(begin + offset, 64), pl.ds(offset, 64)
                    gradient = total[part, layer, block, rows, :] + buffer[part, layer, block, near, :]
                    target = pl.ds(begin - HALF + offset, 64)
                    object_ref[part, layer, target, lane] = (
                        ext_ref[part, layer, 1 + block, rows, :] - OBJECT_STEP * gradient
                    )
    swap_back.wait_recv()

    def finish_probe(rows):
        new_probe_ref[rows, :] = probe_ref[rows, :] - PROBE_STEP * gathered[rows, :]

    by_rows(0, count, 64, finish_probe)
    for item in gathers + [swap_back]:
        item.wait_send()
    links.finish()


def vmem_specs(count):
    return [pl.BlockSpec(memory_space=pltpu.VMEM)] * count


def comm_params(identity, limit):
    return pltpu.CompilerParams(collective_id=identity, has_side_effects=True, vmem_limit_bytes=limit << 20)


def semaphores(count):
    return [pltpu.SemaphoreType.DMA((count,)), pltpu.SemaphoreType.DMA((count,))]


def f32(*shape):
    return pltpu.VMEM(shape, jnp.float32)


EXTENDED = jax.ShapeDtypeStruct((2, 2, 4, 2 * SIDE, HALF), jnp.float32)


def first_exchange(tile, amplitudes, table, probe_modes):
    planes = amplitudes.shape[0]
    inputs = (tile, amplitudes, jnp.asarray(ORDER), jnp.asarray(ORDER.T), table, probe_modes)
    return pl.pallas_call(
        first_kernel,
        out_shape=(
            EXTENDED,
            jax.ShapeDtypeStruct((planes, SIDE, SIDE), jnp.float32),
            jax.ShapeDtypeStruct(table.shape, table.dtype),
            jax.ShapeDtypeStruct(probe_modes.shape, probe_modes.dtype),
        ),
        in_specs=[pl.BlockSpec(memory_space=pltpu.HBM)] * 6,
        out_specs=tuple(vmem_specs(4)),
        scratch_shapes=[
            f32(planes, SIDE, SIDE),
            pltpu.VMEM((SIDE, SIDE), jnp.bfloat16),
            pltpu.VMEM((SIDE, SIDE), jnp.bfloat16),
            f32(2, 3, 2, SIDE // 4, HALF),
            f32(2, 2, 3, 2, HALF // 4, HALF),
            pltpu.SemaphoreType.DMA((7,)),
            *semaphores(8 + 9 * 12),
        ],
        compiler_params=comm_params(0, 14),
    )(*[pltpu.with_memory_space_constraint(value, pltpu.HBM) for value in inputs])


def columns_buffers():
    return [f32(2, 2, 2 * SIDE, HALF), f32(2, 2, 2 * SIDE, HALF), f32(2, 2, 3, HALF, HALF)]


def middle_exchange(extended, gradient):
    return pl.pallas_call(
        middle_kernel,
        out_shape=EXTENDED,
        in_specs=vmem_specs(2),
        out_specs=vmem_specs(1)[0],
        scratch_shapes=[
            *columns_buffers(),
            f32(2, 2, 2, SIDE, HALF),
            f32(2, 2, 2, SIDE, HALF),
            f32(2, 2, 2, 2 * SIDE, HALF),
            f32(2, 2, 3, HALF, HALF),
            *semaphores(72 + 8 + 72),
        ],
        compiler_params=comm_params(1, 24),
    )(extended, gradient)


def last_exchange(extended, gradient, first_probe, second_probe, probe_modes):
    flat = (4 * SIDE, SIDE)
    new_object, new_probe = pl.pallas_call(
        last_kernel,
        out_shape=(
            jax.ShapeDtypeStruct((2, 2, SIDE, SIDE), jnp.float32),
            jax.ShapeDtypeStruct(flat, jnp.float32),
        ),
        in_specs=vmem_specs(5),
        out_specs=tuple(vmem_specs(2)),
        scratch_shapes=[
            *columns_buffers(),
            f32(2, 2, 2, HALF, HALF),
            f32(2, 2, 2, HALF, HALF),
            f32(2, 2, 2, 2 * SIDE, HALF),
            f32(*flat),
            f32(2 * SIDE, SIDE),
            [f32(15, 2 * SIDE // 16, SIDE), f32(3, 2 * SIDE // 64, SIDE)],
            f32(*flat),
            f32(*flat),
            *semaphores(72 + 8 + 2 + 2 * 18),
        ],
        compiler_params=comm_params(2, 26),
    )(extended, gradient, first_probe.reshape(flat), second_probe.reshape(flat), probe_modes.reshape(flat))
    return new_object, new_probe.reshape(probe_modes.shape)


def batch_kernel(
    batch, offset_ref, count_ref, ext_ref, probe_ref, amp_ref, table_ref, grad_ref, probe_grad_ref,
    obj, psi, right_a, right_b, yield_a, yield_b, left_a, left_b, out_a, out_b,
):
    lanes = lax.broadcasted_iota(jnp.int32, (CHUNK, HALF), 1)
    lo, hi = pl.ds(0, HALF), pl.ds(HALF, HALF)

    def chunks(total, body):
        def step(index, carry):
            body(pl.multiple_of(index * CHUNK, CHUNK))
            return carry

        lax.fori_loop(0, total // CHUNK, step, 0, unroll=True)

    def bf(value):
        return value.astype(jnp.bfloat16)

    def zero_grad(row):
        for part in range(2):
            for layer in range(2):
                for block in range(4):
                    grad_ref[part, layer, block, pl.ds(row, CHUNK), :] = jnp.zeros((CHUNK, HALF), jnp.float32)

    chunks(2 * SIDE, zero_grad)

    def zero_probe(row):
        for part in range(2):
            for mode in range(MODES):
                probe_grad_ref[part, mode, pl.ds(row, CHUNK), :] = jnp.zeros((CHUNK, SIDE), jnp.float32)

    chunks(SIDE, zero_probe)

    def right(table_a, table_b):
        yield_a[...] = dot(right_a[...], table_ref[table_a])
        yield_b[...] = dot(right_b[...], table_ref[table_b])

    def left(table_a, table_b):
        out_a[...] = dot(table_ref[table_a], left_a[...])
        out_b[...] = dot(table_ref[table_b], left_b[...])

    def put_split(mode, row, re, im):
        at = pl.ds(mode * SIDE + row, CHUNK)
        right_a[at, lo] = bf(re[0] + re[1])
        right_a[at, hi] = bf(im[0] + im[1])
        right_b[at, lo] = bf(re[0] - re[1])
        right_b[at, hi] = bf(im[0] - im[1])

    def columns(ref, mode):
        return pl.ds(mode * SIDE, HALF), pl.ds(mode * SIDE + HALF, HALF)

    def middle_spread(row):
        for mode in range(MODES):
            here = columns(left_a, mode)
            for part, lane in ((0, lo), (1, hi)):
                top = pl.ds(mode * SIDE + row, CHUNK)
                low = pl.ds(mode * SIDE + HALF + row, CHUNK)
                at, ab = yield_a[top, lane], yield_a[low, lane]
                bt, bb = yield_b[top, lane], yield_b[low, lane]
                to = pl.ds(part * HALF + row, CHUNK)
                a_sum, a_dif = at + ab, at - ab
                b_sum, b_dif = bt + bb, bt - bb
                left_a[to, here[0]] = bf(a_sum + b_sum)
                left_a[to, here[1]] = bf(a_sum - b_sum)
                left_b[to, here[0]] = bf(a_dif + b_dif)
                left_b[to, here[1]] = bf(a_dif - b_dif)

    def middle_forward(row):
        for mode in range(MODES):
            here = columns(left_a, mode)
            for part, lane in ((0, lo), (1, hi)):
                top = pl.ds(mode * SIDE + row, CHUNK)
                low = pl.ds(mode * SIDE + HALF + row, CHUNK)
                to = pl.ds(part * HALF + row, CHUNK)
                for source, at in ((yield_a, here[0]), (yield_b, here[1])):
                    upper, lower = source[top, lane], source[low, lane]
                    left_a[to, at] = bf(upper + lower)
                    left_b[to, at] = bf(upper - lower)

    def middle_backward(row):
        for mode in range(MODES):
            here = columns(left_a, mode)
            for part, lane in ((0, lo), (1, hi)):
                to = pl.ds(part * HALF + row, CHUNK)
                for base, target in ((0, left_a), (HALF, left_b)):
                    at = pl.ds(mode * SIDE + base + row, CHUNK)
                    even, odd = yield_a[at, lane], yield_b[at, lane]
                    target[to, here[0]] = bf(even + odd)
                    target[to, here[1]] = bf(even - odd)

    def joined(mode, row):
        result = []
        for sign in (1, -1):
            pair = []
            for part in range(2):
                at = pl.ds(part * HALF + row, CHUNK)
                halves = []
                for lane in columns(out_a, mode):
                    a, b = out_a[at, lane], out_b[at, lane]
                    halves.append(a + b if sign > 0 else a - b)
                pair.append(halves)
            result.append(pair)
        return result

    def pair_of(ref, first, second, row):
        return [ref[first, second, pl.ds(row, CHUNK), lane] for lane in (lo, hi)]

    def one_slot(slot, carry):
        start_row = offset_ref[batch, 0, slot, 0]
        start_col = offset_ref[batch, 1, slot, 0]
        base = start_col // HALF
        shift = start_col % HALF
        take_left = lanes < HALF - shift
        put_right = lanes >= shift
        back = lax.rem(HALF - shift, HALF)

        def fetch(row):
            for part in range(2):
                for layer in range(2):
                    at = pl.ds(start_row + row, CHUNK)
                    turned = [pltpu.roll(ext_ref[part, layer, base + k, at, :], back, 1) for k in range(3)]
                    obj[part, layer, pl.ds(row, CHUNK), lo] = jnp.where(take_left, turned[0], turned[1])
                    obj[part, layer, pl.ds(row, CHUNK), hi] = jnp.where(take_left, turned[1], turned[2])

        chunks(SIDE, fetch)

        def enter(row):
            o_re, o_im = pair_of(obj, 0, 0, row), pair_of(obj, 1, 0, row)
            for mode in range(MODES):
                p_re, p_im = pair_of(probe_ref, 0, mode, row), pair_of(probe_ref, 1, mode, row)
                re = [p_re[k] * o_re[k] - p_im[k] * o_im[k] for k in range(2)]
                im = [p_re[k] * o_im[k] + p_im[k] * o_re[k] for k in range(2)]
                put_split(mode, row, re, im)

        chunks(SIDE, enter)
        right(SUM_R, DIF_R)
        chunks(HALF, middle_spread)
        left(SUM_L, DIF_L)

        def second_slice(row):
            for side in range(2):
                at = row + side * HALF
                o_re, o_im = pair_of(obj, 0, 1, at), pair_of(obj, 1, 1, at)
                for mode in range(MODES):
                    w_re, w_im = joined(mode, row)[side]
                    for k, lane in ((0, lo), (1, hi)):
                        psi[0, mode, pl.ds(at, CHUNK), lane] = w_re[k]
                        psi[1, mode, pl.ds(at, CHUNK), lane] = w_im[k]
                    re = [w_re[k] * o_re[k] - w_im[k] * o_im[k] for k in range(2)]
                    im = [w_re[k] * o_im[k] + w_im[k] * o_re[k] for k in range(2)]
                    put_split(mode, at, re, im)

        chunks(HALF, second_slice)
        right(EVEN_R, ODD_R)
        chunks(HALF, middle_forward)
        left(EVEN_L, ODD_L)

        def compare(row):
            for base_row, source in ((0, out_a), (HALF, out_b)):
                waves = []
                for mode in range(MODES):
                    here = columns(source, mode)
                    re = [source[pl.ds(row, CHUNK), lane] for lane in here]
                    im = [source[pl.ds(HALF + row, CHUNK), lane] for lane in here]
                    waves.append((re, im))
                for k, lane in ((0, lo), (1, hi)):
                    intensity = waves[0][0][k] * waves[0][0][k] + waves[0][1][k] * waves[0][1][k]
                    for re, im in waves[1:]:
                        intensity = intensity + (re[k] * re[k] + im[k] * im[k])
                    amplitude = amp_ref[batch * (amp_ref.shape[0] // 2) + slot, pl.ds(base_row + row, CHUNK), lane]
                    ratio = 1.0 - amplitude * lax.rsqrt(jnp.maximum(intensity, AMPLITUDE_FLOOR**2))
                    target = right_a if k == 0 else right_b
                    for mode, (re, im) in enumerate(waves):
                        at = pl.ds(mode * SIDE + base_row + row, CHUNK)
                        target[at, lo] = bf(re[k] * ratio)
                        target[at, hi] = bf(im[k] * ratio)

        chunks(HALF, compare)
        right(EVEN_L, ODD_L)
        chunks(HALF, middle_backward)
        left(EVEN_R, ODD_R)

        def add_term(part, layer, row, term):
            turned = [pltpu.roll(value, shift, 1) for value in term]
            zero = jnp.zeros_like(turned[0])
            spread = [
                jnp.where(put_right, turned[0], zero),
                jnp.where(put_right, turned[1], turned[0]),
                jnp.where(put_right, zero, turned[1]),
            ]
            at = pl.ds(start_row + row, CHUNK)
            for k in range(3):
                grad_ref[part, layer, base + k, at, :] = grad_ref[part, layer, base + k, at, :] + spread[k]

        def object_term(layer, row, waves, backs):
            re, im = [], []
            for k in range(2):
                re.append(sum(w[0][k] * b[0][k] + w[1][k] * b[1][k] for w, b in zip(waves, backs)))
                im.append(sum(w[0][k] * b[1][k] - w[1][k] * b[0][k] for w, b in zip(waves, backs)))
            add_term(0, layer, row, re)
            add_term(1, layer, row, im)

        def last_back(row):
            for side in range(2):
                at = row + side * HALF
                backs = [joined(mode, row)[side] for mode in range(MODES)]
                waves = [(pair_of(psi, 0, mode, at), pair_of(psi, 1, mode, at)) for mode in range(MODES)]
                o_re, o_im = pair_of(obj, 0, 1, at), pair_of(obj, 1, 1, at)
                for mode, (b_re, b_im) in enumerate(backs):
                    re = [o_re[k] * b_re[k] + o_im[k] * b_im[k] for k in range(2)]
                    im = [o_re[k] * b_im[k] - o_im[k] * b_re[k] for k in range(2)]
                    put_split(mode, at, re, im)
                object_term(1, at, waves, backs)

        chunks(HALF, last_back)
        right(SUM_L, DIF_L)
        chunks(HALF, middle_spread)
        left(SUM_R, DIF_R)

        def first_back(row):
            for side in range(2):
                at = row + side * HALF
                backs = [joined(mode, row)[side] for mode in range(MODES)]
                waves = [(pair_of(probe_ref, 0, mode, at), pair_of(probe_ref, 1, mode, at)) for mode in range(MODES)]
                o_re, o_im = pair_of(obj, 0, 0, at), pair_of(obj, 1, 0, at)
                for mode, (b_re, b_im) in enumerate(backs):
                    for k, lane in ((0, lo), (1, hi)):
                        spot = (mode, pl.ds(at, CHUNK), lane)
                        probe_grad_ref[(0, *spot)] = probe_grad_ref[(0, *spot)] + (o_re[k] * b_re[k] + o_im[k] * b_im[k])
                        probe_grad_ref[(1, *spot)] = probe_grad_ref[(1, *spot)] + (o_re[k] * b_im[k] - o_im[k] * b_re[k])
                object_term(0, at, waves, backs)

        chunks(HALF, first_back)
        return carry

    lax.fori_loop(0, count_ref[batch, 0, 0], one_slot, 0)


def batch_terms(batch, extended, probe_modes, amplitudes, offsets, counts, table):
    vmem = pl.BlockSpec(memory_space=pltpu.VMEM)
    smem = pl.BlockSpec(memory_space=pltpu.SMEM)
    field = pltpu.VMEM((2, 2, SIDE, SIDE), jnp.float32)
    return pl.pallas_call(
        functools.partial(batch_kernel, batch),
        out_shape=(
            jax.ShapeDtypeStruct((2, 2, 4, 2 * SIDE, HALF), jnp.float32),
            jax.ShapeDtypeStruct((2, MODES, SIDE, SIDE), jnp.float32),
        ),
        in_specs=[smem, smem, vmem, vmem, vmem, vmem],
        out_specs=(vmem, vmem),
        scratch_shapes=[
            field,
            field,
            pltpu.VMEM((MODES * SIDE, SIDE), jnp.bfloat16),
            pltpu.VMEM((MODES * SIDE, SIDE), jnp.bfloat16),
            pltpu.VMEM((MODES * SIDE, SIDE), jnp.float32),
            pltpu.VMEM((MODES * SIDE, SIDE), jnp.float32),
            pltpu.VMEM((SIDE, MODES * SIDE), jnp.bfloat16),
            pltpu.VMEM((SIDE, MODES * SIDE), jnp.bfloat16),
            pltpu.VMEM((SIDE, MODES * SIDE), jnp.float32),
            pltpu.VMEM((SIDE, MODES * SIDE), jnp.float32),
        ],
        compiler_params=pltpu.CompilerParams(vmem_limit_bytes=26 << 20),
        cost_estimate=pl.CostEstimate(flops=3 * 64 * SIDE**3, bytes_accessed=12 << 20, transcendentals=0),
    )(offsets, counts, extended, probe_modes, amplitudes, table)


def body(object_field, probe_modes, amplitudes, offsets, counts):
    batches, slots = amplitudes.shape[:2]
    table = jnp.asarray(TABLES)
    extended, ordered, table, probe_modes = first_exchange(
        object_field, amplitudes.reshape(batches * slots, SIDE, SIDE), table, probe_modes
    )
    terms = lambda cells, batch: batch_terms(batch, cells, probe_modes, ordered, offsets, counts, table)
    gradient, first_probe = terms(extended, 0)
    extended = middle_exchange(extended, gradient)
    gradient, second_probe = terms(extended, 1)
    return last_exchange(extended, gradient, first_probe, second_probe, probe_modes)


def solution(mesh):
    return jax.shard_map(
        body,
        mesh=mesh,
        in_specs=(
            P(None, None, "row", "col"),
            P(),
            P(None, "row", "col", None, None),
            P(None, None, "row", "col"),
            P(None, "row", "col"),
        ),
        out_specs=(P(None, None, "row", "col"), P()),
        check_vma=False,
    )
```

```python
import functools
import math

import jax
import jax.numpy as jnp
import numpy as np
from jax import lax
from jax.experimental import pallas as pl
from jax.experimental.pallas import tpu as pltpu
from jax.sharding import PartitionSpec as P

AMPLITUDE_FLOOR = 0.5
OBJECT_STEP = 0.25
PROBE_STEP = 0.125
SIDE = 256
HALF = SIDE // 2
MODES = 2
CHUNK = 16
RELAYED_CORNER_LAYERS = 1
MIDDLE_DIRECT_GRADIENTS = (0,)
MIDDLE_DIRECT_HALOS = (3,)
LAST_DIRECT_GRADIENTS = (0,)
MESH = pl.DeviceIdType.MESH
SIDES = ("up", "down", "left", "right")
OPPOSITE = {"up": "down", "down": "up", "left": "right", "right": "left"}


def real_form(table):
    re, im = table.real, table.imag
    return np.block([[re, im], [-im, re]]).astype(jnp.bfloat16)


def make_tables():
    index = np.arange(SIDE)
    angles = (index[:, None] * index[None, :] % SIDE).astype(np.float32) * np.float32(2.0 * math.pi / SIDE)
    scale = np.float32(1.0 / math.sqrt(SIDE))
    rounded = lambda v: (v * scale).astype(jnp.bfloat16).astype(np.float64)
    forward = rounded(np.cos(angles)) - 1j * rounded(np.sin(angles))
    frequency = np.where(index < HALF, index, index - SIDE).astype(np.float64)
    chirp = np.exp(-2j * math.pi * (frequency * frequency % (16 * SIDE)) / (16 * SIDE))
    spread = (forward.conj() * chirp[None, :]) @ forward
    same = 0.25 * (spread[:HALF, :HALF] + spread[HALF:, HALF:] + spread[:HALF, HALF:] + spread[HALF:, :HALF])
    other = 0.25 * (spread[:HALF, :HALF] + spread[HALF:, HALF:] - spread[:HALF, HALF:] - spread[HALF:, :HALF])
    same = 0.5 * (same + same.T)
    other = 0.5 * (other + other.T)
    even = forward[:HALF, 0::2]
    odd = forward[:HALF, 1::2]
    rows = []
    for table in (same, other, even, odd):
        matrix = real_form(table)
        rows += [matrix, np.ascontiguousarray(matrix.T)]
    order = np.zeros((SIDE, SIDE), np.float32)
    order[0::2, :HALF] = np.eye(HALF)
    order[1::2, HALF:] = np.eye(HALF)
    return np.stack(rows), order.astype(jnp.bfloat16)


TABLES, ORDER = make_tables()
(SUM_R, SUM_L, DIF_R, DIF_L, EVEN_R, EVEN_L, ODD_R, ODD_L) = range(8)


def dot(left, right):
    return jnp.dot(left, right, preferred_element_type=jnp.float32)


def three_parts(value):
    high = value.astype(jnp.bfloat16)
    rest = value - high.astype(jnp.float32)
    middle = rest.astype(jnp.bfloat16)
    return high, middle, (rest - middle.astype(jnp.float32)).astype(jnp.bfloat16)


def reorder_plane(plane, order, turn):
    high, middle, low = [dot(part, order) for part in three_parts(plane)]
    high, middle, low = [dot(turn, part) for part in three_parts(high + (middle + low))]
    return high + (middle + low)


class Links:
    def __init__(self, send_sems, recv_sems):
        self.row, self.col = lax.axis_index("row"), lax.axis_index("col")
        rows, cols = lax.axis_size("row"), lax.axis_size("col")
        self.has = {
            "up": self.row > 0,
            "down": self.row < rows - 1,
            "left": self.col > 0,
            "right": self.col < cols - 1,
        }
        self.at = {
            "up": (self.row - 1, self.col),
            "down": (self.row + 1, self.col),
            "left": (self.row, self.col - 1),
            "right": (self.row, self.col + 1),
        }
        middle, last = cols // 2, cols - 1
        relays = {"right": (last, last - 2, last - 4), "left": (0, 2, 4)}
        self.crosses = {"right": self.col == middle - 1, "left": self.col == middle}
        self.beyond = {"right": (self.row, middle), "left": (self.row, middle - 1)}
        self.relay = {side: [(self.row, col) for col in relays[side]] for side in relays}
        self.relays = {side: [self.col == col for col in relays[side]] for side in relays}
        self.send_sems, self.recv_sems = send_sems, recv_sems
        self.used = 0
        self.sent = []

    def greet(self, peers=()):
        barrier = pltpu.get_barrier_semaphore()
        for side in SIDES:

            @pl.when(self.has[side])
            def _():
                pl.semaphore_signal(barrier, inc=1, device_id=self.at[side], device_id_type=MESH)

        inner = jnp.logical_or(self.crosses["left"], self.crosses["right"])
        outer = functools.reduce(jnp.logical_or, self.relays["left"] + self.relays["right"])
        extra = 6 * inner.astype(jnp.int32) + 2 * outer.astype(jnp.int32)
        for condition, devices in (
            (inner, self.relay["left"] + self.relay["right"]),
            (outer, list(self.beyond.values())),
        ):

            @pl.when(condition)
            def _():
                for device in devices:
                    pl.semaphore_signal(barrier, inc=1, device_id=device, device_id_type=MESH)

        for peer in peers:
            pl.semaphore_signal(barrier, inc=1, device_id=peer, device_id_type=MESH)
        pl.semaphore_wait(barrier, len(peers) + extra + sum(self.has[side].astype(jnp.int32) for side in SIDES))

    def copy(self, source, target, device):
        index = self.used
        self.used += 1
        return pltpu.make_async_remote_copy(
            src_ref=source,
            dst_ref=target,
            send_sem=self.send_sems.at[index],
            recv_sem=self.recv_sems.at[index],
            device_id=device,
            device_id_type=MESH,
        )

    def send(self, source, target, side, also=None):
        item = self.copy(source, target, self.at[side])
        condition = self.has[side] if also is None else jnp.logical_and(self.has[side], also)

        @pl.when(condition)
        def _():
            item.start()

        self.sent.append((item, condition))
        source_side = self.has[OPPOSITE[side]]
        arrives = source_side if also is None else jnp.logical_and(source_side, also)

        def arrived():
            @pl.when(arrives)
            def _():
                item.wait_recv()

        return arrived

    def send_straight(self, source, target, side, also):
        rows = source.shape[-2]
        lead = (slice(None),) * (len(source.shape) - 2)
        halves = [(*lead, pl.ds(k * rows // 2, rows // 2)) for k in range(2)]
        waits = [self.send(source.at[at], target.at[at], side, also) for at in halves]
        return (lambda: None), (lambda half: waits[half]())

    def send_columns(self, source, target, side, slots, also=None, relay=True):
        if not relay:
            return self.send_straight(source, target, side, also)
        rows = source.shape[-2]
        lead = (slice(None),) * (len(source.shape) - 2)
        halves = [(*lead, pl.ds(k * rows // 2, rows // 2)) for k in range(2)]
        quarters = [(*lead, pl.ds(k * rows // 4, rows // 4)) for k in range(4)]
        both = lambda a: a if also is None else jnp.logical_and(a, also)
        crosses = self.crosses[side]
        direct = both(jnp.logical_and(self.has[side], jnp.logical_not(crosses)))
        whole = [(self.copy(source.at[at], target.at[at], self.at[side]), direct) for at in halves]
        first = self.copy(source.at[quarters[0]], target.at[quarters[0]], self.at[side])
        detours, onwards = [], []
        for k in range(3):
            at = quarters[k + 1]
            detours.append(self.copy(source.at[at], slots.at[k], self.relay[side][k]))
            onwards.append(self.copy(slots.at[k], target.at[at], self.beyond[side]))
        going = [(item, both(crosses)) for item in [*detours, first]] + whole
        for item, condition in going:

            @pl.when(condition)
            def _():
                item.start()

        relays = [both(here) for here in self.relays[side]]
        self.sent += going + list(zip(onwards, relays))
        receives_parts = self.crosses[OPPOSITE[side]]
        receives_whole = both(jnp.logical_and(self.has[OPPOSITE[side]], jnp.logical_not(receives_parts)))
        receives_parts = both(receives_parts)

        def forward():
            for detour, onward, here in zip(detours, onwards, relays):

                @pl.when(here)
                def _():
                    detour.wait_recv()
                    onward.start()

        def arrived(half):
            @pl.when(receives_whole)
            def _():
                whole[half][0].wait_recv()

            @pl.when(receives_parts)
            def _():
                for item in (first, onwards[0]) if half == 0 else onwards[1:]:
                    item.wait_recv()

        return forward, arrived

    def finish(self):
        for item, condition in self.sent:

            @pl.when(condition)
            def _():
                item.wait_send()


def by_rows(start, stop, step, body):
    def one(index, carry):
        body(pl.ds(pl.multiple_of(start + index * step, 8), step))
        return carry

    lax.fori_loop(0, (stop - start) // step, one, 0)


def first_kernel(
    tile_ref, amp_ref, order_ref, turn_ref, table_ref, probe_ref, ext_ref, ordered_ref, table_out, probe_out,
    planes, order, turn, tile_slots, corner_slots, local_sems, send_sems, recv_sems,
):
    links = Links(send_sems, recv_sems)
    upper, lower, own = pl.ds(0, HALF), pl.ds(3 * HALF, HALF), pl.ds(HALF, SIDE)
    local = [
        pltpu.make_async_copy(amp_ref, planes, local_sems.at[0]),
        pltpu.make_async_copy(order_ref, order, local_sems.at[1]),
        pltpu.make_async_copy(turn_ref, turn, local_sems.at[2]),
    ]
    inner = [
        pltpu.make_async_copy(
            tile_ref.at[:, :, :, pl.ds(block * HALF, HALF)], ext_ref.at[:, :, 1 + block, own], local_sems.at[3 + block]
        )
        for block in range(2)
    ]
    extra = [
        pltpu.make_async_copy(table_ref, table_out, local_sems.at[5]),
        pltpu.make_async_copy(probe_ref, probe_out, local_sems.at[6]),
    ]
    for item in local + inner + extra:
        item.start()
    links.greet()
    waits, col_waits, corner_waits = [], [], []
    for layer in range(2):
        for side, start, block in (("left", 0, 3), ("right", HALF, 0)):
            col_waits.append(
                links.send_columns(
                    tile_ref.at[:, layer, :, pl.ds(start, HALF)],
                    ext_ref.at[:, layer, block, own],
                    side,
                    tile_slots.at[layer],
                )
            )
    for layer in range(2):
        arrivals = []
        for block in range(2):
            lane = pl.ds(block * HALF, HALF)
            arrivals.append(
                links.send(tile_ref.at[:, layer, pl.ds(0, HALF), lane], ext_ref.at[:, layer, 1 + block, lower], "up")
            )
            arrivals.append(
                links.send(tile_ref.at[:, layer, pl.ds(HALF, HALF), lane], ext_ref.at[:, layer, 1 + block, upper], "down")
            )
        waits.append(arrivals)

    def clear(side, blocks, rows):
        @pl.when(jnp.logical_not(links.has[side]))
        def _():
            for part, layer in PLANES:
                for block in blocks:
                    ext_ref[part, layer, block, rows, :] = jnp.zeros((rows.size, HALF), jnp.float32)

    clear("up", (1, 2), upper)
    clear("down", (1, 2), lower)
    clear("left", (0,), own)
    clear("right", (3,), own)
    for rows, side in ((upper, "up"), (lower, "down")):
        for block, other in ((0, "left"), (3, "right")):

            @pl.when(jnp.logical_not(jnp.logical_and(links.has[side], links.has[other])))
            def _():
                for part, layer in PLANES:
                    ext_ref[part, layer, block, rows, :] = jnp.zeros((HALF, HALF), jnp.float32)

    for item in local:
        item.wait()

    def one_plane(index, carry):
        ordered_ref[index] = reorder_plane(planes[index], order[...], turn[...])
        return carry

    lax.fori_loop(0, planes.shape[0], one_plane, 0)
    for forward, _ in col_waits:
        forward()
    for layer in range(2):
        for arrived in waits[layer]:
            arrived()
        for number, (rows, side) in enumerate(((upper, "up"), (lower, "down"))):
            for block, to, target in ((1, "left", 3), (2, "right", 0)):
                corner_waits.append(
                    links.send_columns(
                        ext_ref.at[:, layer, block, rows],
                        ext_ref.at[:, layer, target, rows],
                        to,
                        corner_slots.at[layer, number],
                        also=links.has[side],
                        relay=layer < RELAYED_CORNER_LAYERS,
                    )
                )
    for forward, _ in corner_waits:
        forward()
    for item in inner + extra:
        item.wait()
    for _, arrived in col_waits + corner_waits:
        for half in range(2):
            arrived(half)
    links.finish()


PLANES = [(part, layer) for layer in range(2) for part in range(2)]


def collect_columns(links, grad_ref, from_left, from_right, total, slots, order, straight):
    for side, buffer in (("left", from_left), ("right", from_right)):

        @pl.when(jnp.logical_not(links.has[side]))
        def _():
            for part, layer in order:
                buffer[part, layer] = jnp.zeros((2 * SIDE, HALF), jnp.float32)

    arrivals = []
    for number, (part, layer) in enumerate(order):
        relay = number not in straight
        arrivals.append(
            (
                links.send_columns(grad_ref.at[part, layer, 0], from_right.at[part, layer], "left", slots.at[part, layer], relay=relay),
                links.send_columns(grad_ref.at[part, layer, 3], from_left.at[part, layer], "right", slots.at[part, layer], relay=relay),
            )
        )

    def finish(index, half):
        part, layer = order[index]
        for forward, arrived in arrivals[index]:
            if half == 0:
                forward()
            arrived(half)

        def add(rows):
            total[part, layer, 0, rows, :] = grad_ref[part, layer, 1, rows, :] + from_left[part, layer, rows, :]
            total[part, layer, 1, rows, :] = grad_ref[part, layer, 2, rows, :] + from_right[part, layer, rows, :]

        by_rows(half * SIDE, (half + 1) * SIDE, 64, add)

    return finish


def middle_kernel(
    ext_ref, grad_ref, out_ref, from_left, from_right, slots, from_up, from_down, total, halo_slots, send_sems, recv_sems
):
    links = Links(send_sems, recv_sems)
    links.greet()
    finish_columns = collect_columns(links, grad_ref, from_left, from_right, total, slots, PLANES, MIDDLE_DIRECT_GRADIENTS)
    for side, buffer in (("up", from_up), ("down", from_down)):

        @pl.when(jnp.logical_not(links.has[side]))
        def _():
            for part, layer in PLANES:
                buffer[part, layer] = jnp.zeros((2, SIDE, HALF), jnp.float32)

    for side, block in (("left", 0), ("right", 3)):

        @pl.when(jnp.logical_not(links.has[side]))
        def _():
            for part, layer in PLANES:
                out_ref[part, layer, block] = jnp.zeros((2 * SIDE, HALF), jnp.float32)

    arrivals = []
    for index, (part, layer) in enumerate(PLANES):
        finish_columns(index, 0)
        up = links.send(total.at[part, layer, :, pl.ds(0, SIDE)], from_down.at[part, layer], "up")
        finish_columns(index, 1)
        down = links.send(total.at[part, layer, :, pl.ds(SIDE, SIDE)], from_up.at[part, layer], "down")
        arrivals.append((up, down))
    step_up = jnp.where(links.has["up"], OBJECT_STEP, 0.0).astype(jnp.float32)
    step_down = jnp.where(links.has["down"], OBJECT_STEP, 0.0).astype(jnp.float32)
    halos = []
    for index, (part, layer) in enumerate(PLANES):
        for arrived in arrivals[index]:
            arrived()
        for block in range(2):
            for start, buffer, offset, step in (
                (0, from_up, 0, step_up),
                (HALF, from_up, 0, OBJECT_STEP),
                (SIDE, from_down, SIDE, OBJECT_STEP),
                (3 * HALF, from_down, SIDE, step_down),
            ):
                for row in range(start, start + HALF, 64):
                    rows, near = pl.ds(row, 64), pl.ds(row - offset, 64)
                    gradient = total[part, layer, block, rows, :] + buffer[part, layer, block, near, :]
                    out_ref[part, layer, 1 + block, rows, :] = ext_ref[part, layer, 1 + block, rows, :] - step * gradient
        slot = halo_slots.at[part, layer]
        halos.append(links.send_columns(out_ref.at[part, layer, 1], out_ref.at[part, layer, 3], "left", slot, relay=index not in MIDDLE_DIRECT_HALOS))
        halos.append(links.send_columns(out_ref.at[part, layer, 2], out_ref.at[part, layer, 0], "right", slot, relay=index not in MIDDLE_DIRECT_HALOS))
        for forward, _ in halos[2 * index - 2 : 2 * index]:
            forward()
    for forward, _ in halos[-2:]:
        forward()
    for _, arrived in halos:
        for half in range(2):
            arrived(half)
    links.finish()


def last_kernel(
    ext_ref, grad_ref, first_probe_ref, second_probe_ref, probe_ref, object_ref, new_probe_ref,
    from_left, from_right, slots, from_up, from_down, total, partial, pair, landings, sums, gathered, send_sems, recv_sems,
):
    links = Links(send_sems, recv_sems)
    row, col = links.row, links.col
    core, x, y_low = lax.rem(col, 2), lax.rem(col // 2, 4), col // 8
    y_high, z = lax.rem(row, 2), row // 2
    y = y_high * 2 + y_low
    partner = (row, col + 1 - 2 * core)
    plane = lambda k: ((k // 4) * 2 + y_high, y_low * 8 + lax.rem(k, 4) * 2 + core)
    line = lambda k: (z * 2 + k // 2, lax.rem(k, 2) * 8 + x * 2 + core)
    groups = [(z * 4 + x, plane, 16), (y, line, 4)]
    peers = [partner]
    for place, device, members in groups:
        peers += [device(lax.rem(place + k, members)) for k in range(1, members)]
    links.greet(peers)
    count = 4 * SIDE
    half = count // 2

    def rows_at(start, size):
        return pl.ds(pl.multiple_of(start, 8), size)

    def start(source, target, device):
        item = links.copy(source, target, device)
        item.start()
        return item

    def add_probe(rows):
        partial[rows, :] = first_probe_ref[rows, :] + second_probe_ref[rows, :]

    by_rows(0, count, 64, add_probe)
    swap = start(partial.at[rows_at((1 - core) * half, half)], pair, partner)
    finish_columns = collect_columns(links, grad_ref, from_left, from_right, total, slots, PLANES, LAST_DIRECT_GRADIENTS)
    for side, buffer in (("up", from_up), ("down", from_down)):

        @pl.when(jnp.logical_not(links.has[side]))
        def _():
            for part, layer in PLANES:
                buffer[part, layer] = jnp.zeros((2, HALF, HALF), jnp.float32)

    swap.wait_recv()
    base = core * half

    def add_pair(index, carry):
        near = pl.ds(pl.multiple_of(index * 64, 64), 64)
        mine = rows_at(base + index * 64, 64)
        sums[mine, :] = partial[mine, :] + pair[near, :]
        return carry

    lax.fori_loop(0, half // 64, add_pair, 0)
    gathers = [swap]

    piece = half // 16
    plane_base = base + (z * 4 + x) * piece
    mine = rows_at(plane_base, piece)
    plane_peers = [device for device in peers[1:16]]
    line_peers = peers[16:]

    def spread_plane():
        items = []
        for k in range(1, 16):
            other = lax.rem(z * 4 + x + k, 16)
            source = sums.at[rows_at(base + other * piece, piece)]
            items.append(start(source, landings[0].at[k - 1], plane_peers[k - 1]))
        gathers.extend(items)
        return items

    def add_plane(items):
        for item in items:
            item.wait_recv()
        value = sums[mine, :]
        for k in range(15):
            value = value + landings[0][k]
        landings[1][y] = value

    def spread_line():
        items = [start(landings[1].at[y], landings[1].at[y], device) for device in line_peers]
        gathers.extend(items)
        return items

    def add_line(items):
        for item in items:
            item.wait_recv()
        gathered[mine, :] = (landings[1][0] + landings[1][1]) + (landings[1][2] + landings[1][3])

    def share_plane():
        items = [start(gathered.at[mine], gathered.at[mine], device) for device in plane_peers]
        gathers.extend(items)
        return items

    def await_all(items):
        for item in items:
            item.wait_recv()

    held, arrivals = {}, {}

    def issue(number):
        part, layer = PLANES[number // 2]
        block = number % 2
        up = links.send(total.at[part, layer, block, pl.ds(0, HALF)], from_down.at[part, layer, block], "up")
        down = links.send(total.at[part, layer, block, pl.ds(3 * HALF, HALF)], from_up.at[part, layer, block], "down")
        held[number] = [links.sent.pop(), links.sent.pop()]
        arrivals[number] = (up, down)

    def retire(number):
        for item, condition in held[number]:

            @pl.when(condition)
            def _():
                item.wait_send()

    def columns_in(index):
        finish_columns(index, 0)
        finish_columns(index, 1)

    items = spread_plane()
    columns_in(0)
    issue(0)
    issue(1)
    columns_in(1)
    retire(0)
    issue(2)
    retire(1)
    issue(3)
    add_plane(items)
    items = spread_line()
    columns_in(2)
    retire(2)
    issue(4)
    retire(3)
    issue(5)
    add_line(items)
    items = share_plane()
    columns_in(3)
    retire(4)
    issue(6)
    retire(5)
    issue(7)
    await_all(items)
    retire(6)
    retire(7)
    own_half = gathered.at[rows_at(base, half)]
    swap_back = start(own_half, own_half, partner)
    for number in range(2 * len(PLANES)):
        (part, layer), block = PLANES[number // 2], number % 2
        for arrived in arrivals[number]:
            arrived()
        lane = pl.ds(block * HALF, HALF)
        for begin, buffer in ((HALF, from_up), (SIDE, from_down)):
            for offset in range(0, HALF, 64):
                rows, near = pl.ds(begin + offset, 64), pl.ds(offset, 64)
                gradient = total[part, layer, block, rows, :] + buffer[part, layer, block, near, :]
                target = pl.ds(begin - HALF + offset, 64)
                object_ref[part, layer, target, lane] = ext_ref[part, layer, 1 + block, rows, :] - OBJECT_STEP * gradient
    swap_back.wait_recv()

    def finish_probe(rows):
        new_probe_ref[rows, :] = probe_ref[rows, :] - PROBE_STEP * gathered[rows, :]

    by_rows(0, count, 64, finish_probe)
    for item in gathers + [swap_back]:
        item.wait_send()
    links.finish()


def vmem_specs(count):
    return [pl.BlockSpec(memory_space=pltpu.VMEM)] * count


def comm_params(identity, limit):
    return pltpu.CompilerParams(collective_id=identity, has_side_effects=True, vmem_limit_bytes=limit << 20)


def semaphores(count):
    return [pltpu.SemaphoreType.DMA((count,)), pltpu.SemaphoreType.DMA((count,))]


def f32(*shape):
    return pltpu.VMEM(shape, jnp.float32)


EXTENDED = jax.ShapeDtypeStruct((2, 2, 4, 2 * SIDE, HALF), jnp.float32)


def first_exchange(tile, amplitudes, table, probe_modes):
    planes = amplitudes.shape[0]
    inputs = (tile, amplitudes, jnp.asarray(ORDER), jnp.asarray(ORDER.T), table, probe_modes)
    return pl.pallas_call(
        first_kernel,
        out_shape=(
            EXTENDED,
            jax.ShapeDtypeStruct((planes, SIDE, SIDE), jnp.float32),
            jax.ShapeDtypeStruct(table.shape, table.dtype),
            jax.ShapeDtypeStruct(probe_modes.shape, probe_modes.dtype),
        ),
        in_specs=[pl.BlockSpec(memory_space=pltpu.HBM)] * 6,
        out_specs=tuple(vmem_specs(4)),
        scratch_shapes=[
            f32(planes, SIDE, SIDE),
            pltpu.VMEM((SIDE, SIDE), jnp.bfloat16),
            pltpu.VMEM((SIDE, SIDE), jnp.bfloat16),
            f32(2, 3, 2, SIDE // 4, HALF),
            f32(2, 2, 3, 2, HALF // 4, HALF),
            pltpu.SemaphoreType.DMA((7,)),
            *semaphores(8 + 9 * 12),
        ],
        compiler_params=comm_params(0, 14),
    )(*[pltpu.with_memory_space_constraint(value, pltpu.HBM) for value in inputs])


def columns_buffers():
    return [f32(2, 2, 2 * SIDE, HALF), f32(2, 2, 2 * SIDE, HALF), f32(2, 2, 3, HALF, HALF)]


def middle_exchange(extended, gradient):
    return pl.pallas_call(
        middle_kernel,
        out_shape=EXTENDED,
        in_specs=vmem_specs(2),
        out_specs=vmem_specs(1)[0],
        scratch_shapes=[
            *columns_buffers(),
            f32(2, 2, 2, SIDE, HALF),
            f32(2, 2, 2, SIDE, HALF),
            f32(2, 2, 2, 2 * SIDE, HALF),
            f32(2, 2, 3, HALF, HALF),
            *semaphores(72 + 8 + 72),
        ],
        compiler_params=comm_params(1, 24),
    )(extended, gradient)


def last_exchange(extended, gradient, first_probe, second_probe, probe_modes):
    flat = (4 * SIDE, SIDE)
    new_object, new_probe = pl.pallas_call(
        last_kernel,
        out_shape=(
            jax.ShapeDtypeStruct((2, 2, SIDE, SIDE), jnp.float32),
            jax.ShapeDtypeStruct(flat, jnp.float32),
        ),
        in_specs=vmem_specs(5),
        out_specs=tuple(vmem_specs(2)),
        scratch_shapes=[
            *columns_buffers(),
            f32(2, 2, 2, HALF, HALF),
            f32(2, 2, 2, HALF, HALF),
            f32(2, 2, 2, 2 * SIDE, HALF),
            f32(*flat),
            f32(2 * SIDE, SIDE),
            [f32(15, 2 * SIDE // 16, SIDE), f32(4, 2 * SIDE // 16, SIDE)],
            f32(*flat),
            f32(*flat),
            *semaphores(72 + 16 + 2 + 33),
        ],
        compiler_params=comm_params(2, 26),
    )(extended, gradient, first_probe.reshape(flat), second_probe.reshape(flat), probe_modes.reshape(flat))
    return new_object, new_probe.reshape(probe_modes.shape)


def batch_kernel(
    batch, offset_ref, count_ref, ext_ref, probe_ref, amp_ref, table_ref, grad_ref, probe_grad_ref,
    obj, psi, right_a, right_b, yield_a, yield_b, left_a, left_b, out_a, out_b,
):
    lanes = lax.broadcasted_iota(jnp.int32, (CHUNK, HALF), 1)
    lo, hi = pl.ds(0, HALF), pl.ds(HALF, HALF)

    def chunks(total, body):
        def step(index, carry):
            body(pl.multiple_of(index * CHUNK, CHUNK))
            return carry

        lax.fori_loop(0, total // CHUNK, step, 0, unroll=True)

    def bf(value):
        return value.astype(jnp.bfloat16)

    def zero_grad(row):
        for part in range(2):
            for layer in range(2):
                for block in range(4):
                    grad_ref[part, layer, block, pl.ds(row, CHUNK), :] = jnp.zeros((CHUNK, HALF), jnp.float32)

    chunks(2 * SIDE, zero_grad)

    def zero_probe(row):
        for part in range(2):
            for mode in range(MODES):
                probe_grad_ref[part, mode, pl.ds(row, CHUNK), :] = jnp.zeros((CHUNK, SIDE), jnp.float32)

    chunks(SIDE, zero_probe)

    def right(table_a, table_b):
        yield_a[...] = dot(right_a[...], table_ref[table_a])
        yield_b[...] = dot(right_b[...], table_ref[table_b])

    def left(table_a, table_b):
        out_a[...] = dot(table_ref[table_a], left_a[...])
        out_b[...] = dot(table_ref[table_b], left_b[...])

    def put_split(mode, row, re, im):
        at = pl.ds(mode * SIDE + row, CHUNK)
        right_a[at, lo] = bf(re[0] + re[1])
        right_a[at, hi] = bf(im[0] + im[1])
        right_b[at, lo] = bf(re[0] - re[1])
        right_b[at, hi] = bf(im[0] - im[1])

    def columns(ref, mode):
        return pl.ds(mode * SIDE, HALF), pl.ds(mode * SIDE + HALF, HALF)

    def middle_spread(row):
        for mode in range(MODES):
            here = columns(left_a, mode)
            for part, lane in ((0, lo), (1, hi)):
                top = pl.ds(mode * SIDE + row, CHUNK)
                low = pl.ds(mode * SIDE + HALF + row, CHUNK)
                at, ab = yield_a[top, lane], yield_a[low, lane]
                bt, bb = yield_b[top, lane], yield_b[low, lane]
                to = pl.ds(part * HALF + row, CHUNK)
                a_sum, a_dif = at + ab, at - ab
                b_sum, b_dif = bt + bb, bt - bb
                left_a[to, here[0]] = bf(a_sum + b_sum)
                left_a[to, here[1]] = bf(a_sum - b_sum)
                left_b[to, here[0]] = bf(a_dif + b_dif)
                left_b[to, here[1]] = bf(a_dif - b_dif)

    def middle_forward(row):
        for mode in range(MODES):
            here = columns(left_a, mode)
            for part, lane in ((0, lo), (1, hi)):
                top = pl.ds(mode * SIDE + row, CHUNK)
                low = pl.ds(mode * SIDE + HALF + row, CHUNK)
                to = pl.ds(part * HALF + row, CHUNK)
                for source, at in ((yield_a, here[0]), (yield_b, here[1])):
                    upper, lower = source[top, lane], source[low, lane]
                    left_a[to, at] = bf(upper + lower)
                    left_b[to, at] = bf(upper - lower)

    def middle_backward(row):
        for mode in range(MODES):
            here = columns(left_a, mode)
            for part, lane in ((0, lo), (1, hi)):
                to = pl.ds(part * HALF + row, CHUNK)
                for base, target in ((0, left_a), (HALF, left_b)):
                    at = pl.ds(mode * SIDE + base + row, CHUNK)
                    even, odd = yield_a[at, lane], yield_b[at, lane]
                    target[to, here[0]] = bf(even + odd)
                    target[to, here[1]] = bf(even - odd)

    def joined(mode, row):
        result = []
        for sign in (1, -1):
            pair = []
            for part in range(2):
                at = pl.ds(part * HALF + row, CHUNK)
                halves = []
                for lane in columns(out_a, mode):
                    a, b = out_a[at, lane], out_b[at, lane]
                    halves.append(a + b if sign > 0 else a - b)
                pair.append(halves)
            result.append(pair)
        return result

    def pair_of(ref, first, second, row):
        return [ref[first, second, pl.ds(row, CHUNK), lane] for lane in (lo, hi)]

    def one_slot(slot, carry):
        start_row = offset_ref[batch, 0, slot, 0]
        start_col = offset_ref[batch, 1, slot, 0]
        base = start_col // HALF
        shift = start_col % HALF
        take_left = lanes < HALF - shift
        put_right = lanes >= shift
        back = lax.rem(HALF - shift, HALF)

        def fetch(row):
            for part in range(2):
                for layer in range(2):
                    at = pl.ds(start_row + row, CHUNK)
                    turned = [pltpu.roll(ext_ref[part, layer, base + k, at, :], back, 1) for k in range(3)]
                    obj[part, layer, pl.ds(row, CHUNK), lo] = jnp.where(take_left, turned[0], turned[1])
                    obj[part, layer, pl.ds(row, CHUNK), hi] = jnp.where(take_left, turned[1], turned[2])

        chunks(SIDE, fetch)

        def enter(row):
            o_re, o_im = pair_of(obj, 0, 0, row), pair_of(obj, 1, 0, row)
            for mode in range(MODES):
                p_re, p_im = pair_of(probe_ref, 0, mode, row), pair_of(probe_ref, 1, mode, row)
                re = [p_re[k] * o_re[k] - p_im[k] * o_im[k] for k in range(2)]
                im = [p_re[k] * o_im[k] + p_im[k] * o_re[k] for k in range(2)]
                put_split(mode, row, re, im)

        chunks(SIDE, enter)
        right(SUM_R, DIF_R)
        chunks(HALF, middle_spread)
        left(SUM_L, DIF_L)

        def second_slice(row):
            for side in range(2):
                at = row + side * HALF
                o_re, o_im = pair_of(obj, 0, 1, at), pair_of(obj, 1, 1, at)
                for mode in range(MODES):
                    w_re, w_im = joined(mode, row)[side]
                    for k, lane in ((0, lo), (1, hi)):
                        psi[0, mode, pl.ds(at, CHUNK), lane] = w_re[k]
                        psi[1, mode, pl.ds(at, CHUNK), lane] = w_im[k]
                    re = [w_re[k] * o_re[k] - w_im[k] * o_im[k] for k in range(2)]
                    im = [w_re[k] * o_im[k] + w_im[k] * o_re[k] for k in range(2)]
                    put_split(mode, at, re, im)

        chunks(HALF, second_slice)
        right(EVEN_R, ODD_R)
        chunks(HALF, middle_forward)
        left(EVEN_L, ODD_L)

        def compare(row):
            for base_row, source in ((0, out_a), (HALF, out_b)):
                waves = []
                for mode in range(MODES):
                    here = columns(source, mode)
                    re = [source[pl.ds(row, CHUNK), lane] for lane in here]
                    im = [source[pl.ds(HALF + row, CHUNK), lane] for lane in here]
                    waves.append((re, im))
                for k, lane in ((0, lo), (1, hi)):
                    intensity = waves[0][0][k] * waves[0][0][k] + waves[0][1][k] * waves[0][1][k]
                    for re, im in waves[1:]:
                        intensity = intensity + (re[k] * re[k] + im[k] * im[k])
                    amplitude = amp_ref[batch * (amp_ref.shape[0] // 2) + slot, pl.ds(base_row + row, CHUNK), lane]
                    ratio = 1.0 - amplitude * lax.rsqrt(jnp.maximum(intensity, AMPLITUDE_FLOOR**2))
                    target = right_a if k == 0 else right_b
                    for mode, (re, im) in enumerate(waves):
                        at = pl.ds(mode * SIDE + base_row + row, CHUNK)
                        target[at, lo] = bf(re[k] * ratio)
                        target[at, hi] = bf(im[k] * ratio)

        chunks(HALF, compare)
        right(EVEN_L, ODD_L)
        chunks(HALF, middle_backward)
        left(EVEN_R, ODD_R)

        def add_term(part, layer, row, term):
            turned = [pltpu.roll(value, shift, 1) for value in term]
            zero = jnp.zeros_like(turned[0])
            spread = [
                jnp.where(put_right, turned[0], zero),
                jnp.where(put_right, turned[1], turned[0]),
                jnp.where(put_right, zero, turned[1]),
            ]
            at = pl.ds(start_row + row, CHUNK)
            for k in range(3):
                grad_ref[part, layer, base + k, at, :] = grad_ref[part, layer, base + k, at, :] + spread[k]

        def object_term(layer, row, waves, backs):
            re, im = [], []
            for k in range(2):
                re.append(sum(w[0][k] * b[0][k] + w[1][k] * b[1][k] for w, b in zip(waves, backs)))
                im.append(sum(w[0][k] * b[1][k] - w[1][k] * b[0][k] for w, b in zip(waves, backs)))
            add_term(0, layer, row, re)
            add_term(1, layer, row, im)

        def last_back(row):
            for side in range(2):
                at = row + side * HALF
                backs = [joined(mode, row)[side] for mode in range(MODES)]
                waves = [(pair_of(psi, 0, mode, at), pair_of(psi, 1, mode, at)) for mode in range(MODES)]
                o_re, o_im = pair_of(obj, 0, 1, at), pair_of(obj, 1, 1, at)
                for mode, (b_re, b_im) in enumerate(backs):
                    re = [o_re[k] * b_re[k] + o_im[k] * b_im[k] for k in range(2)]
                    im = [o_re[k] * b_im[k] - o_im[k] * b_re[k] for k in range(2)]
                    put_split(mode, at, re, im)
                object_term(1, at, waves, backs)

        chunks(HALF, last_back)
        right(SUM_L, DIF_L)
        chunks(HALF, middle_spread)
        left(SUM_R, DIF_R)

        def first_back(row):
            for side in range(2):
                at = row + side * HALF
                backs = [joined(mode, row)[side] for mode in range(MODES)]
                waves = [(pair_of(probe_ref, 0, mode, at), pair_of(probe_ref, 1, mode, at)) for mode in range(MODES)]
                o_re, o_im = pair_of(obj, 0, 0, at), pair_of(obj, 1, 0, at)
                for mode, (b_re, b_im) in enumerate(backs):
                    for k, lane in ((0, lo), (1, hi)):
                        spot = (mode, pl.ds(at, CHUNK), lane)
                        probe_grad_ref[(0, *spot)] = probe_grad_ref[(0, *spot)] + (o_re[k] * b_re[k] + o_im[k] * b_im[k])
                        probe_grad_ref[(1, *spot)] = probe_grad_ref[(1, *spot)] + (o_re[k] * b_im[k] - o_im[k] * b_re[k])
                object_term(0, at, waves, backs)

        chunks(HALF, first_back)
        return carry

    lax.fori_loop(0, count_ref[batch, 0, 0], one_slot, 0)


def batch_terms(batch, extended, probe_modes, amplitudes, offsets, counts, table):
    vmem = pl.BlockSpec(memory_space=pltpu.VMEM)
    smem = pl.BlockSpec(memory_space=pltpu.SMEM)
    field = pltpu.VMEM((2, 2, SIDE, SIDE), jnp.float32)
    return pl.pallas_call(
        functools.partial(batch_kernel, batch),
        out_shape=(
            jax.ShapeDtypeStruct((2, 2, 4, 2 * SIDE, HALF), jnp.float32),
            jax.ShapeDtypeStruct((2, MODES, SIDE, SIDE), jnp.float32),
        ),
        in_specs=[smem, smem, vmem, vmem, vmem, vmem],
        out_specs=(vmem, vmem),
        scratch_shapes=[
            field,
            field,
            pltpu.VMEM((MODES * SIDE, SIDE), jnp.bfloat16),
            pltpu.VMEM((MODES * SIDE, SIDE), jnp.bfloat16),
            pltpu.VMEM((MODES * SIDE, SIDE), jnp.float32),
            pltpu.VMEM((MODES * SIDE, SIDE), jnp.float32),
            pltpu.VMEM((SIDE, MODES * SIDE), jnp.bfloat16),
            pltpu.VMEM((SIDE, MODES * SIDE), jnp.bfloat16),
            pltpu.VMEM((SIDE, MODES * SIDE), jnp.float32),
            pltpu.VMEM((SIDE, MODES * SIDE), jnp.float32),
        ],
        compiler_params=pltpu.CompilerParams(vmem_limit_bytes=26 << 20),
        cost_estimate=pl.CostEstimate(flops=3 * 64 * SIDE**3, bytes_accessed=12 << 20, transcendentals=0),
    )(offsets, counts, extended, probe_modes, amplitudes, table)


def body(object_field, probe_modes, amplitudes, offsets, counts):
    batches, slots = amplitudes.shape[:2]
    table = jnp.asarray(TABLES)
    extended, ordered, table, probe_modes = first_exchange(
        object_field, amplitudes.reshape(batches * slots, SIDE, SIDE), table, probe_modes
    )
    terms = lambda cells, batch: batch_terms(batch, cells, probe_modes, ordered, offsets, counts, table)
    gradient, first_probe = terms(extended, 0)
    extended = middle_exchange(extended, gradient)
    gradient, second_probe = terms(extended, 1)
    return last_exchange(extended, gradient, first_probe, second_probe, probe_modes)


def solution(mesh):
    return jax.shard_map(
        body,
        mesh=mesh,
        in_specs=(
            P(None, None, "row", "col"),
            P(),
            P(None, "row", "col", None, None),
            P(None, None, "row", "col"),
            P(None, "row", "col"),
        ),
        out_specs=(P(None, None, "row", "col"), P()),
        check_vma=False,
    )
```

```python
import functools
import math

import jax
import jax.numpy as jnp
import numpy as np
from jax import lax
from jax.experimental import pallas as pl
from jax.experimental.pallas import tpu as pltpu
from jax.sharding import PartitionSpec as P

AMPLITUDE_FLOOR = 0.5
OBJECT_STEP = 0.25
PROBE_STEP = 0.125
SIDE = 256
HALF = SIDE // 2
MODES = 2
CHUNK = 16
IN_FLIGHT = 2
RELAYED_CORNER_LAYERS = 1
MIDDLE_DIRECT_GRADIENTS = (0,)
MIDDLE_DIRECT_HALOS = (3,)
LAST_DIRECT_GRADIENTS = (0,)
MESH = pl.DeviceIdType.MESH
SIDES = ("up", "down", "left", "right")
OPPOSITE = {"up": "down", "down": "up", "left": "right", "right": "left"}


def real_form(table):
    re, im = table.real, table.imag
    return np.block([[re, im], [-im, re]]).astype(jnp.bfloat16)


def make_tables():
    index = np.arange(SIDE)
    angles = (index[:, None] * index[None, :] % SIDE).astype(np.float32) * np.float32(2.0 * math.pi / SIDE)
    scale = np.float32(1.0 / math.sqrt(SIDE))
    rounded = lambda v: (v * scale).astype(jnp.bfloat16).astype(np.float64)
    forward = rounded(np.cos(angles)) - 1j * rounded(np.sin(angles))
    frequency = np.where(index < HALF, index, index - SIDE).astype(np.float64)
    chirp = np.exp(-2j * math.pi * (frequency * frequency % (16 * SIDE)) / (16 * SIDE))
    spread = (forward.conj() * chirp[None, :]) @ forward
    same = 0.25 * (spread[:HALF, :HALF] + spread[HALF:, HALF:] + spread[:HALF, HALF:] + spread[HALF:, :HALF])
    other = 0.25 * (spread[:HALF, :HALF] + spread[HALF:, HALF:] - spread[:HALF, HALF:] - spread[HALF:, :HALF])
    same = 0.5 * (same + same.T)
    other = 0.5 * (other + other.T)
    even = forward[:HALF, 0::2]
    odd = forward[:HALF, 1::2]
    rows = []
    for table in (same, other, even, odd):
        matrix = real_form(table)
        rows += [matrix, np.ascontiguousarray(matrix.T)]
    order = np.zeros((SIDE, SIDE), np.float32)
    order[0::2, :HALF] = np.eye(HALF)
    order[1::2, HALF:] = np.eye(HALF)
    return np.stack(rows), order.astype(jnp.bfloat16)


TABLES, ORDER = make_tables()
(SUM_R, SUM_L, DIF_R, DIF_L, EVEN_R, EVEN_L, ODD_R, ODD_L) = range(8)


def dot(left, right):
    return jnp.dot(left, right, preferred_element_type=jnp.float32)


def three_parts(value):
    high = value.astype(jnp.bfloat16)
    rest = value - high.astype(jnp.float32)
    middle = rest.astype(jnp.bfloat16)
    return high, middle, (rest - middle.astype(jnp.float32)).astype(jnp.bfloat16)


def reorder_plane(plane, order, turn):
    high, middle, low = [dot(part, order) for part in three_parts(plane)]
    high, middle, low = [dot(turn, part) for part in three_parts(high + (middle + low))]
    return high + (middle + low)


class Links:
    def __init__(self, send_sems, recv_sems):
        self.row, self.col = lax.axis_index("row"), lax.axis_index("col")
        rows, cols = lax.axis_size("row"), lax.axis_size("col")
        self.has = {
            "up": self.row > 0,
            "down": self.row < rows - 1,
            "left": self.col > 0,
            "right": self.col < cols - 1,
        }
        self.at = {
            "up": (self.row - 1, self.col),
            "down": (self.row + 1, self.col),
            "left": (self.row, self.col - 1),
            "right": (self.row, self.col + 1),
        }
        middle, last = cols // 2, cols - 1
        relays = {"right": (last, last - 2, last - 4), "left": (0, 2, 4)}
        self.crosses = {"right": self.col == middle - 1, "left": self.col == middle}
        self.beyond = {"right": (self.row, middle), "left": (self.row, middle - 1)}
        self.relay = {side: [(self.row, col) for col in relays[side]] for side in relays}
        self.relays = {side: [self.col == col for col in relays[side]] for side in relays}
        self.send_sems, self.recv_sems = send_sems, recv_sems
        self.used = 0
        self.sent = []

    def greet(self, peers=()):
        barrier = pltpu.get_barrier_semaphore()
        for side in SIDES:

            @pl.when(self.has[side])
            def _():
                pl.semaphore_signal(barrier, inc=1, device_id=self.at[side], device_id_type=MESH)

        inner = jnp.logical_or(self.crosses["left"], self.crosses["right"])
        outer = functools.reduce(jnp.logical_or, self.relays["left"] + self.relays["right"])
        extra = 6 * inner.astype(jnp.int32) + 2 * outer.astype(jnp.int32)
        for condition, devices in (
            (inner, self.relay["left"] + self.relay["right"]),
            (outer, list(self.beyond.values())),
        ):

            @pl.when(condition)
            def _():
                for device in devices:
                    pl.semaphore_signal(barrier, inc=1, device_id=device, device_id_type=MESH)

        for peer in peers:
            pl.semaphore_signal(barrier, inc=1, device_id=peer, device_id_type=MESH)
        pl.semaphore_wait(barrier, len(peers) + extra + sum(self.has[side].astype(jnp.int32) for side in SIDES))

    def copy(self, source, target, device):
        index = self.used
        self.used += 1
        return pltpu.make_async_remote_copy(
            src_ref=source,
            dst_ref=target,
            send_sem=self.send_sems.at[index],
            recv_sem=self.recv_sems.at[index],
            device_id=device,
            device_id_type=MESH,
        )

    def send(self, source, target, side, also=None):
        item = self.copy(source, target, self.at[side])
        condition = self.has[side] if also is None else jnp.logical_and(self.has[side], also)

        @pl.when(condition)
        def _():
            item.start()

        self.sent.append((item, condition))
        source_side = self.has[OPPOSITE[side]]
        arrives = source_side if also is None else jnp.logical_and(source_side, also)

        def arrived():
            @pl.when(arrives)
            def _():
                item.wait_recv()

        return arrived

    def send_straight(self, source, target, side, also):
        rows = source.shape[-2]
        lead = (slice(None),) * (len(source.shape) - 2)
        halves = [(*lead, pl.ds(k * rows // 2, rows // 2)) for k in range(2)]
        waits = [self.send(source.at[at], target.at[at], side, also) for at in halves]
        return (lambda: None), (lambda half: waits[half]())

    def send_columns(self, source, target, side, slots, also=None, relay=True):
        if not relay:
            return self.send_straight(source, target, side, also)
        rows = source.shape[-2]
        lead = (slice(None),) * (len(source.shape) - 2)
        halves = [(*lead, pl.ds(k * rows // 2, rows // 2)) for k in range(2)]
        quarters = [(*lead, pl.ds(k * rows // 4, rows // 4)) for k in range(4)]
        both = lambda a: a if also is None else jnp.logical_and(a, also)
        crosses = self.crosses[side]
        direct = both(jnp.logical_and(self.has[side], jnp.logical_not(crosses)))
        whole = [(self.copy(source.at[at], target.at[at], self.at[side]), direct) for at in halves]
        first = self.copy(source.at[quarters[0]], target.at[quarters[0]], self.at[side])
        detours, onwards = [], []
        for k in range(3):
            at = quarters[k + 1]
            detours.append(self.copy(source.at[at], slots.at[k], self.relay[side][k]))
            onwards.append(self.copy(slots.at[k], target.at[at], self.beyond[side]))
        going = [(item, both(crosses)) for item in [*detours, first]] + whole
        for item, condition in going:

            @pl.when(condition)
            def _():
                item.start()

        relays = [both(here) for here in self.relays[side]]
        self.sent += going + list(zip(onwards, relays))
        receives_parts = self.crosses[OPPOSITE[side]]
        receives_whole = both(jnp.logical_and(self.has[OPPOSITE[side]], jnp.logical_not(receives_parts)))
        receives_parts = both(receives_parts)

        def forward():
            for detour, onward, here in zip(detours, onwards, relays):

                @pl.when(here)
                def _():
                    detour.wait_recv()
                    onward.start()

        def arrived(half):
            @pl.when(receives_whole)
            def _():
                whole[half][0].wait_recv()

            @pl.when(receives_parts)
            def _():
                for item in (first, onwards[0]) if half == 0 else onwards[1:]:
                    item.wait_recv()

        return forward, arrived

    def finish(self):
        for item, condition in self.sent:

            @pl.when(condition)
            def _():
                item.wait_send()


def by_rows(start, stop, step, body):
    def one(index, carry):
        body(pl.ds(pl.multiple_of(start + index * step, 8), step))
        return carry

    lax.fori_loop(0, (stop - start) // step, one, 0)


def first_kernel(
    tile_ref, amp_ref, order_ref, turn_ref, table_ref, probe_ref, ext_ref, ordered_ref, table_out, probe_out,
    planes, order, turn, tile_slots, corner_slots, local_sems, send_sems, recv_sems,
):
    links = Links(send_sems, recv_sems)
    upper, lower, own = pl.ds(0, HALF), pl.ds(3 * HALF, HALF), pl.ds(HALF, SIDE)
    local = [
        pltpu.make_async_copy(amp_ref, planes, local_sems.at[0]),
        pltpu.make_async_copy(order_ref, order, local_sems.at[1]),
        pltpu.make_async_copy(turn_ref, turn, local_sems.at[2]),
    ]
    inner = [
        pltpu.make_async_copy(
            tile_ref.at[:, :, :, pl.ds(block * HALF, HALF)], ext_ref.at[:, :, 1 + block, own], local_sems.at[3 + block]
        )
        for block in range(2)
    ]
    extra = [
        pltpu.make_async_copy(table_ref, table_out, local_sems.at[5]),
        pltpu.make_async_copy(probe_ref, probe_out, local_sems.at[6]),
    ]
    for item in local + inner + extra:
        item.start()
    links.greet()
    waits, col_waits, corner_waits = [], [], []
    for layer in range(2):
        for side, start, block in (("left", 0, 3), ("right", HALF, 0)):
            col_waits.append(
                links.send_columns(
                    tile_ref.at[:, layer, :, pl.ds(start, HALF)],
                    ext_ref.at[:, layer, block, own],
                    side,
                    tile_slots.at[layer],
                )
            )
    for layer in range(2):
        arrivals = []
        for block in range(2):
            lane = pl.ds(block * HALF, HALF)
            arrivals.append(
                links.send(tile_ref.at[:, layer, pl.ds(0, HALF), lane], ext_ref.at[:, layer, 1 + block, lower], "up")
            )
            arrivals.append(
                links.send(tile_ref.at[:, layer, pl.ds(HALF, HALF), lane], ext_ref.at[:, layer, 1 + block, upper], "down")
            )
        waits.append(arrivals)

    def clear(side, blocks, rows):
        @pl.when(jnp.logical_not(links.has[side]))
        def _():
            for part, layer in PLANES:
                for block in blocks:
                    ext_ref[part, layer, block, rows, :] = jnp.zeros((rows.size, HALF), jnp.float32)

    clear("up", (1, 2), upper)
    clear("down", (1, 2), lower)
    clear("left", (0,), own)
    clear("right", (3,), own)
    for rows, side in ((upper, "up"), (lower, "down")):
        for block, other in ((0, "left"), (3, "right")):

            @pl.when(jnp.logical_not(jnp.logical_and(links.has[side], links.has[other])))
            def _():
                for part, layer in PLANES:
                    ext_ref[part, layer, block, rows, :] = jnp.zeros((HALF, HALF), jnp.float32)

    for item in local:
        item.wait()

    def one_plane(index, carry):
        ordered_ref[index] = reorder_plane(planes[index], order[...], turn[...])
        return carry

    lax.fori_loop(0, planes.shape[0], one_plane, 0)
    for forward, _ in col_waits:
        forward()
    for layer in range(2):
        for arrived in waits[layer]:
            arrived()
        for number, (rows, side) in enumerate(((upper, "up"), (lower, "down"))):
            for block, to, target in ((1, "left", 3), (2, "right", 0)):
                corner_waits.append(
                    links.send_columns(
                        ext_ref.at[:, layer, block, rows],
                        ext_ref.at[:, layer, target, rows],
                        to,
                        corner_slots.at[layer, number],
                        also=links.has[side],
                        relay=layer < RELAYED_CORNER_LAYERS,
                    )
                )
    for forward, _ in corner_waits:
        forward()
    for item in inner + extra:
        item.wait()
    for _, arrived in col_waits + corner_waits:
        for half in range(2):
            arrived(half)
    links.finish()


PLANES = [(part, layer) for layer in range(2) for part in range(2)]


def collect_columns(links, grad_ref, from_left, from_right, total, slots, order, straight):
    for side, buffer in (("left", from_left), ("right", from_right)):

        @pl.when(jnp.logical_not(links.has[side]))
        def _():
            for part, layer in order:
                buffer[part, layer] = jnp.zeros((2 * SIDE, HALF), jnp.float32)

    arrivals = []
    for number, (part, layer) in enumerate(order):
        relay = number not in straight
        arrivals.append(
            (
                links.send_columns(grad_ref.at[part, layer, 0], from_right.at[part, layer], "left", slots.at[part, layer], relay=relay),
                links.send_columns(grad_ref.at[part, layer, 3], from_left.at[part, layer], "right", slots.at[part, layer], relay=relay),
            )
        )

    def finish(index, half):
        part, layer = order[index]
        for forward, arrived in arrivals[index]:
            if half == 0:
                forward()
            arrived(half)

        def add(rows):
            total[part, layer, 0, rows, :] = grad_ref[part, layer, 1, rows, :] + from_left[part, layer, rows, :]
            total[part, layer, 1, rows, :] = grad_ref[part, layer, 2, rows, :] + from_right[part, layer, rows, :]

        by_rows(half * SIDE, (half + 1) * SIDE, 64, add)

    return finish


def middle_kernel(
    ext_ref, grad_ref, out_ref, from_left, from_right, slots, from_up, from_down, total, halo_slots, send_sems, recv_sems
):
    links = Links(send_sems, recv_sems)
    links.greet()
    finish_columns = collect_columns(links, grad_ref, from_left, from_right, total, slots, PLANES, MIDDLE_DIRECT_GRADIENTS)
    for side, buffer in (("up", from_up), ("down", from_down)):

        @pl.when(jnp.logical_not(links.has[side]))
        def _():
            for part, layer in PLANES:
                buffer[part, layer] = jnp.zeros((2, SIDE, HALF), jnp.float32)

    for side, block in (("left", 0), ("right", 3)):

        @pl.when(jnp.logical_not(links.has[side]))
        def _():
            for part, layer in PLANES:
                out_ref[part, layer, block] = jnp.zeros((2 * SIDE, HALF), jnp.float32)

    step_up = jnp.where(links.has["up"], OBJECT_STEP, 0.0).astype(jnp.float32)
    step_down = jnp.where(links.has["down"], OBJECT_STEP, 0.0).astype(jnp.float32)
    held, arrivals, halos = {}, {}, []
    pieces = 2 * len(PLANES)

    def issue(number):
        (part, layer), block = PLANES[number // 2], number % 2
        if block == 0:
            finish_columns(number // 2, 0)
        up = links.send(total.at[part, layer, block, pl.ds(0, SIDE)], from_down.at[part, layer, block], "up")
        if block == 0:
            finish_columns(number // 2, 1)
        down = links.send(total.at[part, layer, block, pl.ds(SIDE, SIDE)], from_up.at[part, layer, block], "down")
        held[number] = [links.sent.pop(), links.sent.pop()]
        arrivals[number] = (up, down)

    def retire(number):
        for item, condition in held[number]:

            @pl.when(condition)
            def _():
                item.wait_send()

    for number in range(IN_FLIGHT):
        issue(number)
    for number in range(pieces):
        (part, layer), block = PLANES[number // 2], number % 2
        for arrived in arrivals[number]:
            arrived()
        retire(number)
        if number + IN_FLIGHT < pieces:
            issue(number + IN_FLIGHT)
        for start, buffer, offset, step in (
            (0, from_up, 0, step_up),
            (HALF, from_up, 0, OBJECT_STEP),
            (SIDE, from_down, SIDE, OBJECT_STEP),
            (3 * HALF, from_down, SIDE, step_down),
        ):
            for row in range(start, start + HALF, 64):
                rows, near = pl.ds(row, 64), pl.ds(row - offset, 64)
                gradient = total[part, layer, block, rows, :] + buffer[part, layer, block, near, :]
                out_ref[part, layer, 1 + block, rows, :] = ext_ref[part, layer, 1 + block, rows, :] - step * gradient
        side, target = (("left", 3), ("right", 0))[block]
        halos.append(
            links.send_columns(
                out_ref.at[part, layer, 1 + block],
                out_ref.at[part, layer, target],
                side,
                halo_slots.at[part, layer],
                relay=number // 2 not in MIDDLE_DIRECT_HALOS,
            )
        )
        if number:
            halos[number - 1][0]()
    halos[-1][0]()
    for _, arrived in halos:
        for half in range(2):
            arrived(half)
    links.finish()


def last_kernel(
    ext_ref, grad_ref, first_probe_ref, second_probe_ref, probe_ref, object_ref, new_probe_ref,
    from_left, from_right, slots, from_up, from_down, total, partial, pair, landings, sums, gathered, send_sems, recv_sems,
):
    links = Links(send_sems, recv_sems)
    row, col = links.row, links.col
    core, x, y_low = lax.rem(col, 2), lax.rem(col // 2, 4), col // 8
    y_high, z = lax.rem(row, 2), row // 2
    y = y_high * 2 + y_low
    partner = (row, col + 1 - 2 * core)
    plane = lambda k: ((k // 4) * 2 + y_high, y_low * 8 + lax.rem(k, 4) * 2 + core)
    line = lambda k: (z * 2 + k // 2, lax.rem(k, 2) * 8 + x * 2 + core)
    groups = [(z * 4 + x, plane, 16), (y, line, 4)]
    peers = [partner]
    for place, device, members in groups:
        peers += [device(lax.rem(place + k, members)) for k in range(1, members)]
    links.greet(peers)
    count = 4 * SIDE
    half = count // 2

    def rows_at(start, size):
        return pl.ds(pl.multiple_of(start, 8), size)

    def start(source, target, device):
        item = links.copy(source, target, device)
        item.start()
        return item

    def add_probe(rows):
        partial[rows, :] = first_probe_ref[rows, :] + second_probe_ref[rows, :]

    by_rows(0, count, 64, add_probe)
    swap = start(partial.at[rows_at((1 - core) * half, half)], pair, partner)
    finish_columns = collect_columns(links, grad_ref, from_left, from_right, total, slots, PLANES, LAST_DIRECT_GRADIENTS)
    for side, buffer in (("up", from_up), ("down", from_down)):

        @pl.when(jnp.logical_not(links.has[side]))
        def _():
            for part, layer in PLANES:
                buffer[part, layer] = jnp.zeros((2, HALF, HALF), jnp.float32)

    swap.wait_recv()
    base = core * half

    def add_pair(index, carry):
        near = pl.ds(pl.multiple_of(index * 64, 64), 64)
        mine = rows_at(base + index * 64, 64)
        sums[mine, :] = partial[mine, :] + pair[near, :]
        return carry

    lax.fori_loop(0, half // 64, add_pair, 0)
    gathers = [swap]

    piece = half // 16
    plane_base = base + (z * 4 + x) * piece
    mine = rows_at(plane_base, piece)
    plane_peers = [device for device in peers[1:16]]
    line_peers = peers[16:]

    def spread_plane():
        items = []
        for k in range(1, 16):
            other = lax.rem(z * 4 + x + k, 16)
            source = sums.at[rows_at(base + other * piece, piece)]
            items.append(start(source, landings[0].at[k - 1], plane_peers[k - 1]))
        gathers.extend(items)
        return items

    def add_plane(items):
        for item in items:
            item.wait_recv()
        value = sums[mine, :]
        for k in range(15):
            value = value + landings[0][k]
        landings[1][y] = value

    def spread_line():
        items = [start(landings[1].at[y], landings[1].at[y], device) for device in line_peers]
        gathers.extend(items)
        return items

    def add_line(items):
        for item in items:
            item.wait_recv()
        gathered[mine, :] = (landings[1][0] + landings[1][1]) + (landings[1][2] + landings[1][3])

    def share_plane():
        items = [start(gathered.at[mine], gathered.at[mine], device) for device in plane_peers]
        gathers.extend(items)
        return items

    def await_all(items):
        for item in items:
            item.wait_recv()

    held, arrivals = {}, {}

    def issue(number):
        part, layer = PLANES[number // 2]
        block = number % 2
        up = links.send(total.at[part, layer, block, pl.ds(0, HALF)], from_down.at[part, layer, block], "up")
        down = links.send(total.at[part, layer, block, pl.ds(3 * HALF, HALF)], from_up.at[part, layer, block], "down")
        held[number] = [links.sent.pop(), links.sent.pop()]
        arrivals[number] = (up, down)

    def retire(number):
        for item, condition in held[number]:

            @pl.when(condition)
            def _():
                item.wait_send()

    def columns_in(index):
        finish_columns(index, 0)
        finish_columns(index, 1)

    items = spread_plane()
    columns_in(0)
    issue(0)
    issue(1)
    columns_in(1)
    retire(0)
    issue(2)
    retire(1)
    issue(3)
    add_plane(items)
    items = spread_line()
    columns_in(2)
    retire(2)
    issue(4)
    retire(3)
    issue(5)
    add_line(items)
    items = share_plane()
    columns_in(3)
    retire(4)
    issue(6)
    retire(5)
    issue(7)
    await_all(items)
    retire(6)
    retire(7)
    own_half = gathered.at[rows_at(base, half)]
    swap_back = start(own_half, own_half, partner)
    for number in range(2 * len(PLANES)):
        (part, layer), block = PLANES[number // 2], number % 2
        for arrived in arrivals[number]:
            arrived()
        lane = pl.ds(block * HALF, HALF)
        for begin, buffer in ((HALF, from_up), (SIDE, from_down)):
            for offset in range(0, HALF, 64):
                rows, near = pl.ds(begin + offset, 64), pl.ds(offset, 64)
                gradient = total[part, layer, block, rows, :] + buffer[part, layer, block, near, :]
                target = pl.ds(begin - HALF + offset, 64)
                object_ref[part, layer, target, lane] = ext_ref[part, layer, 1 + block, rows, :] - OBJECT_STEP * gradient
    swap_back.wait_recv()

    def finish_probe(rows):
        new_probe_ref[rows, :] = probe_ref[rows, :] - PROBE_STEP * gathered[rows, :]

    by_rows(0, count, 64, finish_probe)
    for item in gathers + [swap_back]:
        item.wait_send()
    links.finish()


def vmem_specs(count):
    return [pl.BlockSpec(memory_space=pltpu.VMEM)] * count


def comm_params(identity, limit):
    return pltpu.CompilerParams(collective_id=identity, has_side_effects=True, vmem_limit_bytes=limit << 20)


def semaphores(count):
    return [pltpu.SemaphoreType.DMA((count,)), pltpu.SemaphoreType.DMA((count,))]


def f32(*shape):
    return pltpu.VMEM(shape, jnp.float32)


EXTENDED = jax.ShapeDtypeStruct((2, 2, 4, 2 * SIDE, HALF), jnp.float32)


def first_exchange(tile, amplitudes, table, probe_modes):
    planes = amplitudes.shape[0]
    inputs = (tile, amplitudes, jnp.asarray(ORDER), jnp.asarray(ORDER.T), table, probe_modes)
    return pl.pallas_call(
        first_kernel,
        out_shape=(
            EXTENDED,
            jax.ShapeDtypeStruct((planes, SIDE, SIDE), jnp.float32),
            jax.ShapeDtypeStruct(table.shape, table.dtype),
            jax.ShapeDtypeStruct(probe_modes.shape, probe_modes.dtype),
        ),
        in_specs=[pl.BlockSpec(memory_space=pltpu.HBM)] * 6,
        out_specs=tuple(vmem_specs(4)),
        scratch_shapes=[
            f32(planes, SIDE, SIDE),
            pltpu.VMEM((SIDE, SIDE), jnp.bfloat16),
            pltpu.VMEM((SIDE, SIDE), jnp.bfloat16),
            f32(2, 3, 2, SIDE // 4, HALF),
            f32(2, 2, 3, 2, HALF // 4, HALF),
            pltpu.SemaphoreType.DMA((7,)),
            *semaphores(8 + 9 * 12),
        ],
        compiler_params=comm_params(0, 14),
    )(*[pltpu.with_memory_space_constraint(value, pltpu.HBM) for value in inputs])


def columns_buffers():
    return [f32(2, 2, 2 * SIDE, HALF), f32(2, 2, 2 * SIDE, HALF), f32(2, 2, 3, HALF, HALF)]


def middle_exchange(extended, gradient):
    return pl.pallas_call(
        middle_kernel,
        out_shape=EXTENDED,
        in_specs=vmem_specs(2),
        out_specs=vmem_specs(1)[0],
        scratch_shapes=[
            *columns_buffers(),
            f32(2, 2, 2, SIDE, HALF),
            f32(2, 2, 2, SIDE, HALF),
            f32(2, 2, 2, 2 * SIDE, HALF),
            f32(2, 2, 3, HALF, HALF),
            *semaphores(72 + 16 + 72),
        ],
        compiler_params=comm_params(1, 24),
    )(extended, gradient)


def last_exchange(extended, gradient, first_probe, second_probe, probe_modes):
    flat = (4 * SIDE, SIDE)
    new_object, new_probe = pl.pallas_call(
        last_kernel,
        out_shape=(
            jax.ShapeDtypeStruct((2, 2, SIDE, SIDE), jnp.float32),
            jax.ShapeDtypeStruct(flat, jnp.float32),
        ),
        in_specs=vmem_specs(5),
        out_specs=tuple(vmem_specs(2)),
        scratch_shapes=[
            *columns_buffers(),
            f32(2, 2, 2, HALF, HALF),
            f32(2, 2, 2, HALF, HALF),
            f32(2, 2, 2, 2 * SIDE, HALF),
            f32(*flat),
            f32(2 * SIDE, SIDE),
            [f32(15, 2 * SIDE // 16, SIDE), f32(4, 2 * SIDE // 16, SIDE)],
            f32(*flat),
            f32(*flat),
            *semaphores(72 + 16 + 2 + 33),
        ],
        compiler_params=comm_params(2, 26),
    )(extended, gradient, first_probe.reshape(flat), second_probe.reshape(flat), probe_modes.reshape(flat))
    return new_object, new_probe.reshape(probe_modes.shape)


def batch_kernel(
    batch, offset_ref, count_ref, ext_ref, probe_ref, amp_ref, table_ref, grad_ref, probe_grad_ref,
    obj, psi, right_a, right_b, yield_a, yield_b, left_a, left_b, out_a, out_b,
):
    lanes = lax.broadcasted_iota(jnp.int32, (CHUNK, HALF), 1)
    lo, hi = pl.ds(0, HALF), pl.ds(HALF, HALF)

    def chunks(total, body):
        def step(index, carry):
            body(pl.multiple_of(index * CHUNK, CHUNK))
            return carry

        lax.fori_loop(0, total // CHUNK, step, 0, unroll=True)

    def bf(value):
        return value.astype(jnp.bfloat16)

    def zero_grad(row):
        for part in range(2):
            for layer in range(2):
                for block in range(4):
                    grad_ref[part, layer, block, pl.ds(row, CHUNK), :] = jnp.zeros((CHUNK, HALF), jnp.float32)

    chunks(2 * SIDE, zero_grad)

    def zero_probe(row):
        for part in range(2):
            for mode in range(MODES):
                probe_grad_ref[part, mode, pl.ds(row, CHUNK), :] = jnp.zeros((CHUNK, SIDE), jnp.float32)

    chunks(SIDE, zero_probe)

    def right(table_a, table_b):
        yield_a[...] = dot(right_a[...], table_ref[table_a])
        yield_b[...] = dot(right_b[...], table_ref[table_b])

    def left(table_a, table_b):
        out_a[...] = dot(table_ref[table_a], left_a[...])
        out_b[...] = dot(table_ref[table_b], left_b[...])

    def put_split(mode, row, re, im):
        at = pl.ds(mode * SIDE + row, CHUNK)
        right_a[at, lo] = bf(re[0] + re[1])
        right_a[at, hi] = bf(im[0] + im[1])
        right_b[at, lo] = bf(re[0] - re[1])
        right_b[at, hi] = bf(im[0] - im[1])

    def columns(ref, mode):
        return pl.ds(mode * SIDE, HALF), pl.ds(mode * SIDE + HALF, HALF)

    def middle_spread(row):
        for mode in range(MODES):
            here = columns(left_a, mode)
            for part, lane in ((0, lo), (1, hi)):
                top = pl.ds(mode * SIDE + row, CHUNK)
                low = pl.ds(mode * SIDE + HALF + row, CHUNK)
                at, ab = yield_a[top, lane], yield_a[low, lane]
                bt, bb = yield_b[top, lane], yield_b[low, lane]
                to = pl.ds(part * HALF + row, CHUNK)
                a_sum, a_dif = at + ab, at - ab
                b_sum, b_dif = bt + bb, bt - bb
                left_a[to, here[0]] = bf(a_sum + b_sum)
                left_a[to, here[1]] = bf(a_sum - b_sum)
                left_b[to, here[0]] = bf(a_dif + b_dif)
                left_b[to, here[1]] = bf(a_dif - b_dif)

    def middle_forward(row):
        for mode in range(MODES):
            here = columns(left_a, mode)
            for part, lane in ((0, lo), (1, hi)):
                top = pl.ds(mode * SIDE + row, CHUNK)
                low = pl.ds(mode * SIDE + HALF + row, CHUNK)
                to = pl.ds(part * HALF + row, CHUNK)
                for source, at in ((yield_a, here[0]), (yield_b, here[1])):
                    upper, lower = source[top, lane], source[low, lane]
                    left_a[to, at] = bf(upper + lower)
                    left_b[to, at] = bf(upper - lower)

    def middle_backward(row):
        for mode in range(MODES):
            here = columns(left_a, mode)
            for part, lane in ((0, lo), (1, hi)):
                to = pl.ds(part * HALF + row, CHUNK)
                for base, target in ((0, left_a), (HALF, left_b)):
                    at = pl.ds(mode * SIDE + base + row, CHUNK)
                    even, odd = yield_a[at, lane], yield_b[at, lane]
                    target[to, here[0]] = bf(even + odd)
                    target[to, here[1]] = bf(even - odd)

    def joined(mode, row):
        result = []
        for sign in (1, -1):
            pair = []
            for part in range(2):
                at = pl.ds(part * HALF + row, CHUNK)
                halves = []
                for lane in columns(out_a, mode):
                    a, b = out_a[at, lane], out_b[at, lane]
                    halves.append(a + b if sign > 0 else a - b)
                pair.append(halves)
            result.append(pair)
        return result

    def pair_of(ref, first, second, row):
        return [ref[first, second, pl.ds(row, CHUNK), lane] for lane in (lo, hi)]

    def one_slot(slot, carry):
        start_row = offset_ref[batch, 0, slot, 0]
        start_col = offset_ref[batch, 1, slot, 0]
        base = start_col // HALF
        shift = start_col % HALF
        take_left = lanes < HALF - shift
        put_right = lanes >= shift
        back = lax.rem(HALF - shift, HALF)

        def fetch(row):
            for part in range(2):
                for layer in range(2):
                    at = pl.ds(start_row + row, CHUNK)
                    turned = [pltpu.roll(ext_ref[part, layer, base + k, at, :], back, 1) for k in range(3)]
                    obj[part, layer, pl.ds(row, CHUNK), lo] = jnp.where(take_left, turned[0], turned[1])
                    obj[part, layer, pl.ds(row, CHUNK), hi] = jnp.where(take_left, turned[1], turned[2])

        chunks(SIDE, fetch)

        def enter(row):
            o_re, o_im = pair_of(obj, 0, 0, row), pair_of(obj, 1, 0, row)
            for mode in range(MODES):
                p_re, p_im = pair_of(probe_ref, 0, mode, row), pair_of(probe_ref, 1, mode, row)
                re = [p_re[k] * o_re[k] - p_im[k] * o_im[k] for k in range(2)]
                im = [p_re[k] * o_im[k] + p_im[k] * o_re[k] for k in range(2)]
                put_split(mode, row, re, im)

        chunks(SIDE, enter)
        right(SUM_R, DIF_R)
        chunks(HALF, middle_spread)
        left(SUM_L, DIF_L)

        def second_slice(row):
            for side in range(2):
                at = row + side * HALF
                o_re, o_im = pair_of(obj, 0, 1, at), pair_of(obj, 1, 1, at)
                for mode in range(MODES):
                    w_re, w_im = joined(mode, row)[side]
                    for k, lane in ((0, lo), (1, hi)):
                        psi[0, mode, pl.ds(at, CHUNK), lane] = w_re[k]
                        psi[1, mode, pl.ds(at, CHUNK), lane] = w_im[k]
                    re = [w_re[k] * o_re[k] - w_im[k] * o_im[k] for k in range(2)]
                    im = [w_re[k] * o_im[k] + w_im[k] * o_re[k] for k in range(2)]
                    put_split(mode, at, re, im)

        chunks(HALF, second_slice)
        right(EVEN_R, ODD_R)
        chunks(HALF, middle_forward)
        left(EVEN_L, ODD_L)

        def compare(row):
            for base_row, source in ((0, out_a), (HALF, out_b)):
                waves = []
                for mode in range(MODES):
                    here = columns(source, mode)
                    re = [source[pl.ds(row, CHUNK), lane] for lane in here]
                    im = [source[pl.ds(HALF + row, CHUNK), lane] for lane in here]
                    waves.append((re, im))
                for k, lane in ((0, lo), (1, hi)):
                    intensity = waves[0][0][k] * waves[0][0][k] + waves[0][1][k] * waves[0][1][k]
                    for re, im in waves[1:]:
                        intensity = intensity + (re[k] * re[k] + im[k] * im[k])
                    amplitude = amp_ref[batch * (amp_ref.shape[0] // 2) + slot, pl.ds(base_row + row, CHUNK), lane]
                    ratio = 1.0 - amplitude * lax.rsqrt(jnp.maximum(intensity, AMPLITUDE_FLOOR**2))
                    target = right_a if k == 0 else right_b
                    for mode, (re, im) in enumerate(waves):
                        at = pl.ds(mode * SIDE + base_row + row, CHUNK)
                        target[at, lo] = bf(re[k] * ratio)
                        target[at, hi] = bf(im[k] * ratio)

        chunks(HALF, compare)
        right(EVEN_L, ODD_L)
        chunks(HALF, middle_backward)
        left(EVEN_R, ODD_R)

        def add_term(part, layer, row, term):
            turned = [pltpu.roll(value, shift, 1) for value in term]
            zero = jnp.zeros_like(turned[0])
            spread = [
                jnp.where(put_right, turned[0], zero),
                jnp.where(put_right, turned[1], turned[0]),
                jnp.where(put_right, zero, turned[1]),
            ]
            at = pl.ds(start_row + row, CHUNK)
            for k in range(3):
                grad_ref[part, layer, base + k, at, :] = grad_ref[part, layer, base + k, at, :] + spread[k]

        def object_term(layer, row, waves, backs):
            re, im = [], []
            for k in range(2):
                re.append(sum(w[0][k] * b[0][k] + w[1][k] * b[1][k] for w, b in zip(waves, backs)))
                im.append(sum(w[0][k] * b[1][k] - w[1][k] * b[0][k] for w, b in zip(waves, backs)))
            add_term(0, layer, row, re)
            add_term(1, layer, row, im)

        def last_back(row):
            for side in range(2):
                at = row + side * HALF
                backs = [joined(mode, row)[side] for mode in range(MODES)]
                waves = [(pair_of(psi, 0, mode, at), pair_of(psi, 1, mode, at)) for mode in range(MODES)]
                o_re, o_im = pair_of(obj, 0, 1, at), pair_of(obj, 1, 1, at)
                for mode, (b_re, b_im) in enumerate(backs):
                    re = [o_re[k] * b_re[k] + o_im[k] * b_im[k] for k in range(2)]
                    im = [o_re[k] * b_im[k] - o_im[k] * b_re[k] for k in range(2)]
                    put_split(mode, at, re, im)
                object_term(1, at, waves, backs)

        chunks(HALF, last_back)
        right(SUM_L, DIF_L)
        chunks(HALF, middle_spread)
        left(SUM_R, DIF_R)

        def first_back(row):
            for side in range(2):
                at = row + side * HALF
                backs = [joined(mode, row)[side] for mode in range(MODES)]
                waves = [(pair_of(probe_ref, 0, mode, at), pair_of(probe_ref, 1, mode, at)) for mode in range(MODES)]
                o_re, o_im = pair_of(obj, 0, 0, at), pair_of(obj, 1, 0, at)
                for mode, (b_re, b_im) in enumerate(backs):
                    for k, lane in ((0, lo), (1, hi)):
                        spot = (mode, pl.ds(at, CHUNK), lane)
                        probe_grad_ref[(0, *spot)] = probe_grad_ref[(0, *spot)] + (o_re[k] * b_re[k] + o_im[k] * b_im[k])
                        probe_grad_ref[(1, *spot)] = probe_grad_ref[(1, *spot)] + (o_re[k] * b_im[k] - o_im[k] * b_re[k])
                object_term(0, at, waves, backs)

        chunks(HALF, first_back)
        return carry

    lax.fori_loop(0, count_ref[batch, 0, 0], one_slot, 0)


def batch_terms(batch, extended, probe_modes, amplitudes, offsets, counts, table):
    vmem = pl.BlockSpec(memory_space=pltpu.VMEM)
    smem = pl.BlockSpec(memory_space=pltpu.SMEM)
    field = pltpu.VMEM((2, 2, SIDE, SIDE), jnp.float32)
    return pl.pallas_call(
        functools.partial(batch_kernel, batch),
        out_shape=(
            jax.ShapeDtypeStruct((2, 2, 4, 2 * SIDE, HALF), jnp.float32),
            jax.ShapeDtypeStruct((2, MODES, SIDE, SIDE), jnp.float32),
        ),
        in_specs=[smem, smem, vmem, vmem, vmem, vmem],
        out_specs=(vmem, vmem),
        scratch_shapes=[
            field,
            field,
            pltpu.VMEM((MODES * SIDE, SIDE), jnp.bfloat16),
            pltpu.VMEM((MODES * SIDE, SIDE), jnp.bfloat16),
            pltpu.VMEM((MODES * SIDE, SIDE), jnp.float32),
            pltpu.VMEM((MODES * SIDE, SIDE), jnp.float32),
            pltpu.VMEM((SIDE, MODES * SIDE), jnp.bfloat16),
            pltpu.VMEM((SIDE, MODES * SIDE), jnp.bfloat16),
            pltpu.VMEM((SIDE, MODES * SIDE), jnp.float32),
            pltpu.VMEM((SIDE, MODES * SIDE), jnp.float32),
        ],
        compiler_params=pltpu.CompilerParams(vmem_limit_bytes=26 << 20),
        cost_estimate=pl.CostEstimate(flops=3 * 64 * SIDE**3, bytes_accessed=12 << 20, transcendentals=0),
    )(offsets, counts, extended, probe_modes, amplitudes, table)


def body(object_field, probe_modes, amplitudes, offsets, counts):
    batches, slots = amplitudes.shape[:2]
    table = jnp.asarray(TABLES)
    extended, ordered, table, probe_modes = first_exchange(
        object_field, amplitudes.reshape(batches * slots, SIDE, SIDE), table, probe_modes
    )
    terms = lambda cells, batch: batch_terms(batch, cells, probe_modes, ordered, offsets, counts, table)
    gradient, first_probe = terms(extended, 0)
    extended = middle_exchange(extended, gradient)
    gradient, second_probe = terms(extended, 1)
    return last_exchange(extended, gradient, first_probe, second_probe, probe_modes)


def solution(mesh):
    return jax.shard_map(
        body,
        mesh=mesh,
        in_specs=(
            P(None, None, "row", "col"),
            P(),
            P(None, "row", "col", None, None),
            P(None, None, "row", "col"),
            P(None, "row", "col"),
        ),
        out_specs=(P(None, None, "row", "col"), P()),
        check_vma=False,
    )
```

```python
import functools
import math

import jax
import jax.numpy as jnp
import numpy as np
from jax import lax
from jax.experimental import pallas as pl
from jax.experimental.pallas import tpu as pltpu
from jax.sharding import PartitionSpec as P

AMPLITUDE_FLOOR = 0.5
OBJECT_STEP = 0.25
PROBE_STEP = 0.125
SIDE = 256
HALF = SIDE // 2
MODES = 2
CHUNK = 16
IN_FLIGHT = 2
RELAYED_CORNER_LAYERS = 1
MIDDLE_DIRECT_GRADIENTS = (0,)
MIDDLE_DIRECT_HALOS = (3,)
LAST_DIRECT_GRADIENTS = (0,)
MESH = pl.DeviceIdType.MESH
SIDES = ("up", "down", "left", "right")
OPPOSITE = {"up": "down", "down": "up", "left": "right", "right": "left"}


def real_form(table):
    re, im = table.real, table.imag
    return np.block([[re, im], [-im, re]]).astype(jnp.bfloat16)


def make_tables():
    index = np.arange(SIDE)
    angles = (index[:, None] * index[None, :] % SIDE).astype(np.float32) * np.float32(2.0 * math.pi / SIDE)
    scale = np.float32(1.0 / math.sqrt(SIDE))
    rounded = lambda v: (v * scale).astype(jnp.bfloat16).astype(np.float64)
    forward = rounded(np.cos(angles)) - 1j * rounded(np.sin(angles))
    frequency = np.where(index < HALF, index, index - SIDE).astype(np.float64)
    chirp = np.exp(-2j * math.pi * (frequency * frequency % (16 * SIDE)) / (16 * SIDE))
    spread = (forward.conj() * chirp[None, :]) @ forward
    same = 0.25 * (spread[:HALF, :HALF] + spread[HALF:, HALF:] + spread[:HALF, HALF:] + spread[HALF:, :HALF])
    other = 0.25 * (spread[:HALF, :HALF] + spread[HALF:, HALF:] - spread[:HALF, HALF:] - spread[HALF:, :HALF])
    same = 0.5 * (same + same.T)
    other = 0.5 * (other + other.T)
    even = forward[:HALF, 0::2]
    odd = forward[:HALF, 1::2]
    rows = []
    for table in (same, other, even, odd):
        matrix = real_form(table)
        rows += [matrix, np.ascontiguousarray(matrix.T)]
    order = np.zeros((SIDE, SIDE), np.float32)
    order[0::2, :HALF] = np.eye(HALF)
    order[1::2, HALF:] = np.eye(HALF)
    return np.stack(rows), order.astype(jnp.bfloat16)


TABLES, ORDER = make_tables()
(SUM_R, SUM_L, DIF_R, DIF_L, EVEN_R, EVEN_L, ODD_R, ODD_L) = range(8)


def dot(left, right):
    return jnp.dot(left, right, preferred_element_type=jnp.float32)


def three_parts(value):
    high = value.astype(jnp.bfloat16)
    rest = value - high.astype(jnp.float32)
    middle = rest.astype(jnp.bfloat16)
    return high, middle, (rest - middle.astype(jnp.float32)).astype(jnp.bfloat16)


def reorder_plane(plane, order, turn):
    high, middle, low = [dot(part, order) for part in three_parts(plane)]
    high, middle, low = [dot(turn, part) for part in three_parts(high + (middle + low))]
    return high + (middle + low)


class Links:
    def __init__(self, send_sems, recv_sems):
        self.row, self.col = lax.axis_index("row"), lax.axis_index("col")
        rows, cols = lax.axis_size("row"), lax.axis_size("col")
        self.has = {
            "up": self.row > 0,
            "down": self.row < rows - 1,
            "left": self.col > 0,
            "right": self.col < cols - 1,
        }
        self.at = {
            "up": (self.row - 1, self.col),
            "down": (self.row + 1, self.col),
            "left": (self.row, self.col - 1),
            "right": (self.row, self.col + 1),
        }
        middle, last = cols // 2, cols - 1
        relays = {"right": (last, last - 2, last - 4), "left": (0, 2, 4)}
        self.crosses = {"right": self.col == middle - 1, "left": self.col == middle}
        self.beyond = {"right": (self.row, middle), "left": (self.row, middle - 1)}
        self.relay = {side: [(self.row, col) for col in relays[side]] for side in relays}
        self.relays = {side: [self.col == col for col in relays[side]] for side in relays}
        self.send_sems, self.recv_sems = send_sems, recv_sems
        self.used = 0
        self.sent = []

    def greet(self, peers=()):
        barrier = pltpu.get_barrier_semaphore()
        for side in SIDES:

            @pl.when(self.has[side])
            def _():
                pl.semaphore_signal(barrier, inc=1, device_id=self.at[side], device_id_type=MESH)

        inner = jnp.logical_or(self.crosses["left"], self.crosses["right"])
        outer = functools.reduce(jnp.logical_or, self.relays["left"] + self.relays["right"])
        extra = 6 * inner.astype(jnp.int32) + 2 * outer.astype(jnp.int32)
        for condition, devices in (
            (inner, self.relay["left"] + self.relay["right"]),
            (outer, list(self.beyond.values())),
        ):

            @pl.when(condition)
            def _():
                for device in devices:
                    pl.semaphore_signal(barrier, inc=1, device_id=device, device_id_type=MESH)

        for peer in peers:
            pl.semaphore_signal(barrier, inc=1, device_id=peer, device_id_type=MESH)
        pl.semaphore_wait(barrier, len(peers) + extra + sum(self.has[side].astype(jnp.int32) for side in SIDES))

    def copy(self, source, target, device):
        index = self.used
        self.used += 1
        return pltpu.make_async_remote_copy(
            src_ref=source,
            dst_ref=target,
            send_sem=self.send_sems.at[index],
            recv_sem=self.recv_sems.at[index],
            device_id=device,
            device_id_type=MESH,
        )

    def send(self, source, target, side, also=None):
        item = self.copy(source, target, self.at[side])
        condition = self.has[side] if also is None else jnp.logical_and(self.has[side], also)

        @pl.when(condition)
        def _():
            item.start()

        self.sent.append((item, condition))
        source_side = self.has[OPPOSITE[side]]
        arrives = source_side if also is None else jnp.logical_and(source_side, also)

        def arrived():
            @pl.when(arrives)
            def _():
                item.wait_recv()

        return arrived

    def send_straight(self, source, target, side, also):
        rows = source.shape[-2]
        lead = (slice(None),) * (len(source.shape) - 2)
        halves = [(*lead, pl.ds(k * rows // 2, rows // 2)) for k in range(2)]
        waits = [self.send(source.at[at], target.at[at], side, also) for at in halves]
        return (lambda: None), (lambda half: waits[half]())

    def send_columns(self, source, target, side, slots, also=None, relay=True):
        if not relay:
            return self.send_straight(source, target, side, also)
        rows = source.shape[-2]
        lead = (slice(None),) * (len(source.shape) - 2)
        halves = [(*lead, pl.ds(k * rows // 2, rows // 2)) for k in range(2)]
        quarters = [(*lead, pl.ds(k * rows // 4, rows // 4)) for k in range(4)]
        both = lambda a: a if also is None else jnp.logical_and(a, also)
        crosses = self.crosses[side]
        direct = both(jnp.logical_and(self.has[side], jnp.logical_not(crosses)))
        whole = [(self.copy(source.at[at], target.at[at], self.at[side]), direct) for at in halves]
        first = self.copy(source.at[quarters[0]], target.at[quarters[0]], self.at[side])
        detours, onwards = [], []
        for k in range(3):
            at = quarters[k + 1]
            detours.append(self.copy(source.at[at], slots.at[k], self.relay[side][k]))
            onwards.append(self.copy(slots.at[k], target.at[at], self.beyond[side]))
        going = [(item, both(crosses)) for item in [*detours, first]] + whole
        for item, condition in going:

            @pl.when(condition)
            def _():
                item.start()

        relays = [both(here) for here in self.relays[side]]
        self.sent += going + list(zip(onwards, relays))
        receives_parts = self.crosses[OPPOSITE[side]]
        receives_whole = both(jnp.logical_and(self.has[OPPOSITE[side]], jnp.logical_not(receives_parts)))
        receives_parts = both(receives_parts)

        def forward():
            for detour, onward, here in zip(detours, onwards, relays):

                @pl.when(here)
                def _():
                    detour.wait_recv()
                    onward.start()

        def arrived(half):
            @pl.when(receives_whole)
            def _():
                whole[half][0].wait_recv()

            @pl.when(receives_parts)
            def _():
                for item in (first, onwards[0]) if half == 0 else onwards[1:]:
                    item.wait_recv()

        return forward, arrived

    def finish(self):
        for item, condition in self.sent:

            @pl.when(condition)
            def _():
                item.wait_send()


def by_rows(start, stop, step, body):
    def one(index, carry):
        body(pl.ds(pl.multiple_of(start + index * step, 8), step))
        return carry

    lax.fori_loop(0, (stop - start) // step, one, 0)


def first_kernel(
    tile_ref, amp_ref, order_ref, turn_ref, table_ref, probe_ref, ext_ref, ordered_ref, table_out, probe_out,
    planes, order, turn, tile_slots, corner_slots, local_sems, send_sems, recv_sems,
):
    links = Links(send_sems, recv_sems)
    upper, lower, own = pl.ds(0, HALF), pl.ds(3 * HALF, HALF), pl.ds(HALF, SIDE)
    local = [
        pltpu.make_async_copy(amp_ref, planes, local_sems.at[0]),
        pltpu.make_async_copy(order_ref, order, local_sems.at[1]),
        pltpu.make_async_copy(turn_ref, turn, local_sems.at[2]),
    ]
    inner = [
        pltpu.make_async_copy(
            tile_ref.at[:, :, :, pl.ds(block * HALF, HALF)], ext_ref.at[:, :, 1 + block, own], local_sems.at[3 + block]
        )
        for block in range(2)
    ]
    extra = [
        pltpu.make_async_copy(table_ref, table_out, local_sems.at[5]),
        pltpu.make_async_copy(probe_ref, probe_out, local_sems.at[6]),
    ]
    for item in local + inner + extra:
        item.start()
    links.greet()
    waits, col_waits, corner_waits = [], [], []
    for layer in range(2):
        for side, start, block in (("left", 0, 3), ("right", HALF, 0)):
            col_waits.append(
                links.send_columns(
                    tile_ref.at[:, layer, :, pl.ds(start, HALF)],
                    ext_ref.at[:, layer, block, own],
                    side,
                    tile_slots.at[layer],
                )
            )
    for layer in range(2):
        arrivals = []
        for block in range(2):
            lane = pl.ds(block * HALF, HALF)
            arrivals.append(
                links.send(tile_ref.at[:, layer, pl.ds(0, HALF), lane], ext_ref.at[:, layer, 1 + block, lower], "up")
            )
            arrivals.append(
                links.send(tile_ref.at[:, layer, pl.ds(HALF, HALF), lane], ext_ref.at[:, layer, 1 + block, upper], "down")
            )
        waits.append(arrivals)

    def clear(side, blocks, rows):
        @pl.when(jnp.logical_not(links.has[side]))
        def _():
            for part, layer in PLANES:
                for block in blocks:
                    ext_ref[part, layer, block, rows, :] = jnp.zeros((rows.size, HALF), jnp.float32)

    clear("up", (1, 2), upper)
    clear("down", (1, 2), lower)
    clear("left", (0,), own)
    clear("right", (3,), own)
    for rows, side in ((upper, "up"), (lower, "down")):
        for block, other in ((0, "left"), (3, "right")):

            @pl.when(jnp.logical_not(jnp.logical_and(links.has[side], links.has[other])))
            def _():
                for part, layer in PLANES:
                    ext_ref[part, layer, block, rows, :] = jnp.zeros((HALF, HALF), jnp.float32)

    for item in local:
        item.wait()

    def one_plane(index, carry):
        ordered_ref[index] = reorder_plane(planes[index], order[...], turn[...])
        return carry

    lax.fori_loop(0, planes.shape[0], one_plane, 0)
    for forward, _ in col_waits:
        forward()
    for layer in range(2):
        for arrived in waits[layer]:
            arrived()
        for number, (rows, side) in enumerate(((upper, "up"), (lower, "down"))):
            for block, to, target in ((1, "left", 3), (2, "right", 0)):
                corner_waits.append(
                    links.send_columns(
                        ext_ref.at[:, layer, block, rows],
                        ext_ref.at[:, layer, target, rows],
                        to,
                        corner_slots.at[layer, number],
                        also=links.has[side],
                        relay=layer < RELAYED_CORNER_LAYERS,
                    )
                )
    for forward, _ in corner_waits:
        forward()
    for item in inner + extra:
        item.wait()
    for _, arrived in col_waits + corner_waits:
        for half in range(2):
            arrived(half)
    links.finish()


PLANES = [(part, layer) for layer in range(2) for part in range(2)]


def collect_columns(links, grad_ref, from_left, from_right, total, slots, order, straight):
    for side, buffer in (("left", from_left), ("right", from_right)):

        @pl.when(jnp.logical_not(links.has[side]))
        def _():
            for part, layer in order:
                buffer[part, layer] = jnp.zeros((2 * SIDE, HALF), jnp.float32)

    arrivals = []
    for number, (part, layer) in enumerate(order):
        relay = number not in straight
        arrivals.append(
            (
                links.send_columns(grad_ref.at[part, layer, 0], from_right.at[part, layer], "left", slots.at[part, layer], relay=relay),
                links.send_columns(grad_ref.at[part, layer, 3], from_left.at[part, layer], "right", slots.at[part, layer], relay=relay),
            )
        )

    def finish(index, half):
        part, layer = order[index]
        for forward, arrived in arrivals[index]:
            if half == 0:
                forward()
            arrived(half)

        def add(rows):
            total[part, layer, 0, rows, :] = grad_ref[part, layer, 1, rows, :] + from_left[part, layer, rows, :]
            total[part, layer, 1, rows, :] = grad_ref[part, layer, 2, rows, :] + from_right[part, layer, rows, :]

        by_rows(half * SIDE, (half + 1) * SIDE, 64, add)

    return finish


def middle_kernel(
    ext_ref, grad_ref, out_ref, from_left, from_right, slots, from_up, from_down, total, halo_slots, send_sems, recv_sems
):
    links = Links(send_sems, recv_sems)
    links.greet()
    finish_columns = collect_columns(links, grad_ref, from_left, from_right, total, slots, PLANES, MIDDLE_DIRECT_GRADIENTS)
    for side, buffer in (("up", from_up), ("down", from_down)):

        @pl.when(jnp.logical_not(links.has[side]))
        def _():
            for part, layer in PLANES:
                buffer[part, layer] = jnp.zeros((2, SIDE, HALF), jnp.float32)

    for side, block in (("left", 0), ("right", 3)):

        @pl.when(jnp.logical_not(links.has[side]))
        def _():
            for part, layer in PLANES:
                out_ref[part, layer, block] = jnp.zeros((2 * SIDE, HALF), jnp.float32)

    step_up = jnp.where(links.has["up"], OBJECT_STEP, 0.0).astype(jnp.float32)
    step_down = jnp.where(links.has["down"], OBJECT_STEP, 0.0).astype(jnp.float32)
    held, arrivals, halos = {}, {}, []
    pieces = 2 * len(PLANES)

    def issue(number):
        (part, layer), block = PLANES[number // 2], number % 2
        if block == 0:
            finish_columns(number // 2, 0)
        up = links.send(total.at[part, layer, block, pl.ds(0, SIDE)], from_down.at[part, layer, block], "up")
        if block == 0:
            finish_columns(number // 2, 1)
        down = links.send(total.at[part, layer, block, pl.ds(SIDE, SIDE)], from_up.at[part, layer, block], "down")
        held[number] = [links.sent.pop(), links.sent.pop()]
        arrivals[number] = (up, down)

    def retire(number):
        for item, condition in held[number]:

            @pl.when(condition)
            def _():
                item.wait_send()

    for number in range(IN_FLIGHT):
        issue(number)
    for number in range(pieces):
        (part, layer), block = PLANES[number // 2], number % 2
        for arrived in arrivals[number]:
            arrived()
        retire(number)
        if number + IN_FLIGHT < pieces:
            issue(number + IN_FLIGHT)
        for start, buffer, offset, step in (
            (0, from_up, 0, step_up),
            (HALF, from_up, 0, OBJECT_STEP),
            (SIDE, from_down, SIDE, OBJECT_STEP),
            (3 * HALF, from_down, SIDE, step_down),
        ):
            for row in range(start, start + HALF, 64):
                rows, near = pl.ds(row, 64), pl.ds(row - offset, 64)
                gradient = total[part, layer, block, rows, :] + buffer[part, layer, block, near, :]
                out_ref[part, layer, 1 + block, rows, :] = ext_ref[part, layer, 1 + block, rows, :] - step * gradient
        side, target = (("left", 3), ("right", 0))[block]
        halos.append(
            links.send_columns(
                out_ref.at[part, layer, 1 + block],
                out_ref.at[part, layer, target],
                side,
                halo_slots.at[part, layer],
                relay=number // 2 not in MIDDLE_DIRECT_HALOS,
            )
        )
        if number:
            halos[number - 1][0]()
    halos[-1][0]()
    for _, arrived in halos:
        for half in range(2):
            arrived(half)
    links.finish()


def last_kernel(
    ext_ref, grad_ref, first_probe_ref, second_probe_ref, probe_ref, object_ref, new_probe_ref,
    from_left, from_right, slots, from_up, from_down, total, partial, pair, landings, sums, gathered, send_sems, recv_sems,
):
    links = Links(send_sems, recv_sems)
    row, col = links.row, links.col
    core, x, y_low = lax.rem(col, 2), lax.rem(col // 2, 4), col // 8
    y_high, z = lax.rem(row, 2), row // 2
    y = y_high * 2 + y_low
    partner = (row, col + 1 - 2 * core)
    plane = lambda k: ((k // 4) * 2 + y_high, y_low * 8 + lax.rem(k, 4) * 2 + core)
    line = lambda k: (z * 2 + k // 2, lax.rem(k, 2) * 8 + x * 2 + core)
    groups = [(z * 4 + x, plane, 16), (y, line, 4)]
    peers = [partner]
    for place, device, members in groups:
        peers += [device(lax.rem(place + k, members)) for k in range(1, members)]
    links.greet(peers)
    count = 4 * SIDE
    half = count // 2

    def rows_at(start, size):
        return pl.ds(pl.multiple_of(start, 8), size)

    def start(source, target, device):
        item = links.copy(source, target, device)
        item.start()
        return item

    def add_probe(rows):
        partial[rows, :] = first_probe_ref[rows, :] + second_probe_ref[rows, :]

    by_rows(0, count, 64, add_probe)
    swap = start(partial.at[rows_at((1 - core) * half, half)], pair, partner)
    finish_columns = collect_columns(links, grad_ref, from_left, from_right, total, slots, PLANES, LAST_DIRECT_GRADIENTS)
    for side, buffer in (("up", from_up), ("down", from_down)):

        @pl.when(jnp.logical_not(links.has[side]))
        def _():
            for part, layer in PLANES:
                buffer[part, layer] = jnp.zeros((2, HALF, HALF), jnp.float32)

    swap.wait_recv()
    base = core * half

    def add_pair(index, carry):
        near = pl.ds(pl.multiple_of(index * 64, 64), 64)
        mine = rows_at(base + index * 64, 64)
        sums[mine, :] = partial[mine, :] + pair[near, :]
        return carry

    lax.fori_loop(0, half // 64, add_pair, 0)
    gathers = [swap]

    piece = half // 16
    plane_base = base + (z * 4 + x) * piece
    mine = rows_at(plane_base, piece)
    plane_peers = [device for device in peers[1:16]]
    line_peers = peers[16:]

    def spread_plane():
        items = []
        for k in range(1, 16):
            other = lax.rem(z * 4 + x + k, 16)
            source = sums.at[rows_at(base + other * piece, piece)]
            items.append(start(source, landings[0].at[k - 1], plane_peers[k - 1]))
        gathers.extend(items)
        return items

    def add_plane(items):
        for item in items:
            item.wait_recv()
        value = sums[mine, :]
        for k in range(15):
            value = value + landings[0][k]
        landings[1][y] = value

    def spread_line():
        items = [start(landings[1].at[y], landings[1].at[y], device) for device in line_peers]
        gathers.extend(items)
        return items

    def add_line(items):
        for item in items:
            item.wait_recv()
        gathered[mine, :] = (landings[1][0] + landings[1][1]) + (landings[1][2] + landings[1][3])

    def share_plane():
        items = [start(gathered.at[mine], gathered.at[mine], device) for device in plane_peers]
        gathers.extend(items)
        return items

    def await_all(items):
        for item in items:
            item.wait_recv()

    held, arrivals = {}, {}

    def issue(number):
        part, layer = PLANES[number // 2]
        block = number % 2
        up = links.send(total.at[part, layer, block, pl.ds(0, HALF)], from_down.at[part, layer, block], "up")
        down = links.send(total.at[part, layer, block, pl.ds(3 * HALF, HALF)], from_up.at[part, layer, block], "down")
        held[number] = [links.sent.pop(), links.sent.pop()]
        arrivals[number] = (up, down)

    def retire(number):
        for item, condition in held[number]:

            @pl.when(condition)
            def _():
                item.wait_send()

    def columns_in(index):
        finish_columns(index, 0)
        finish_columns(index, 1)

    items = spread_plane()
    columns_in(0)
    issue(0)
    issue(1)
    columns_in(1)
    retire(0)
    issue(2)
    retire(1)
    issue(3)
    add_plane(items)
    items = spread_line()
    columns_in(2)
    retire(2)
    issue(4)
    retire(3)
    issue(5)
    add_line(items)
    items = share_plane()
    columns_in(3)
    retire(4)
    issue(6)
    retire(5)
    issue(7)
    await_all(items)
    retire(6)
    retire(7)
    own_half = gathered.at[rows_at(base, half)]
    swap_back = start(own_half, own_half, partner)
    for number in range(2 * len(PLANES)):
        (part, layer), block = PLANES[number // 2], number % 2
        for arrived in arrivals[number]:
            arrived()
        lane = pl.ds(block * HALF, HALF)
        for begin, buffer in ((HALF, from_up), (SIDE, from_down)):
            for offset in range(0, HALF, 64):
                rows, near = pl.ds(begin + offset, 64), pl.ds(offset, 64)
                gradient = total[part, layer, block, rows, :] + buffer[part, layer, block, near, :]
                target = pl.ds(begin - HALF + offset, 64)
                object_ref[part, layer, target, lane] = ext_ref[part, layer, 1 + block, rows, :] - OBJECT_STEP * gradient
    swap_back.wait_recv()

    def finish_probe(rows):
        new_probe_ref[rows, :] = probe_ref[rows, :] - PROBE_STEP * gathered[rows, :]

    by_rows(0, count, 64, finish_probe)
    for item in gathers + [swap_back]:
        item.wait_send()
    links.finish()


def vmem_specs(count):
    return [pl.BlockSpec(memory_space=pltpu.VMEM)] * count


def comm_params(identity, limit):
    return pltpu.CompilerParams(collective_id=identity, has_side_effects=True, vmem_limit_bytes=limit << 20)


def semaphores(count):
    return [pltpu.SemaphoreType.DMA((count,)), pltpu.SemaphoreType.DMA((count,))]


def f32(*shape):
    return pltpu.VMEM(shape, jnp.float32)


EXTENDED = jax.ShapeDtypeStruct((2, 2, 4, 2 * SIDE, HALF), jnp.float32)


def first_exchange(tile, amplitudes, table, probe_modes):
    planes = amplitudes.shape[0]
    inputs = (tile, amplitudes, jnp.asarray(ORDER), jnp.asarray(ORDER.T), table, probe_modes)
    return pl.pallas_call(
        first_kernel,
        out_shape=(
            EXTENDED,
            jax.ShapeDtypeStruct((planes, SIDE, SIDE), jnp.float32),
            jax.ShapeDtypeStruct(table.shape, table.dtype),
            jax.ShapeDtypeStruct(probe_modes.shape, probe_modes.dtype),
        ),
        in_specs=[pl.BlockSpec(memory_space=pltpu.HBM)] * 6,
        out_specs=tuple(vmem_specs(4)),
        scratch_shapes=[
            f32(planes, SIDE, SIDE),
            pltpu.VMEM((SIDE, SIDE), jnp.bfloat16),
            pltpu.VMEM((SIDE, SIDE), jnp.bfloat16),
            f32(2, 3, 2, SIDE // 4, HALF),
            f32(2, 2, 3, 2, HALF // 4, HALF),
            pltpu.SemaphoreType.DMA((7,)),
            *semaphores(8 + 9 * 12),
        ],
        compiler_params=comm_params(0, 14),
    )(*[pltpu.with_memory_space_constraint(value, pltpu.HBM) for value in inputs])


def columns_buffers():
    return [f32(2, 2, 2 * SIDE, HALF), f32(2, 2, 2 * SIDE, HALF), f32(2, 2, 3, HALF, HALF)]


def middle_exchange(extended, gradient):
    return pl.pallas_call(
        middle_kernel,
        out_shape=EXTENDED,
        in_specs=vmem_specs(2),
        out_specs=vmem_specs(1)[0],
        scratch_shapes=[
            *columns_buffers(),
            f32(2, 2, 2, SIDE, HALF),
            f32(2, 2, 2, SIDE, HALF),
            f32(2, 2, 2, 2 * SIDE, HALF),
            f32(2, 2, 3, HALF, HALF),
            *semaphores(72 + 16 + 72),
        ],
        compiler_params=comm_params(1, 24),
    )(extended, gradient)


def last_exchange(extended, gradient, first_probe, second_probe, probe_modes):
    flat = (4 * SIDE, SIDE)
    new_object, new_probe = pl.pallas_call(
        last_kernel,
        out_shape=(
            jax.ShapeDtypeStruct((2, 2, SIDE, SIDE), jnp.float32),
            jax.ShapeDtypeStruct(flat, jnp.float32),
        ),
        in_specs=vmem_specs(5),
        out_specs=tuple(vmem_specs(2)),
        scratch_shapes=[
            *columns_buffers(),
            f32(2, 2, 2, HALF, HALF),
            f32(2, 2, 2, HALF, HALF),
            f32(2, 2, 2, 2 * SIDE, HALF),
            f32(*flat),
            f32(2 * SIDE, SIDE),
            [f32(15, 2 * SIDE // 16, SIDE), f32(4, 2 * SIDE // 16, SIDE)],
            f32(*flat),
            f32(*flat),
            *semaphores(72 + 16 + 2 + 33),
        ],
        compiler_params=comm_params(2, 26),
    )(extended, gradient, first_probe.reshape(flat), second_probe.reshape(flat), probe_modes.reshape(flat))
    return new_object, new_probe.reshape(probe_modes.shape)


def batch_kernel(
    batch, offset_ref, count_ref, ext_ref, probe_ref, amp_ref, table_ref, grad_ref, probe_grad_ref,
    obj, psi, right_a, right_b, yield_a, yield_b, left_a, left_b, out_a, out_b,
):
    lanes = lax.broadcasted_iota(jnp.int32, (CHUNK, HALF), 1)
    lo, hi = pl.ds(0, HALF), pl.ds(HALF, HALF)

    def chunks(total, body):
        def step(index, carry):
            body(pl.multiple_of(index * CHUNK, CHUNK))
            return carry

        lax.fori_loop(0, total // CHUNK, step, 0, unroll=True)

    def bf(value):
        return value.astype(jnp.bfloat16)

    def zero_grad(row):
        for part in range(2):
            for layer in range(2):
                for block in range(4):
                    grad_ref[part, layer, block, pl.ds(row, CHUNK), :] = jnp.zeros((CHUNK, HALF), jnp.float32)

    chunks(2 * SIDE, zero_grad)

    def zero_probe(row):
        for part in range(2):
            for mode in range(MODES):
                probe_grad_ref[part, mode, pl.ds(row, CHUNK), :] = jnp.zeros((CHUNK, SIDE), jnp.float32)

    chunks(SIDE, zero_probe)

    def right(table_a, table_b):
        yield_a[...] = dot(right_a[...], table_ref[table_a])
        yield_b[...] = dot(right_b[...], table_ref[table_b])

    def left(table_a, table_b):
        out_a[...] = dot(table_ref[table_a], left_a[...])
        out_b[...] = dot(table_ref[table_b], left_b[...])

    def put_split(mode, row, re, im):
        at = pl.ds(mode * SIDE + row, CHUNK)
        right_a[at, lo] = bf(re[0] + re[1])
        right_a[at, hi] = bf(im[0] + im[1])
        right_b[at, lo] = bf(re[0] - re[1])
        right_b[at, hi] = bf(im[0] - im[1])

    def columns(ref, mode):
        return pl.ds(mode * SIDE, HALF), pl.ds(mode * SIDE + HALF, HALF)

    def middle_spread(row):
        for mode in range(MODES):
            here = columns(left_a, mode)
            for part, lane in ((0, lo), (1, hi)):
                top = pl.ds(mode * SIDE + row, CHUNK)
                low = pl.ds(mode * SIDE + HALF + row, CHUNK)
                at, ab = yield_a[top, lane], yield_a[low, lane]
                bt, bb = yield_b[top, lane], yield_b[low, lane]
                to = pl.ds(part * HALF + row, CHUNK)
                a_sum, a_dif = at + ab, at - ab
                b_sum, b_dif = bt + bb, bt - bb
                left_a[to, here[0]] = bf(a_sum + b_sum)
                left_a[to, here[1]] = bf(a_sum - b_sum)
                left_b[to, here[0]] = bf(a_dif + b_dif)
                left_b[to, here[1]] = bf(a_dif - b_dif)

    def middle_forward(row):
        for mode in range(MODES):
            here = columns(left_a, mode)
            for part, lane in ((0, lo), (1, hi)):
                top = pl.ds(mode * SIDE + row, CHUNK)
                low = pl.ds(mode * SIDE + HALF + row, CHUNK)
                to = pl.ds(part * HALF + row, CHUNK)
                for source, at in ((yield_a, here[0]), (yield_b, here[1])):
                    upper, lower = source[top, lane], source[low, lane]
                    left_a[to, at] = bf(upper + lower)
                    left_b[to, at] = bf(upper - lower)

    def middle_backward(row):
        for mode in range(MODES):
            here = columns(left_a, mode)
            for part, lane in ((0, lo), (1, hi)):
                to = pl.ds(part * HALF + row, CHUNK)
                for base, target in ((0, left_a), (HALF, left_b)):
                    at = pl.ds(mode * SIDE + base + row, CHUNK)
                    even, odd = yield_a[at, lane], yield_b[at, lane]
                    target[to, here[0]] = bf(even + odd)
                    target[to, here[1]] = bf(even - odd)

    def joined(mode, row):
        result = []
        for sign in (1, -1):
            pair = []
            for part in range(2):
                at = pl.ds(part * HALF + row, CHUNK)
                halves = []
                for lane in columns(out_a, mode):
                    a, b = out_a[at, lane], out_b[at, lane]
                    halves.append(a + b if sign > 0 else a - b)
                pair.append(halves)
            result.append(pair)
        return result

    def pair_of(ref, first, second, row):
        return [ref[first, second, pl.ds(row, CHUNK), lane] for lane in (lo, hi)]

    def one_slot(slot, carry):
        start_row = offset_ref[batch * 2, slot]
        start_col = offset_ref[batch * 2 + 1, slot]
        base = start_col // HALF
        shift = start_col % HALF
        take_left = lanes < HALF - shift
        put_right = lanes >= shift
        back = lax.rem(HALF - shift, HALF)

        def fetch(row):
            for part in range(2):
                for layer in range(2):
                    at = pl.ds(start_row + row, CHUNK)
                    turned = [pltpu.roll(ext_ref[part, layer, base + k, at, :], back, 1) for k in range(3)]
                    obj[part, layer, pl.ds(row, CHUNK), lo] = jnp.where(take_left, turned[0], turned[1])
                    obj[part, layer, pl.ds(row, CHUNK), hi] = jnp.where(take_left, turned[1], turned[2])

        chunks(SIDE, fetch)

        def enter(row):
            o_re, o_im = pair_of(obj, 0, 0, row), pair_of(obj, 1, 0, row)
            for mode in range(MODES):
                p_re, p_im = pair_of(probe_ref, 0, mode, row), pair_of(probe_ref, 1, mode, row)
                re = [p_re[k] * o_re[k] - p_im[k] * o_im[k] for k in range(2)]
                im = [p_re[k] * o_im[k] + p_im[k] * o_re[k] for k in range(2)]
                put_split(mode, row, re, im)

        chunks(SIDE, enter)
        right(SUM_R, DIF_R)
        chunks(HALF, middle_spread)
        left(SUM_L, DIF_L)

        def second_slice(row):
            for side in range(2):
                at = row + side * HALF
                o_re, o_im = pair_of(obj, 0, 1, at), pair_of(obj, 1, 1, at)
                for mode in range(MODES):
                    w_re, w_im = joined(mode, row)[side]
                    for k, lane in ((0, lo), (1, hi)):
                        psi[0, mode, pl.ds(at, CHUNK), lane] = w_re[k]
                        psi[1, mode, pl.ds(at, CHUNK), lane] = w_im[k]
                    re = [w_re[k] * o_re[k] - w_im[k] * o_im[k] for k in range(2)]
                    im = [w_re[k] * o_im[k] + w_im[k] * o_re[k] for k in range(2)]
                    put_split(mode, at, re, im)

        chunks(HALF, second_slice)
        right(EVEN_R, ODD_R)
        chunks(HALF, middle_forward)
        left(EVEN_L, ODD_L)

        def compare(row):
            for base_row, source in ((0, out_a), (HALF, out_b)):
                waves = []
                for mode in range(MODES):
                    here = columns(source, mode)
                    re = [source[pl.ds(row, CHUNK), lane] for lane in here]
                    im = [source[pl.ds(HALF + row, CHUNK), lane] for lane in here]
                    waves.append((re, im))
                for k, lane in ((0, lo), (1, hi)):
                    intensity = waves[0][0][k] * waves[0][0][k] + waves[0][1][k] * waves[0][1][k]
                    for re, im in waves[1:]:
                        intensity = intensity + (re[k] * re[k] + im[k] * im[k])
                    amplitude = amp_ref[batch * (amp_ref.shape[0] // 2) + slot, pl.ds(base_row + row, CHUNK), lane]
                    ratio = 1.0 - amplitude * lax.rsqrt(jnp.maximum(intensity, AMPLITUDE_FLOOR**2))
                    target = right_a if k == 0 else right_b
                    for mode, (re, im) in enumerate(waves):
                        at = pl.ds(mode * SIDE + base_row + row, CHUNK)
                        target[at, lo] = bf(re[k] * ratio)
                        target[at, hi] = bf(im[k] * ratio)

        chunks(HALF, compare)
        right(EVEN_L, ODD_L)
        chunks(HALF, middle_backward)
        left(EVEN_R, ODD_R)

        def add_term(part, layer, row, term):
            turned = [pltpu.roll(value, shift, 1) for value in term]
            zero = jnp.zeros_like(turned[0])
            spread = [
                jnp.where(put_right, turned[0], zero),
                jnp.where(put_right, turned[1], turned[0]),
                jnp.where(put_right, zero, turned[1]),
            ]
            at = pl.ds(start_row + row, CHUNK)
            for k in range(3):
                grad_ref[part, layer, base + k, at, :] = grad_ref[part, layer, base + k, at, :] + spread[k]

        def object_term(layer, row, waves, backs):
            re, im = [], []
            for k in range(2):
                re.append(sum(w[0][k] * b[0][k] + w[1][k] * b[1][k] for w, b in zip(waves, backs)))
                im.append(sum(w[0][k] * b[1][k] - w[1][k] * b[0][k] for w, b in zip(waves, backs)))
            add_term(0, layer, row, re)
            add_term(1, layer, row, im)

        def last_back(row):
            for side in range(2):
                at = row + side * HALF
                backs = [joined(mode, row)[side] for mode in range(MODES)]
                waves = [(pair_of(psi, 0, mode, at), pair_of(psi, 1, mode, at)) for mode in range(MODES)]
                o_re, o_im = pair_of(obj, 0, 1, at), pair_of(obj, 1, 1, at)
                for mode, (b_re, b_im) in enumerate(backs):
                    re = [o_re[k] * b_re[k] + o_im[k] * b_im[k] for k in range(2)]
                    im = [o_re[k] * b_im[k] - o_im[k] * b_re[k] for k in range(2)]
                    put_split(mode, at, re, im)
                object_term(1, at, waves, backs)

        chunks(HALF, last_back)
        right(SUM_L, DIF_L)
        chunks(HALF, middle_spread)
        left(SUM_R, DIF_R)

        def first_back(row):
            for side in range(2):
                at = row + side * HALF
                backs = [joined(mode, row)[side] for mode in range(MODES)]
                waves = [(pair_of(probe_ref, 0, mode, at), pair_of(probe_ref, 1, mode, at)) for mode in range(MODES)]
                o_re, o_im = pair_of(obj, 0, 0, at), pair_of(obj, 1, 0, at)
                for mode, (b_re, b_im) in enumerate(backs):
                    for k, lane in ((0, lo), (1, hi)):
                        spot = (mode, pl.ds(at, CHUNK), lane)
                        probe_grad_ref[(0, *spot)] = probe_grad_ref[(0, *spot)] + (o_re[k] * b_re[k] + o_im[k] * b_im[k])
                        probe_grad_ref[(1, *spot)] = probe_grad_ref[(1, *spot)] + (o_re[k] * b_im[k] - o_im[k] * b_re[k])
                object_term(0, at, waves, backs)

        chunks(HALF, first_back)
        return carry

    lax.fori_loop(0, count_ref[batch], one_slot, 0)


def batch_terms(batch, extended, probe_modes, amplitudes, offsets, counts, table):
    vmem = pl.BlockSpec(memory_space=pltpu.VMEM)
    smem = pl.BlockSpec(memory_space=pltpu.SMEM)
    field = pltpu.VMEM((2, 2, SIDE, SIDE), jnp.float32)
    return pl.pallas_call(
        functools.partial(batch_kernel, batch),
        out_shape=(
            jax.ShapeDtypeStruct((2, 2, 4, 2 * SIDE, HALF), jnp.float32),
            jax.ShapeDtypeStruct((2, MODES, SIDE, SIDE), jnp.float32),
        ),
        in_specs=[smem, smem, vmem, vmem, vmem, vmem],
        out_specs=(vmem, vmem),
        scratch_shapes=[
            field,
            field,
            pltpu.VMEM((MODES * SIDE, SIDE), jnp.bfloat16),
            pltpu.VMEM((MODES * SIDE, SIDE), jnp.bfloat16),
            pltpu.VMEM((MODES * SIDE, SIDE), jnp.float32),
            pltpu.VMEM((MODES * SIDE, SIDE), jnp.float32),
            pltpu.VMEM((SIDE, MODES * SIDE), jnp.bfloat16),
            pltpu.VMEM((SIDE, MODES * SIDE), jnp.bfloat16),
            pltpu.VMEM((SIDE, MODES * SIDE), jnp.float32),
            pltpu.VMEM((SIDE, MODES * SIDE), jnp.float32),
        ],
        compiler_params=pltpu.CompilerParams(vmem_limit_bytes=26 << 20),
        cost_estimate=pl.CostEstimate(flops=3 * 64 * SIDE**3, bytes_accessed=12 << 20, transcendentals=0),
    )(offsets, counts, extended, probe_modes, amplitudes, table)


def body(object_field, probe_modes, amplitudes, offsets, counts):
    batches, slots = amplitudes.shape[:2]
    table = jnp.asarray(TABLES)
    extended, ordered, table, probe_modes = first_exchange(
        object_field, amplitudes.reshape(batches * slots, SIDE, SIDE), table, probe_modes
    )
    offsets, counts = offsets.reshape(2 * batches, slots), counts.reshape(batches)
    terms = lambda cells, batch: batch_terms(batch, cells, probe_modes, ordered, offsets, counts, table)
    gradient, first_probe = terms(extended, 0)
    extended = middle_exchange(extended, gradient)
    gradient, second_probe = terms(extended, 1)
    return last_exchange(extended, gradient, first_probe, second_probe, probe_modes)


def solution(mesh):
    return jax.shard_map(
        body,
        mesh=mesh,
        in_specs=(
            P(None, None, "row", "col"),
            P(),
            P(None, "row", "col", None, None),
            P(None, None, "row", "col"),
            P(None, "row", "col"),
        ),
        out_specs=(P(None, None, "row", "col"), P()),
        check_vma=False,
    )
```

```python
import functools
import math

import jax
import jax.numpy as jnp
import numpy as np
from jax import lax
from jax.experimental import pallas as pl
from jax.experimental.pallas import tpu as pltpu
from jax.sharding import PartitionSpec as P

AMPLITUDE_FLOOR = 0.5
OBJECT_STEP = 0.25
PROBE_STEP = 0.125
SIDE = 256
HALF = SIDE // 2
MODES = 2
CHUNK = 16
IN_FLIGHT = 2
RELAYED_CORNER_LAYERS = 1
MIDDLE_DIRECT_GRADIENTS = (0,)
MIDDLE_DIRECT_HALOS = (3,)
LAST_DIRECT_GRADIENTS = (0,)
MESH = pl.DeviceIdType.MESH
SIDES = ("up", "down", "left", "right")
OPPOSITE = {"up": "down", "down": "up", "left": "right", "right": "left"}


def real_form(table):
    re, im = table.real, table.imag
    return np.block([[re, im], [-im, re]]).astype(jnp.bfloat16)


def make_tables():
    index = np.arange(SIDE)
    angles = (index[:, None] * index[None, :] % SIDE).astype(np.float32) * np.float32(2.0 * math.pi / SIDE)
    scale = np.float32(1.0 / math.sqrt(SIDE))
    rounded = lambda v: (v * scale).astype(jnp.bfloat16).astype(np.float64)
    forward = rounded(np.cos(angles)) - 1j * rounded(np.sin(angles))
    frequency = np.where(index < HALF, index, index - SIDE).astype(np.float64)
    chirp = np.exp(-2j * math.pi * (frequency * frequency % (16 * SIDE)) / (16 * SIDE))
    spread = (forward.conj() * chirp[None, :]) @ forward
    same = 0.25 * (spread[:HALF, :HALF] + spread[HALF:, HALF:] + spread[:HALF, HALF:] + spread[HALF:, :HALF])
    other = 0.25 * (spread[:HALF, :HALF] + spread[HALF:, HALF:] - spread[:HALF, HALF:] - spread[HALF:, :HALF])
    same = 0.5 * (same + same.T)
    other = 0.5 * (other + other.T)
    even = forward[:HALF, 0::2]
    odd = forward[:HALF, 1::2]
    rows = []
    for table in (same, other, even, odd):
        matrix = real_form(table)
        rows += [matrix, np.ascontiguousarray(matrix.T)]
    order = np.zeros((SIDE, SIDE), np.float32)
    order[0::2, :HALF] = np.eye(HALF)
    order[1::2, HALF:] = np.eye(HALF)
    return np.stack(rows), order.astype(jnp.bfloat16)


TABLES, ORDER = make_tables()
(SUM_R, SUM_L, DIF_R, DIF_L, EVEN_R, EVEN_L, ODD_R, ODD_L) = range(8)


def dot(left, right):
    return jnp.dot(left, right, preferred_element_type=jnp.float32)


def three_parts(value):
    high = value.astype(jnp.bfloat16)
    rest = value - high.astype(jnp.float32)
    middle = rest.astype(jnp.bfloat16)
    return high, middle, (rest - middle.astype(jnp.float32)).astype(jnp.bfloat16)


def reorder_plane(plane, order, turn):
    high, middle, low = [dot(part, order) for part in three_parts(plane)]
    high, middle, low = [dot(turn, part) for part in three_parts(high + (middle + low))]
    return high + (middle + low)


class Links:
    def __init__(self, send_sems, recv_sems):
        self.row, self.col = lax.axis_index("row"), lax.axis_index("col")
        rows, cols = lax.axis_size("row"), lax.axis_size("col")
        self.has = {
            "up": self.row > 0,
            "down": self.row < rows - 1,
            "left": self.col > 0,
            "right": self.col < cols - 1,
        }
        self.at = {
            "up": (self.row - 1, self.col),
            "down": (self.row + 1, self.col),
            "left": (self.row, self.col - 1),
            "right": (self.row, self.col + 1),
        }
        middle, last = cols // 2, cols - 1
        relays = {"right": (last, last - 2, last - 4), "left": (0, 2, 4)}
        self.crosses = {"right": self.col == middle - 1, "left": self.col == middle}
        self.beyond = {"right": (self.row, middle), "left": (self.row, middle - 1)}
        self.relay = {side: [(self.row, col) for col in relays[side]] for side in relays}
        self.relays = {side: [self.col == col for col in relays[side]] for side in relays}
        self.send_sems, self.recv_sems = send_sems, recv_sems
        self.used = 0
        self.sent = []

    def greet(self, peers=()):
        barrier = pltpu.get_barrier_semaphore()
        for side in SIDES:

            @pl.when(self.has[side])
            def _():
                pl.semaphore_signal(barrier, inc=1, device_id=self.at[side], device_id_type=MESH)

        inner = jnp.logical_or(self.crosses["left"], self.crosses["right"])
        outer = functools.reduce(jnp.logical_or, self.relays["left"] + self.relays["right"])
        extra = 6 * inner.astype(jnp.int32) + 2 * outer.astype(jnp.int32)
        for condition, devices in (
            (inner, self.relay["left"] + self.relay["right"]),
            (outer, list(self.beyond.values())),
        ):

            @pl.when(condition)
            def _():
                for device in devices:
                    pl.semaphore_signal(barrier, inc=1, device_id=device, device_id_type=MESH)

        for peer in peers:
            pl.semaphore_signal(barrier, inc=1, device_id=peer, device_id_type=MESH)
        pl.semaphore_wait(barrier, len(peers) + extra + sum(self.has[side].astype(jnp.int32) for side in SIDES))

    def copy(self, source, target, device):
        index = self.used
        self.used += 1
        return pltpu.make_async_remote_copy(
            src_ref=source,
            dst_ref=target,
            send_sem=self.send_sems.at[index],
            recv_sem=self.recv_sems.at[index],
            device_id=device,
            device_id_type=MESH,
        )

    def send(self, source, target, side, also=None):
        item = self.copy(source, target, self.at[side])
        condition = self.has[side] if also is None else jnp.logical_and(self.has[side], also)

        @pl.when(condition)
        def _():
            item.start()

        self.sent.append((item, condition))
        source_side = self.has[OPPOSITE[side]]
        arrives = source_side if also is None else jnp.logical_and(source_side, also)

        def arrived():
            @pl.when(arrives)
            def _():
                item.wait_recv()

        return arrived

    def send_straight(self, source, target, side, also):
        rows = source.shape[-2]
        lead = (slice(None),) * (len(source.shape) - 2)
        halves = [(*lead, pl.ds(k * rows // 2, rows // 2)) for k in range(2)]
        waits = [self.send(source.at[at], target.at[at], side, also) for at in halves]
        return (lambda: None), (lambda half: waits[half]())

    def send_columns(self, source, target, side, slots, also=None, relay=True):
        if not relay:
            return self.send_straight(source, target, side, also)
        rows = source.shape[-2]
        lead = (slice(None),) * (len(source.shape) - 2)
        halves = [(*lead, pl.ds(k * rows // 2, rows // 2)) for k in range(2)]
        quarters = [(*lead, pl.ds(k * rows // 4, rows // 4)) for k in range(4)]
        both = lambda a: a if also is None else jnp.logical_and(a, also)
        crosses = self.crosses[side]
        direct = both(jnp.logical_and(self.has[side], jnp.logical_not(crosses)))
        whole = [(self.copy(source.at[at], target.at[at], self.at[side]), direct) for at in halves]
        first = self.copy(source.at[quarters[0]], target.at[quarters[0]], self.at[side])
        detours, onwards = [], []
        for k in range(3):
            at = quarters[k + 1]
            detours.append(self.copy(source.at[at], slots.at[k], self.relay[side][k]))
            onwards.append(self.copy(slots.at[k], target.at[at], self.beyond[side]))
        going = [(item, both(crosses)) for item in [*detours, first]] + whole
        for item, condition in going:

            @pl.when(condition)
            def _():
                item.start()

        relays = [both(here) for here in self.relays[side]]
        self.sent += going + list(zip(onwards, relays))
        receives_parts = self.crosses[OPPOSITE[side]]
        receives_whole = both(jnp.logical_and(self.has[OPPOSITE[side]], jnp.logical_not(receives_parts)))
        receives_parts = both(receives_parts)

        def forward():
            for detour, onward, here in zip(detours, onwards, relays):

                @pl.when(here)
                def _():
                    detour.wait_recv()
                    onward.start()

        def arrived(half):
            @pl.when(receives_whole)
            def _():
                whole[half][0].wait_recv()

            @pl.when(receives_parts)
            def _():
                for item in (first, onwards[0]) if half == 0 else onwards[1:]:
                    item.wait_recv()

        return forward, arrived

    def finish(self):
        for item, condition in self.sent:

            @pl.when(condition)
            def _():
                item.wait_send()


def by_rows(start, stop, step, body):
    def one(index, carry):
        body(pl.ds(pl.multiple_of(start + index * step, 8), step))
        return carry

    lax.fori_loop(0, (stop - start) // step, one, 0, unroll=True)


def first_kernel(
    tile_ref, amp_ref, order_ref, turn_ref, table_ref, probe_ref, ext_ref, ordered_ref, table_out, probe_out,
    planes, order, turn, tile_slots, corner_slots, local_sems, send_sems, recv_sems,
):
    links = Links(send_sems, recv_sems)
    upper, lower, own = pl.ds(0, HALF), pl.ds(3 * HALF, HALF), pl.ds(HALF, SIDE)
    local = [
        pltpu.make_async_copy(amp_ref, planes, local_sems.at[0]),
        pltpu.make_async_copy(order_ref, order, local_sems.at[1]),
        pltpu.make_async_copy(turn_ref, turn, local_sems.at[2]),
    ]
    inner = [
        pltpu.make_async_copy(
            tile_ref.at[:, :, :, pl.ds(block * HALF, HALF)], ext_ref.at[:, :, 1 + block, own], local_sems.at[3 + block]
        )
        for block in range(2)
    ]
    extra = [
        pltpu.make_async_copy(table_ref, table_out, local_sems.at[5]),
        pltpu.make_async_copy(probe_ref, probe_out, local_sems.at[6]),
    ]
    for item in local + inner + extra:
        item.start()
    links.greet()
    waits, col_waits, corner_waits = [], [], []
    for layer in range(2):
        for side, start, block in (("left", 0, 3), ("right", HALF, 0)):
            col_waits.append(
                links.send_columns(
                    tile_ref.at[:, layer, :, pl.ds(start, HALF)],
                    ext_ref.at[:, layer, block, own],
                    side,
                    tile_slots.at[layer],
                )
            )
    for layer in range(2):
        arrivals = []
        for block in range(2):
            lane = pl.ds(block * HALF, HALF)
            arrivals.append(
                links.send(tile_ref.at[:, layer, pl.ds(0, HALF), lane], ext_ref.at[:, layer, 1 + block, lower], "up")
            )
            arrivals.append(
                links.send(tile_ref.at[:, layer, pl.ds(HALF, HALF), lane], ext_ref.at[:, layer, 1 + block, upper], "down")
            )
        waits.append(arrivals)

    def clear(side, blocks, rows):
        @pl.when(jnp.logical_not(links.has[side]))
        def _():
            for part, layer in PLANES:
                for block in blocks:
                    ext_ref[part, layer, block, rows, :] = jnp.zeros((rows.size, HALF), jnp.float32)

    clear("up", (1, 2), upper)
    clear("down", (1, 2), lower)
    clear("left", (0,), own)
    clear("right", (3,), own)
    for rows, side in ((upper, "up"), (lower, "down")):
        for block, other in ((0, "left"), (3, "right")):

            @pl.when(jnp.logical_not(jnp.logical_and(links.has[side], links.has[other])))
            def _():
                for part, layer in PLANES:
                    ext_ref[part, layer, block, rows, :] = jnp.zeros((HALF, HALF), jnp.float32)

    for item in local:
        item.wait()

    def one_plane(index, carry):
        ordered_ref[index] = reorder_plane(planes[index], order[...], turn[...])
        return carry

    lax.fori_loop(0, planes.shape[0], one_plane, 0)
    for forward, _ in col_waits:
        forward()
    for layer in range(2):
        for arrived in waits[layer]:
            arrived()
        for number, (rows, side) in enumerate(((upper, "up"), (lower, "down"))):
            for block, to, target in ((1, "left", 3), (2, "right", 0)):
                corner_waits.append(
                    links.send_columns(
                        ext_ref.at[:, layer, block, rows],
                        ext_ref.at[:, layer, target, rows],
                        to,
                        corner_slots.at[layer, number],
                        also=links.has[side],
                        relay=layer < RELAYED_CORNER_LAYERS,
                    )
                )
    for forward, _ in corner_waits:
        forward()
    for item in inner + extra:
        item.wait()
    for _, arrived in col_waits + corner_waits:
        for half in range(2):
            arrived(half)
    links.finish()


PLANES = [(part, layer) for layer in range(2) for part in range(2)]


def collect_columns(links, grad_ref, from_left, from_right, total, slots, order, straight):
    for side, buffer in (("left", from_left), ("right", from_right)):

        @pl.when(jnp.logical_not(links.has[side]))
        def _():
            for part, layer in order:
                buffer[part, layer] = jnp.zeros((2 * SIDE, HALF), jnp.float32)

    arrivals = []
    for number, (part, layer) in enumerate(order):
        relay = number not in straight
        arrivals.append(
            (
                links.send_columns(grad_ref.at[part, layer, 0], from_right.at[part, layer], "left", slots.at[part, layer], relay=relay),
                links.send_columns(grad_ref.at[part, layer, 3], from_left.at[part, layer], "right", slots.at[part, layer], relay=relay),
            )
        )

    def finish(index, half):
        part, layer = order[index]
        for forward, arrived in arrivals[index]:
            if half == 0:
                forward()
            arrived(half)

        def add(rows):
            total[part, layer, 0, rows, :] = grad_ref[part, layer, 1, rows, :] + from_left[part, layer, rows, :]
            total[part, layer, 1, rows, :] = grad_ref[part, layer, 2, rows, :] + from_right[part, layer, rows, :]

        by_rows(half * SIDE, (half + 1) * SIDE, 64, add)

    return finish


def middle_kernel(
    ext_ref, grad_ref, out_ref, from_left, from_right, slots, from_up, from_down, total, halo_slots, send_sems, recv_sems
):
    links = Links(send_sems, recv_sems)
    links.greet()
    finish_columns = collect_columns(links, grad_ref, from_left, from_right, total, slots, PLANES, MIDDLE_DIRECT_GRADIENTS)
    for side, buffer in (("up", from_up), ("down", from_down)):

        @pl.when(jnp.logical_not(links.has[side]))
        def _():
            for part, layer in PLANES:
                buffer[part, layer] = jnp.zeros((2, SIDE, HALF), jnp.float32)

    for side, block in (("left", 0), ("right", 3)):

        @pl.when(jnp.logical_not(links.has[side]))
        def _():
            for part, layer in PLANES:
                out_ref[part, layer, block] = jnp.zeros((2 * SIDE, HALF), jnp.float32)

    step_up = jnp.where(links.has["up"], OBJECT_STEP, 0.0).astype(jnp.float32)
    step_down = jnp.where(links.has["down"], OBJECT_STEP, 0.0).astype(jnp.float32)
    held, arrivals, halos = {}, {}, []
    pieces = 2 * len(PLANES)

    def issue(number):
        (part, layer), block = PLANES[number // 2], number % 2
        if block == 0:
            finish_columns(number // 2, 0)
        up = links.send(total.at[part, layer, block, pl.ds(0, SIDE)], from_down.at[part, layer, block], "up")
        if block == 0:
            finish_columns(number // 2, 1)
        down = links.send(total.at[part, layer, block, pl.ds(SIDE, SIDE)], from_up.at[part, layer, block], "down")
        held[number] = [links.sent.pop(), links.sent.pop()]
        arrivals[number] = (up, down)

    def retire(number):
        for item, condition in held[number]:

            @pl.when(condition)
            def _():
                item.wait_send()

    for number in range(IN_FLIGHT):
        issue(number)
    for number in range(pieces):
        (part, layer), block = PLANES[number // 2], number % 2
        for arrived in arrivals[number]:
            arrived()
        retire(number)
        if number + IN_FLIGHT < pieces:
            issue(number + IN_FLIGHT)
        for start, buffer, offset, step in (
            (0, from_up, 0, step_up),
            (HALF, from_up, 0, OBJECT_STEP),
            (SIDE, from_down, SIDE, OBJECT_STEP),
            (3 * HALF, from_down, SIDE, step_down),
        ):
            for row in range(start, start + HALF, 64):
                rows, near = pl.ds(row, 64), pl.ds(row - offset, 64)
                gradient = total[part, layer, block, rows, :] + buffer[part, layer, block, near, :]
                out_ref[part, layer, 1 + block, rows, :] = ext_ref[part, layer, 1 + block, rows, :] - step * gradient
        side, target = (("left", 3), ("right", 0))[block]
        halos.append(
            links.send_columns(
                out_ref.at[part, layer, 1 + block],
                out_ref.at[part, layer, target],
                side,
                halo_slots.at[part, layer],
                relay=number // 2 not in MIDDLE_DIRECT_HALOS,
            )
        )
        if number:
            halos[number - 1][0]()
    halos[-1][0]()
    for _, arrived in halos:
        for half in range(2):
            arrived(half)
    links.finish()


def last_kernel(
    ext_ref, grad_ref, first_probe_ref, second_probe_ref, probe_ref, object_ref, new_probe_ref,
    from_left, from_right, slots, from_up, from_down, total, partial, pair, landings, sums, gathered, send_sems, recv_sems,
):
    links = Links(send_sems, recv_sems)
    row, col = links.row, links.col
    core, x, y_low = lax.rem(col, 2), lax.rem(col // 2, 4), col // 8
    y_high, z = lax.rem(row, 2), row // 2
    y = y_high * 2 + y_low
    partner = (row, col + 1 - 2 * core)
    plane = lambda k: ((k // 4) * 2 + y_high, y_low * 8 + lax.rem(k, 4) * 2 + core)
    line = lambda k: (z * 2 + k // 2, lax.rem(k, 2) * 8 + x * 2 + core)
    groups = [(z * 4 + x, plane, 16), (y, line, 4)]
    peers = [partner]
    for place, device, members in groups:
        peers += [device(lax.rem(place + k, members)) for k in range(1, members)]
    links.greet(peers)
    count = 4 * SIDE
    half = count // 2

    def rows_at(start, size):
        return pl.ds(pl.multiple_of(start, 8), size)

    def start(source, target, device):
        item = links.copy(source, target, device)
        item.start()
        return item

    def add_probe(rows):
        partial[rows, :] = first_probe_ref[rows, :] + second_probe_ref[rows, :]

    by_rows(0, count, 64, add_probe)
    swap = start(partial.at[rows_at((1 - core) * half, half)], pair, partner)
    finish_columns = collect_columns(links, grad_ref, from_left, from_right, total, slots, PLANES, LAST_DIRECT_GRADIENTS)
    for side, buffer in (("up", from_up), ("down", from_down)):

        @pl.when(jnp.logical_not(links.has[side]))
        def _():
            for part, layer in PLANES:
                buffer[part, layer] = jnp.zeros((2, HALF, HALF), jnp.float32)

    swap.wait_recv()
    base = core * half

    def add_pair(index, carry):
        near = pl.ds(pl.multiple_of(index * 64, 64), 64)
        mine = rows_at(base + index * 64, 64)
        sums[mine, :] = partial[mine, :] + pair[near, :]
        return carry

    lax.fori_loop(0, half // 64, add_pair, 0, unroll=True)
    gathers = [swap]

    piece = half // 16
    plane_base = base + (z * 4 + x) * piece
    mine = rows_at(plane_base, piece)
    plane_peers = [device for device in peers[1:16]]
    line_peers = peers[16:]

    def spread_plane():
        items = []
        for k in range(1, 16):
            other = lax.rem(z * 4 + x + k, 16)
            source = sums.at[rows_at(base + other * piece, piece)]
            items.append(start(source, landings[0].at[k - 1], plane_peers[k - 1]))
        gathers.extend(items)
        return items

    def add_plane(items):
        for item in items:
            item.wait_recv()
        value = sums[mine, :]
        for k in range(15):
            value = value + landings[0][k]
        landings[1][y] = value

    def spread_line():
        items = [start(landings[1].at[y], landings[1].at[y], device) for device in line_peers]
        gathers.extend(items)
        return items

    def add_line(items):
        for item in items:
            item.wait_recv()
        gathered[mine, :] = (landings[1][0] + landings[1][1]) + (landings[1][2] + landings[1][3])

    def share_plane():
        items = [start(gathered.at[mine], gathered.at[mine], device) for device in plane_peers]
        gathers.extend(items)
        return items

    def await_all(items):
        for item in items:
            item.wait_recv()

    held, arrivals = {}, {}

    def issue(number):
        part, layer = PLANES[number // 2]
        block = number % 2
        up = links.send(total.at[part, layer, block, pl.ds(0, HALF)], from_down.at[part, layer, block], "up")
        down = links.send(total.at[part, layer, block, pl.ds(3 * HALF, HALF)], from_up.at[part, layer, block], "down")
        held[number] = [links.sent.pop(), links.sent.pop()]
        arrivals[number] = (up, down)

    def retire(number):
        for item, condition in held[number]:

            @pl.when(condition)
            def _():
                item.wait_send()

    def columns_in(index):
        finish_columns(index, 0)
        finish_columns(index, 1)

    items = spread_plane()
    columns_in(0)
    issue(0)
    issue(1)
    columns_in(1)
    retire(0)
    issue(2)
    retire(1)
    issue(3)
    add_plane(items)
    items = spread_line()
    columns_in(2)
    retire(2)
    issue(4)
    retire(3)
    issue(5)
    add_line(items)
    items = share_plane()
    columns_in(3)
    retire(4)
    issue(6)
    retire(5)
    issue(7)
    await_all(items)
    retire(6)
    retire(7)
    own_half = gathered.at[rows_at(base, half)]
    swap_back = start(own_half, own_half, partner)
    for number in range(2 * len(PLANES)):
        (part, layer), block = PLANES[number // 2], number % 2
        for arrived in arrivals[number]:
            arrived()
        lane = pl.ds(block * HALF, HALF)
        for begin, buffer in ((HALF, from_up), (SIDE, from_down)):
            for offset in range(0, HALF, 64):
                rows, near = pl.ds(begin + offset, 64), pl.ds(offset, 64)
                gradient = total[part, layer, block, rows, :] + buffer[part, layer, block, near, :]
                target = pl.ds(begin - HALF + offset, 64)
                object_ref[part, layer, target, lane] = ext_ref[part, layer, 1 + block, rows, :] - OBJECT_STEP * gradient
    swap_back.wait_recv()

    def finish_probe(rows):
        new_probe_ref[rows, :] = probe_ref[rows, :] - PROBE_STEP * gathered[rows, :]

    by_rows(0, count, 64, finish_probe)
    for item in gathers + [swap_back]:
        item.wait_send()
    links.finish()


def vmem_specs(count):
    return [pl.BlockSpec(memory_space=pltpu.VMEM)] * count


def comm_params(identity, limit):
    return pltpu.CompilerParams(collective_id=identity, has_side_effects=True, vmem_limit_bytes=limit << 20)


def semaphores(count):
    return [pltpu.SemaphoreType.DMA((count,)), pltpu.SemaphoreType.DMA((count,))]


def f32(*shape):
    return pltpu.VMEM(shape, jnp.float32)


EXTENDED = jax.ShapeDtypeStruct((2, 2, 4, 2 * SIDE, HALF), jnp.float32)


def first_exchange(tile, amplitudes, table, probe_modes):
    planes = amplitudes.shape[0]
    inputs = (tile, amplitudes, jnp.asarray(ORDER), jnp.asarray(ORDER.T), table, probe_modes)
    return pl.pallas_call(
        first_kernel,
        out_shape=(
            EXTENDED,
            jax.ShapeDtypeStruct((planes, SIDE, SIDE), jnp.float32),
            jax.ShapeDtypeStruct(table.shape, table.dtype),
            jax.ShapeDtypeStruct(probe_modes.shape, probe_modes.dtype),
        ),
        in_specs=[pl.BlockSpec(memory_space=pltpu.HBM)] * 6,
        out_specs=tuple(vmem_specs(4)),
        scratch_shapes=[
            f32(planes, SIDE, SIDE),
            pltpu.VMEM((SIDE, SIDE), jnp.bfloat16),
            pltpu.VMEM((SIDE, SIDE), jnp.bfloat16),
            f32(2, 3, 2, SIDE // 4, HALF),
            f32(2, 2, 3, 2, HALF // 4, HALF),
            pltpu.SemaphoreType.DMA((7,)),
            *semaphores(8 + 9 * 12),
        ],
        compiler_params=comm_params(0, 14),
    )(*[pltpu.with_memory_space_constraint(value, pltpu.HBM) for value in inputs])


def columns_buffers():
    return [f32(2, 2, 2 * SIDE, HALF), f32(2, 2, 2 * SIDE, HALF), f32(2, 2, 3, HALF, HALF)]


def middle_exchange(extended, gradient):
    return pl.pallas_call(
        middle_kernel,
        out_shape=EXTENDED,
        in_specs=vmem_specs(2),
        out_specs=vmem_specs(1)[0],
        scratch_shapes=[
            *columns_buffers(),
            f32(2, 2, 2, SIDE, HALF),
            f32(2, 2, 2, SIDE, HALF),
            f32(2, 2, 2, 2 * SIDE, HALF),
            f32(2, 2, 3, HALF, HALF),
            *semaphores(72 + 16 + 72),
        ],
        compiler_params=comm_params(1, 24),
    )(extended, gradient)


def last_exchange(extended, gradient, first_probe, second_probe, probe_modes):
    flat = (4 * SIDE, SIDE)
    new_object, new_probe = pl.pallas_call(
        last_kernel,
        out_shape=(
            jax.ShapeDtypeStruct((2, 2, SIDE, SIDE), jnp.float32),
            jax.ShapeDtypeStruct(flat, jnp.float32),
        ),
        in_specs=vmem_specs(5),
        out_specs=tuple(vmem_specs(2)),
        scratch_shapes=[
            *columns_buffers(),
            f32(2, 2, 2, HALF, HALF),
            f32(2, 2, 2, HALF, HALF),
            f32(2, 2, 2, 2 * SIDE, HALF),
            f32(*flat),
            f32(2 * SIDE, SIDE),
            [f32(15, 2 * SIDE // 16, SIDE), f32(4, 2 * SIDE // 16, SIDE)],
            f32(*flat),
            f32(*flat),
            *semaphores(72 + 16 + 2 + 33),
        ],
        compiler_params=comm_params(2, 26),
    )(extended, gradient, first_probe.reshape(flat), second_probe.reshape(flat), probe_modes.reshape(flat))
    return new_object, new_probe.reshape(probe_modes.shape)


def batch_kernel(
    batch, offset_ref, count_ref, ext_ref, probe_ref, amp_ref, table_ref, grad_ref, probe_grad_ref,
    obj, psi, right_a, right_b, yield_a, yield_b, left_a, left_b, out_a, out_b,
):
    lanes = lax.broadcasted_iota(jnp.int32, (CHUNK, HALF), 1)
    lo, hi = pl.ds(0, HALF), pl.ds(HALF, HALF)

    def chunks(total, body):
        def step(index, carry):
            body(pl.multiple_of(index * CHUNK, CHUNK))
            return carry

        lax.fori_loop(0, total // CHUNK, step, 0, unroll=True)

    def bf(value):
        return value.astype(jnp.bfloat16)

    def zero_grad(row):
        for part in range(2):
            for layer in range(2):
                for block in range(4):
                    grad_ref[part, layer, block, pl.ds(row, CHUNK), :] = jnp.zeros((CHUNK, HALF), jnp.float32)

    chunks(2 * SIDE, zero_grad)

    def zero_probe(row):
        for part in range(2):
            for mode in range(MODES):
                probe_grad_ref[part, mode, pl.ds(row, CHUNK), :] = jnp.zeros((CHUNK, SIDE), jnp.float32)

    chunks(SIDE, zero_probe)

    def right(table_a, table_b):
        yield_a[...] = dot(right_a[...], table_ref[table_a])
        yield_b[...] = dot(right_b[...], table_ref[table_b])

    def left(table_a, table_b):
        out_a[...] = dot(table_ref[table_a], left_a[...])
        out_b[...] = dot(table_ref[table_b], left_b[...])

    def put_split(mode, row, re, im):
        at = pl.ds(mode * SIDE + row, CHUNK)
        right_a[at, lo] = bf(re[0] + re[1])
        right_a[at, hi] = bf(im[0] + im[1])
        right_b[at, lo] = bf(re[0] - re[1])
        right_b[at, hi] = bf(im[0] - im[1])

    def columns(ref, mode):
        return pl.ds(mode * SIDE, HALF), pl.ds(mode * SIDE + HALF, HALF)

    def middle_spread(row):
        for mode in range(MODES):
            here = columns(left_a, mode)
            for part, lane in ((0, lo), (1, hi)):
                top = pl.ds(mode * SIDE + row, CHUNK)
                low = pl.ds(mode * SIDE + HALF + row, CHUNK)
                at, ab = yield_a[top, lane], yield_a[low, lane]
                bt, bb = yield_b[top, lane], yield_b[low, lane]
                to = pl.ds(part * HALF + row, CHUNK)
                a_sum, a_dif = at + ab, at - ab
                b_sum, b_dif = bt + bb, bt - bb
                left_a[to, here[0]] = bf(a_sum + b_sum)
                left_a[to, here[1]] = bf(a_sum - b_sum)
                left_b[to, here[0]] = bf(a_dif + b_dif)
                left_b[to, here[1]] = bf(a_dif - b_dif)

    def middle_forward(row):
        for mode in range(MODES):
            here = columns(left_a, mode)
            for part, lane in ((0, lo), (1, hi)):
                top = pl.ds(mode * SIDE + row, CHUNK)
                low = pl.ds(mode * SIDE + HALF + row, CHUNK)
                to = pl.ds(part * HALF + row, CHUNK)
                for source, at in ((yield_a, here[0]), (yield_b, here[1])):
                    upper, lower = source[top, lane], source[low, lane]
                    left_a[to, at] = bf(upper + lower)
                    left_b[to, at] = bf(upper - lower)

    def middle_backward(row):
        for mode in range(MODES):
            here = columns(left_a, mode)
            for part, lane in ((0, lo), (1, hi)):
                to = pl.ds(part * HALF + row, CHUNK)
                for base, target in ((0, left_a), (HALF, left_b)):
                    at = pl.ds(mode * SIDE + base + row, CHUNK)
                    even, odd = yield_a[at, lane], yield_b[at, lane]
                    target[to, here[0]] = bf(even + odd)
                    target[to, here[1]] = bf(even - odd)

    def joined(mode, row):
        result = []
        for sign in (1, -1):
            pair = []
            for part in range(2):
                at = pl.ds(part * HALF + row, CHUNK)
                halves = []
                for lane in columns(out_a, mode):
                    a, b = out_a[at, lane], out_b[at, lane]
                    halves.append(a + b if sign > 0 else a - b)
                pair.append(halves)
            result.append(pair)
        return result

    def pair_of(ref, first, second, row):
        return [ref[first, second, pl.ds(row, CHUNK), lane] for lane in (lo, hi)]

    def one_slot(slot, carry):
        start_row = offset_ref[batch * 2, slot]
        start_col = offset_ref[batch * 2 + 1, slot]
        base = start_col // HALF
        shift = start_col % HALF
        take_left = lanes < HALF - shift
        put_right = lanes >= shift
        back = lax.rem(HALF - shift, HALF)

        def fetch(row):
            for part in range(2):
                for layer in range(2):
                    at = pl.ds(start_row + row, CHUNK)
                    turned = [pltpu.roll(ext_ref[part, layer, base + k, at, :], back, 1) for k in range(3)]
                    obj[part, layer, pl.ds(row, CHUNK), lo] = jnp.where(take_left, turned[0], turned[1])
                    obj[part, layer, pl.ds(row, CHUNK), hi] = jnp.where(take_left, turned[1], turned[2])

        chunks(SIDE, fetch)

        def enter(row):
            o_re, o_im = pair_of(obj, 0, 0, row), pair_of(obj, 1, 0, row)
            for mode in range(MODES):
                p_re, p_im = pair_of(probe_ref, 0, mode, row), pair_of(probe_ref, 1, mode, row)
                re = [p_re[k] * o_re[k] - p_im[k] * o_im[k] for k in range(2)]
                im = [p_re[k] * o_im[k] + p_im[k] * o_re[k] for k in range(2)]
                put_split(mode, row, re, im)

        chunks(SIDE, enter)
        right(SUM_R, DIF_R)
        chunks(HALF, middle_spread)
        left(SUM_L, DIF_L)

        def second_slice(row):
            for side in range(2):
                at = row + side * HALF
                o_re, o_im = pair_of(obj, 0, 1, at), pair_of(obj, 1, 1, at)
                for mode in range(MODES):
                    w_re, w_im = joined(mode, row)[side]
                    for k, lane in ((0, lo), (1, hi)):
                        psi[0, mode, pl.ds(at, CHUNK), lane] = w_re[k]
                        psi[1, mode, pl.ds(at, CHUNK), lane] = w_im[k]
                    re = [w_re[k] * o_re[k] - w_im[k] * o_im[k] for k in range(2)]
                    im = [w_re[k] * o_im[k] + w_im[k] * o_re[k] for k in range(2)]
                    put_split(mode, at, re, im)

        chunks(HALF, second_slice)
        right(EVEN_R, ODD_R)
        chunks(HALF, middle_forward)
        left(EVEN_L, ODD_L)

        def compare(row):
            for base_row, source in ((0, out_a), (HALF, out_b)):
                waves = []
                for mode in range(MODES):
                    here = columns(source, mode)
                    re = [source[pl.ds(row, CHUNK), lane] for lane in here]
                    im = [source[pl.ds(HALF + row, CHUNK), lane] for lane in here]
                    waves.append((re, im))
                for k, lane in ((0, lo), (1, hi)):
                    intensity = waves[0][0][k] * waves[0][0][k] + waves[0][1][k] * waves[0][1][k]
                    for re, im in waves[1:]:
                        intensity = intensity + (re[k] * re[k] + im[k] * im[k])
                    amplitude = amp_ref[batch * (amp_ref.shape[0] // 2) + slot, pl.ds(base_row + row, CHUNK), lane]
                    ratio = 1.0 - amplitude * lax.rsqrt(jnp.maximum(intensity, AMPLITUDE_FLOOR**2))
                    target = right_a if k == 0 else right_b
                    for mode, (re, im) in enumerate(waves):
                        at = pl.ds(mode * SIDE + base_row + row, CHUNK)
                        target[at, lo] = bf(re[k] * ratio)
                        target[at, hi] = bf(im[k] * ratio)

        chunks(HALF, compare)
        right(EVEN_L, ODD_L)
        chunks(HALF, middle_backward)
        left(EVEN_R, ODD_R)

        def add_term(part, layer, row, term):
            turned = [pltpu.roll(value, shift, 1) for value in term]
            zero = jnp.zeros_like(turned[0])
            spread = [
                jnp.where(put_right, turned[0], zero),
                jnp.where(put_right, turned[1], turned[0]),
                jnp.where(put_right, zero, turned[1]),
            ]
            at = pl.ds(start_row + row, CHUNK)
            for k in range(3):
                grad_ref[part, layer, base + k, at, :] = grad_ref[part, layer, base + k, at, :] + spread[k]

        def object_term(layer, row, waves, backs):
            re, im = [], []
            for k in range(2):
                re.append(sum(w[0][k] * b[0][k] + w[1][k] * b[1][k] for w, b in zip(waves, backs)))
                im.append(sum(w[0][k] * b[1][k] - w[1][k] * b[0][k] for w, b in zip(waves, backs)))
            add_term(0, layer, row, re)
            add_term(1, layer, row, im)

        def last_back(row):
            for side in range(2):
                at = row + side * HALF
                backs = [joined(mode, row)[side] for mode in range(MODES)]
                waves = [(pair_of(psi, 0, mode, at), pair_of(psi, 1, mode, at)) for mode in range(MODES)]
                o_re, o_im = pair_of(obj, 0, 1, at), pair_of(obj, 1, 1, at)
                for mode, (b_re, b_im) in enumerate(backs):
                    re = [o_re[k] * b_re[k] + o_im[k] * b_im[k] for k in range(2)]
                    im = [o_re[k] * b_im[k] - o_im[k] * b_re[k] for k in range(2)]
                    put_split(mode, at, re, im)
                object_term(1, at, waves, backs)

        chunks(HALF, last_back)
        right(SUM_L, DIF_L)
        chunks(HALF, middle_spread)
        left(SUM_R, DIF_R)

        def first_back(row):
            for side in range(2):
                at = row + side * HALF
                backs = [joined(mode, row)[side] for mode in range(MODES)]
                waves = [(pair_of(probe_ref, 0, mode, at), pair_of(probe_ref, 1, mode, at)) for mode in range(MODES)]
                o_re, o_im = pair_of(obj, 0, 0, at), pair_of(obj, 1, 0, at)
                for mode, (b_re, b_im) in enumerate(backs):
                    for k, lane in ((0, lo), (1, hi)):
                        spot = (mode, pl.ds(at, CHUNK), lane)
                        probe_grad_ref[(0, *spot)] = probe_grad_ref[(0, *spot)] + (o_re[k] * b_re[k] + o_im[k] * b_im[k])
                        probe_grad_ref[(1, *spot)] = probe_grad_ref[(1, *spot)] + (o_re[k] * b_im[k] - o_im[k] * b_re[k])
                object_term(0, at, waves, backs)

        chunks(HALF, first_back)
        return carry

    lax.fori_loop(0, count_ref[batch], one_slot, 0)


def batch_terms(batch, extended, probe_modes, amplitudes, offsets, counts, table):
    vmem = pl.BlockSpec(memory_space=pltpu.VMEM)
    smem = pl.BlockSpec(memory_space=pltpu.SMEM)
    field = pltpu.VMEM((2, 2, SIDE, SIDE), jnp.float32)
    return pl.pallas_call(
        functools.partial(batch_kernel, batch),
        out_shape=(
            jax.ShapeDtypeStruct((2, 2, 4, 2 * SIDE, HALF), jnp.float32),
            jax.ShapeDtypeStruct((2, MODES, SIDE, SIDE), jnp.float32),
        ),
        in_specs=[smem, smem, vmem, vmem, vmem, vmem],
        out_specs=(vmem, vmem),
        scratch_shapes=[
            field,
            field,
            pltpu.VMEM((MODES * SIDE, SIDE), jnp.bfloat16),
            pltpu.VMEM((MODES * SIDE, SIDE), jnp.bfloat16),
            pltpu.VMEM((MODES * SIDE, SIDE), jnp.float32),
            pltpu.VMEM((MODES * SIDE, SIDE), jnp.float32),
            pltpu.VMEM((SIDE, MODES * SIDE), jnp.bfloat16),
            pltpu.VMEM((SIDE, MODES * SIDE), jnp.bfloat16),
            pltpu.VMEM((SIDE, MODES * SIDE), jnp.float32),
            pltpu.VMEM((SIDE, MODES * SIDE), jnp.float32),
        ],
        compiler_params=pltpu.CompilerParams(vmem_limit_bytes=26 << 20),
        cost_estimate=pl.CostEstimate(flops=3 * 64 * SIDE**3, bytes_accessed=12 << 20, transcendentals=0),
    )(offsets, counts, extended, probe_modes, amplitudes, table)


def body(object_field, probe_modes, amplitudes, offsets, counts):
    batches, slots = amplitudes.shape[:2]
    table = jnp.asarray(TABLES)
    extended, ordered, table, probe_modes = first_exchange(
        object_field, amplitudes.reshape(batches * slots, SIDE, SIDE), table, probe_modes
    )
    offsets, counts = offsets.reshape(2 * batches, slots), counts.reshape(batches)
    terms = lambda cells, batch: batch_terms(batch, cells, probe_modes, ordered, offsets, counts, table)
    gradient, first_probe = terms(extended, 0)
    extended = middle_exchange(extended, gradient)
    gradient, second_probe = terms(extended, 1)
    return last_exchange(extended, gradient, first_probe, second_probe, probe_modes)


def solution(mesh):
    return jax.shard_map(
        body,
        mesh=mesh,
        in_specs=(
            P(None, None, "row", "col"),
            P(),
            P(None, "row", "col", None, None),
            P(None, None, "row", "col"),
            P(None, "row", "col"),
        ),
        out_specs=(P(None, None, "row", "col"), P()),
        check_vma=False,
    )
```
